32 devices in a mesh: dp: 8 (over z, x), mp: 4 (over y, core).
Axes of the slice: x: 2, y: 2, z: 4, core: 2. Of those that a mesh axis runs over, the one named last changes fastest.
Arguments:
- tokens: bfloat16 [2, 2, 8192, 768], P(None, None, ('dp', 'mp')), may hold values from -6 to 6
- cotangent: bfloat16 [2, 2, 8192, 768], P(None, None, ('dp', 'mp')), may hold values from -6 to 6
- lengths: int32 [2, 8, 3], P(None, 'dp'), may hold values from 1 to 768, 1024 in all within a row
- norm1_gain: bfloat16 [2, 768], replicated, may hold values from 0.5 to 1.5
- norm1_shift: bfloat16 [2, 768], replicated, may hold values from -1.25 to 1.25
- query_key_value_weight: bfloat16 [2, 768, 3, 768], P(None, 'dp', None, 'mp'), may hold values from -0.21875 to 0.21875
- query_key_value_bias: bfloat16 [2, 3, 768], P(None, None, 'mp'), may hold values from -1.25 to 1.25
- out_weight: bfloat16 [2, 768, 768], P(None, 'mp', 'dp'), may hold values from -1.5 to 1.5
- out_bias: bfloat16 [2, 768], replicated, may hold values from -1.25 to 1.25
- norm2_gain: bfloat16 [2, 768], replicated, may hold values from 0.5 to 1.5
- norm2_shift: bfloat16 [2, 768], replicated, may hold values from -1.25 to 1.25
- normy_gain: bfloat16 [2, 768], replicated, may hold values from 0.5 to 1.5
- normy_shift: bfloat16 [2, 768], replicated, may hold values from -1.25 to 1.25
- cross_q_weight: bfloat16 [2, 768, 768], P(None, 'dp', 'mp'), may hold values from -0.21875 to 0.21875
- cross_q_bias: bfloat16 [2, 768], P(None, 'mp'), may hold values from -1.25 to 1.25
- cross_key_value_weight: bfloat16 [2, 768, 2, 768], P(None, 'dp', None, 'mp'), may hold values from -0.21875 to 0.21875
- cross_key_value_bias: bfloat16 [2, 2, 768], P(None, None, 'mp'), may hold values from -1.25 to 1.25
- cross_out_weight: bfloat16 [2, 768, 768], P(None, 'mp', 'dp'), may hold values from -1.5 to 1.5
- cross_out_bias: bfloat16 [2, 768], replicated, may hold values from -1.25 to 1.25
- norm3_gain: bfloat16 [2, 768], replicated, may hold values from 0.5 to 1.5
- norm3_shift: bfloat16 [2, 768], replicated, may hold values from -1.25 to 1.25
- up_weight: bfloat16 [2, 768, 3072], P(None, 'dp', 'mp'), may hold values from -0.21875 to 0.21875
- up_bias: bfloat16 [2, 3072], P(None, 'mp'), may hold values from -1.25 to 1.25
- down_weight: bfloat16 [2, 3072, 768], P(None, 'mp', 'dp'), may hold values from -0.109375 to 0.109375
- down_bias: bfloat16 [2, 768], replicated, may hold values from -1.25 to 1.25
Outputs:
- block_output: bfloat16 [2, 2, 8192, 768], P(None, None, ('dp', 'mp'))
- input_grad: float32 [2, 2, 8192, 768], P(None, None, ('dp', 'mp'))
- norm1_gain_grad: float32 [2, 768], replicated
- norm1_shift_grad: float32 [2, 768], replicated
- qkv_weight_grad: float32 [2, 768, 3, 768], P(None, 'dp', None, 'mp')
- qkv_bias_grad: float32 [2, 3, 768], P(None, None, 'mp')
- out_weight_grad: float32 [2, 768, 768], P(None, 'mp', 'dp')
- out_bias_grad: float32 [2, 768], replicated
- norm2_gain_grad: float32 [2, 768], replicated
- norm2_shift_grad: float32 [2, 768], replicated
- normy_gain_grad: float32 [2, 768], replicated
- normy_shift_grad: float32 [2, 768], replicated
- cross_q_weight_grad: float32 [2, 768, 768], P(None, 'dp', 'mp')
- cross_q_bias_grad: float32 [2, 768], P(None, 'mp')
- cross_kv_weight_grad: float32 [2, 768, 2, 768], P(None, 'dp', None, 'mp')
- cross_kv_bias_grad: float32 [2, 2, 768], P(None, None, 'mp')
- cross_out_weight_grad: float32 [2, 768, 768], P(None, 'mp', 'dp')
- cross_out_bias_grad: float32 [2, 768], replicated
- norm3_gain_grad: float32 [2, 768], replicated
- norm3_shift_grad: float32 [2, 768], replicated
- up_weight_grad: float32 [2, 768, 3072], P(None, 'dp', 'mp')
- up_bias_grad: float32 [2, 3072], P(None, 'mp')
- down_weight_grad: float32 [2, 3072, 768], P(None, 'mp', 'dp')
- down_bias_grad: float32 [2, 768], replicated
The draws below stay inside these ranges and needn't reach their ends.
Inputs may be any that keep to these rules, and one draw needn't show every extreme that they name: In every buffer the 3 image lengths sum to 1024 and the longest is exactly 768.
All inputs are finite; a program needn't handle non-finite values.
Results may differ from the reference program's by a relative error of at most 0.015.
Values may be sent and summed in bfloat16 or wider, within the bound.
No kernel may reach another device: no remote copies, remote signals or barrier semaphores. Data moves between devices by JAX's collectives and lax.ppermute only.
A program may use at most 448 MiB of HBM per device.

```python
import math
import jax
import jax.numpy as jnp
import numpy as np
from jax import lax

D = 768
HEAD_DIM = 64
FF = 3072
BUF = 1024
IMGS = 3
LONGEST = 768
MB = 2
TOKENS = 8192
N_DP = 8


def strengthened(values, own_key, source, target, blocks, factor):
    owner, partner = [(jnp.arange(values.shape[axis_at]) // (values.shape[axis_at] // blocks)).reshape([-1 if axis == axis_at else 1 for axis in range(values.ndim)]) for axis_at in (source, target)]
    chosen = jax.random.permutation(own_key, blocks)[partner]
    strong = (owner == chosen) | (owner == (partner + blocks // 2) % blocks)
    return jnp.where(strong, factor * values, values)


def block_scale(stream_key, shape, pieces, least, high):
    level = 1.0
    for position, blocks in pieces:
        draws = jax.random.uniform(jax.random.fold_in(jax.random.fold_in(stream_key, 6), position), (blocks,), jnp.float32, least / len(pieces), high / len(pieces))
        level = level * jnp.repeat(jnp.exp(draws), shape[position] // blocks).reshape((-1,) + (1,) * (len(shape) - 1 - position))
    return level


def split_up(amount, total, limit, slope):
    weights = [(1 << 20) // math.isqrt(standing ** slope) + 1 for standing in range(2, amount + 1)]
    spare, given = total - limit - (amount - 1), [1] * (amount - 1)
    while spare > 0:
        free = [i for i in range(amount - 1) if given[i] < limit]
        whole, remaining = sum([weights[i] for i in free]), spare
        for i in free:
            addition = min(limit - given[i], max(1, remaining * weights[i] // whole), spare)
            given[i] = given[i] + addition
            spare = spare - addition
    return np.array([limit] + given)


def uneven_parts(key, count, total, most, skew):
    if count == 2:
        one = jax.random.randint(key, (), max(1, total - most), min(most, total - 1) + 1)
        return jnp.stack([one, total - one])
    tallies = jnp.asarray(split_up(count, total, most, skew), jnp.int32)
    pairs = (count - 1) // 2
    donor, taker = tallies[1:1 + 2 * pairs:2], tallies[2:2 + 2 * pairs:2]
    slack = jnp.minimum(donor - 1, most - taker)
    moved = jax.random.randint(jax.random.fold_in(key, 1), (pairs,), 0, 1 << 20) % (slack + 1)
    tallies = tallies.at[1:1 + 2 * pairs:2].set(donor - moved).at[2:2 + 2 * pairs:2].set(taker + moved)
    return tallies[jax.random.permutation(jax.random.fold_in(key, 2), count)]


def bell_draw(own_key, extent, width, limit, cuts=(), kind=jnp.bfloat16):
    values = jax.random.normal(own_key, extent, jnp.float32) * width
    if len(cuts) > 0:
        values = block_scale(own_key, extent, cuts, -0.22, 0.18) * values
    return jnp.clip(values, min=-limit, max=limit).astype(kind)


def bell_draw_with(key, shape, width, bound, cuts, heavy, held_as=jnp.bfloat16):
    values = width * jax.random.normal(key, shape, jnp.float32)
    if cuts:
        values = values * block_scale(key, shape, cuts, -0.22, 0.18)
    return jnp.clip(strengthened(values, jax.random.fold_in(key, 3), *heavy), -bound, bound).astype(held_as)


def setup_inputs(seed: int = 0) -> dict:
    seeds = jax.random.split(jax.random.key(seed), 26)
    tokens = bell_draw_with(seeds[0], (MB, 2, TOKENS, D), 1.0, 6.0, ((2, 32),), (2, 3, 32, 2.75))
    cotangent = bell_draw_with(seeds[1], (MB, 2, TOKENS, D), 1.0, 6.0, ((2, 32),), (2, 3, 32, 2.75))
    lengths = jax.vmap(lambda own: uneven_parts(own, IMGS, BUF, LONGEST, 2))(jax.random.split(seeds[2], MB * N_DP)).reshape((MB, N_DP, IMGS)).astype(jnp.int32)
    norm1_gain = jnp.clip(1.0 + 0.1 * jax.random.normal(seeds[3], (2, D), jnp.float32), 0.5, 1.5).astype(jnp.bfloat16)
    norm1_shift = bell_draw(seeds[4], (2, D), 0.2, 1.25)
    query_key_value_weight = bell_draw(seeds[5], (2, D, 3, D), D ** -0.5, 0.21875, ((1, 8), (3, 4)))
    query_key_value_bias = bell_draw(seeds[6], (2, 3, D), 0.2, 1.25, ((2, 4),))
    out_weight = bell_draw(seeds[7], (2, D, D), 16 ** -0.5, 1.5, ((1, 4), (2, 8)))
    out_bias = bell_draw(seeds[8], (2, D), 0.2, 1.25)
    norm2_gain = jnp.clip(1.0 + 0.1 * jax.random.normal(seeds[9], (2, D), jnp.float32), 0.5, 1.5).astype(jnp.bfloat16)
    norm2_shift = bell_draw(seeds[10], (2, D), 0.2, 1.25)
    normy_gain = jnp.clip(1.0 + 0.1 * jax.random.normal(seeds[11], (2, D), jnp.float32), 0.5, 1.5).astype(jnp.bfloat16)
    normy_shift = bell_draw(seeds[12], (2, D), 0.2, 1.25)
    cross_q_weight = bell_draw(seeds[13], (2, D, D), D ** -0.5, 0.21875, ((1, 8), (2, 4)))
    cross_q_bias = bell_draw(seeds[14], (2, D), 0.2, 1.25, ((1, 4),))
    cross_key_value_weight = bell_draw(seeds[15], (2, D, 2, D), D ** -0.5, 0.21875, ((1, 8), (3, 4)))
    cross_key_value_bias = bell_draw(seeds[16], (2, 2, D), 0.2, 1.25, ((2, 4),))
    cross_out_weight = bell_draw(seeds[17], (2, D, D), 16 ** -0.5, 1.5, ((1, 4), (2, 8)))
    cross_out_bias = bell_draw(seeds[18], (2, D), 0.2, 1.25)
    norm3_gain = jnp.clip(1.0 + 0.1 * jax.random.normal(seeds[19], (2, D), jnp.float32), 0.5, 1.5).astype(jnp.bfloat16)
    norm3_shift = bell_draw(seeds[20], (2, D), 0.2, 1.25)
    up_weight = bell_draw(seeds[21], (2, D, FF), D ** -0.5, 0.21875, ((1, 8), (2, 4)))
    up_bias = bell_draw(seeds[22], (2, FF), 0.2, 1.25, ((1, 4),))
    down_weight = bell_draw(seeds[23], (2, FF, D), FF ** -0.5, 0.109375, ((1, 4), (2, 8)))
    down_bias = bell_draw(seeds[24], (2, D), 0.2, 1.25)
    return dict(tokens=tokens, cotangent=cotangent, lengths=lengths, norm1_gain=norm1_gain, norm1_shift=norm1_shift, query_key_value_weight=query_key_value_weight, query_key_value_bias=query_key_value_bias, out_weight=out_weight, out_bias=out_bias, norm2_gain=norm2_gain, norm2_shift=norm2_shift, normy_gain=normy_gain, normy_shift=normy_shift, cross_q_weight=cross_q_weight, cross_q_bias=cross_q_bias, cross_key_value_weight=cross_key_value_weight, cross_key_value_bias=cross_key_value_bias, cross_out_weight=cross_out_weight, cross_out_bias=cross_out_bias, norm3_gain=norm3_gain, norm3_shift=norm3_shift, up_weight=up_weight, up_bias=up_bias, down_weight=down_weight, down_bias=down_bias)


@jax.custom_vjp
def low(v):
    return lax.optimization_barrier(v.astype(jnp.bfloat16)).astype(jnp.float32)

@jax.custom_vjp
def lowered_backward(v):
    return v

def low_keep(v):
    return (low(v), None)

def low_pass(kept, grad):
    return (grad,)

def back_keep(v):
    return (v, None)

def back_low(kept, grad):
    return (low(grad),)
low.defvjp(low_keep, low_pass)
lowered_backward.defvjp(back_keep, back_low)
highest_precision = lax.Precision.HIGHEST
norm_epsilon = 1e-06

def layer_norm(rows, gain, shift):
    centre = lax.optimization_barrier(jnp.mean(rows, -1, keepdims=True))
    centred = rows - centre
    spread = lax.optimization_barrier(jnp.mean(centred * centred, -1, keepdims=True))
    return centred * lax.rsqrt(spread + norm_epsilon) * gain + shift

def rope_turn(vectors, cosine, sine):
    half = vectors.shape[-1] // 2
    first = vectors[..., :half]
    second = vectors[..., half:]
    return jnp.concatenate([first * cosine - second * sine, second * cosine + first * sine], -1)

def tables(image_sizes, count, half):
    places = jnp.arange(count, dtype=jnp.int32)
    ends = jnp.cumsum(image_sizes).astype(jnp.int32)
    passed = places[:, None] >= ends[None, :]
    segment = lax.optimization_barrier(jnp.sum(passed.astype(jnp.int32), -1))
    start = lax.optimization_barrier(jnp.sum(jnp.where(passed, image_sizes[None, :], 0), -1)).astype(jnp.int32)
    place = (places - start).astype(jnp.float32)
    freqs = 100.0 ** (-(jnp.arange(half, dtype=jnp.float32) / half))
    angles = place[:, None] * freqs[None, :]
    return (segment, jnp.cos(angles)[:, None, :], jnp.sin(angles)[:, None, :])

def attention(queries, keys, values, same):
    count = queries.shape[0]
    scores = lowered_backward(jnp.einsum('qhc,khc->hqk', queries, keys, precision=highest_precision) * HEAD_DIM ** (-0.5))
    scores = jnp.where(same[None], scores, -1e+30)
    probs = low(jax.nn.softmax(scores, axis=-1))
    attended = jnp.einsum('hqk,khc->qhc', probs, values, precision=highest_precision).reshape(count, -1)
    return lowered_backward(low(attended))

def view_block(rows, other_rows, weights, same, cosine, sine):
    norm1_gain, norm1_shift, query_key_value_weight, query_key_value_bias, out_weight, out_bias, norm2_gain, norm2_shift, normy_gain, normy_shift, cross_q_weight, cross_q_bias, cross_key_value_weight, cross_key_value_bias, cross_out_weight, cross_out_bias, norm3_gain, norm3_shift, up_weight, up_bias, down_weight, down_bias = weights
    count = rows.shape[0]
    heads = query_key_value_weight.shape[2] // HEAD_DIM
    normalized_rows = low(layer_norm(rows, norm1_gain, norm1_shift))
    blended_output = lowered_backward(jnp.einsum('rj,jqw->rqw', normalized_rows, query_key_value_weight, precision=highest_precision) + query_key_value_bias)
    queries = low(rope_turn(blended_output[:, 0].reshape(count, heads, HEAD_DIM), cosine, sine))
    keys_turned = low(rope_turn(blended_output[:, 1].reshape(count, heads, HEAD_DIM), cosine, sine))
    values = low(blended_output[:, 2].reshape(count, heads, HEAD_DIM))
    attended = attention(queries, keys_turned, values, same)
    middle = rows + lowered_backward(jnp.dot(attended, out_weight, precision=highest_precision) + out_bias)
    normed_two = low(layer_norm(middle, norm2_gain, norm2_shift))
    source_tokens = low(layer_norm(other_rows, normy_gain, normy_shift))
    cross_query = lowered_backward(jnp.dot(normed_two, cross_q_weight, precision=highest_precision) + cross_q_bias)
    cross_queries = low(rope_turn(cross_query.reshape(count, heads, HEAD_DIM), cosine, sine))
    cross_blended = lowered_backward(jnp.einsum('rj,jqw->rqw', source_tokens, cross_key_value_weight, precision=highest_precision) + cross_key_value_bias)
    cross_keys = low(rope_turn(cross_blended[:, 0].reshape(count, heads, HEAD_DIM), cosine, sine))
    cross_values = low(cross_blended[:, 1].reshape(count, heads, HEAD_DIM))
    cross_attended = attention(cross_queries, cross_keys, cross_values, same)
    middle_two = middle + lowered_backward(jnp.dot(cross_attended, cross_out_weight, precision=highest_precision) + cross_out_bias)
    normed_three = low(layer_norm(middle_two, norm3_gain, norm3_shift))
    hidden_in = lowered_backward(jnp.dot(normed_three, up_weight, precision=highest_precision) + up_bias)
    hidden = low(jax.nn.gelu(hidden_in, approximate=False))
    update = lowered_backward(jnp.dot(hidden, down_weight, precision=highest_precision) + down_bias)
    return middle_two + update

def reference(tokens, cotangent, lengths, norm1_gain, norm1_shift, query_key_value_weight, query_key_value_bias, out_weight, out_bias, norm2_gain, norm2_shift, normy_gain, normy_shift, cross_q_weight, cross_q_bias, cross_key_value_weight, cross_key_value_bias, cross_out_weight, cross_out_bias, norm3_gain, norm3_shift, up_weight, up_bias, down_weight, down_bias):
    weights = tuple((w.astype(jnp.float32) for w in (norm1_gain, norm1_shift, query_key_value_weight, query_key_value_bias, out_weight, out_bias, norm2_gain, norm2_shift, normy_gain, normy_shift, cross_q_weight, cross_q_bias, cross_key_value_weight, cross_key_value_bias, cross_out_weight, cross_out_bias, norm3_gain, norm3_shift, up_weight, up_bias, down_weight, down_bias)))
    rows_all = tokens.astype(jnp.float32).reshape(MB, 2, N_DP, BUF, D).transpose(0, 2, 1, 3, 4)
    rows_all = rows_all.reshape(MB * N_DP, 2, BUF, D)
    cot_all = cotangent.astype(jnp.float32).reshape(MB, 2, N_DP, BUF, D).transpose(0, 2, 1, 3, 4)
    cot_all = cot_all.reshape(MB * N_DP, 2, BUF, D)
    sizes_all = lengths.reshape(MB * N_DP, IMGS)

    def one(carry, item):
        rows, cot_rows, image_sizes = item
        segment, cosine, sine = tables(image_sizes, BUF, HEAD_DIM // 2)
        same = segment[:, None] == segment[None, :]

        def forward(rows_in, weights_in):
            first = tuple((w[0] for w in weights_in))
            second = tuple((w[1] for w in weights_in))
            return jnp.stack([view_block(rows_in[0], rows_in[1], first, same, cosine, sine), view_block(rows_in[1], rows_in[0], second, same, cosine, sine)], 0)
        result, pullback = jax.vjp(forward, rows, weights)
        rows_grad, weight_grads = pullback(cot_rows)
        carry = jax.tree.map(lambda left, right: left + right, carry, weight_grads)
        return (carry, (result, rows_grad))
    zeros = jax.tree.map(jnp.zeros_like, weights)
    totals, (results, row_grads) = lax.scan(one, zeros, (rows_all, cot_all, sizes_all))
    block_output = results.reshape(MB, N_DP, 2, BUF, D).transpose(0, 2, 1, 3, 4)
    block_output = block_output.reshape(MB, 2, N_DP * BUF, D).astype(jnp.bfloat16)
    input_grad = row_grads.reshape(MB, N_DP, 2, BUF, D).transpose(0, 2, 1, 3, 4)
    input_grad = input_grad.reshape(MB, 2, N_DP * BUF, D).astype(jnp.float32)
    return (block_output, input_grad, totals[0], totals[1], totals[2], totals[3], totals[4], totals[5], totals[6], totals[7], totals[8], totals[9], totals[10], totals[11], totals[12], totals[13], totals[14], totals[15], totals[16], totals[17], totals[18], totals[19], totals[20], totals[21])
```

```python
import functools
import math
import jax
import jax.numpy as jnp
from jax import lax
from jax.experimental import pallas as pl
from jax.experimental.pallas import tpu as pltpu
from jax.sharding import PartitionSpec as P

HEAD_DIM = 64
PAIR = 2 * HEAD_DIM
FAR = 1e30


def swap_halves(u, lane):
    half = HEAD_DIM // 2
    fwd = pltpu.roll(u, half, 1)
    bwd = pltpu.roll(u, PAIR - half, 1)
    return jnp.where(lane % HEAD_DIM < half, bwd, fwd)


def attend_kernel(q_ref, k_ref, v_ref, qf_ref, kf_ref, cos_ref, sin_ref, o_ref, lse_ref, qr_ref, kr_ref, *, tile):
    rows = k_ref.shape[0]
    lane_all = lax.broadcasted_iota(jnp.int32, (rows, PAIR), 1)
    cosine, sine = cos_ref[...], sin_ref[...]
    k = k_ref[...]
    kr = (k * cosine + swap_halves(k, lane_all) * sine).astype(jnp.bfloat16)
    kr_ref[...] = kr
    q = q_ref[...]
    qr_ref[...] = (q * cosine + swap_halves(q, lane_all) * sine).astype(jnp.bfloat16)
    low = lane_all < HEAD_DIM
    kf = kf_ref[...]
    v = v_ref[...].astype(jnp.bfloat16)
    one = jnp.ones_like(v)
    keys = (jnp.where(low, kr, kf), jnp.where(low, kf, kr))
    vals = (jnp.where(low, v, one), jnp.where(low, one, v))
    lane = lax.broadcasted_iota(jnp.int32, (tile, PAIR), 1)
    low_t = lane < HEAD_DIM

    for t in range(rows // tile):
        at = pl.ds(t * tile, tile)
        qs = qr_ref[at, :] * jnp.bfloat16(HEAD_DIM ** -0.5)
        qf = qf_ref[at, :]
        outs, lses = [], []
        for h in range(2):
            qh = jnp.where(low_t, qs, qf) if h == 0 else jnp.where(low_t, qf, qs)
            s = lax.dot_general(qh, keys[h], (((1,), (1,)), ((), ())), preferred_element_type=jnp.float32)
            top = jnp.max(s, -1, keepdims=True)
            p = jnp.exp(s - top).astype(jnp.bfloat16)
            o = jnp.dot(p, vals[h], preferred_element_type=jnp.float32)
            total = pltpu.roll(o, HEAD_DIM, 1)
            outs.append(o / total)
            lses.append(top + jnp.log(total))
        o_ref[at, :] = jnp.where(low_t, outs[0], outs[1]).astype(jnp.bfloat16)
        lse_ref[at, :] = jnp.where(low_t, lses[0], lses[1])


def three_parts(u):
    a = u.astype(jnp.bfloat16).astype(jnp.float32)
    r = u - a
    b = r.astype(jnp.bfloat16).astype(jnp.float32)
    return a, b, r - b


def attend_back_kernel(qr_ref, kr_ref, v_ref, o_ref, do_ref, lse_ref, qf_ref, kf_ref, cos_ref, sin_ref,
                       dq_ref, dk_ref, dv_ref, dk_acc, dv_acc, *, tile):
    rows = kr_ref.shape[0]
    lane_all = lax.broadcasted_iota(jnp.int32, (rows, PAIR), 1)
    low = lane_all < HEAD_DIM
    within = lane_all % HEAD_DIM
    kr = kr_ref[...]
    kf = kf_ref[...]
    v = v_ref[...]
    ones3 = jnp.where(within < 3, 1.0, 0.0).astype(jnp.bfloat16)
    ones6 = jnp.where((within >= 3) & (within < 6), 1.0, 0.0).astype(jnp.bfloat16)
    kfull = kf + ones6
    keys = (jnp.where(low, kr, kfull), jnp.where(low, kfull, kr))
    vals = (jnp.where(low, v, ones3), jnp.where(low, ones3, v))
    lane = lax.broadcasted_iota(jnp.int32, (tile, PAIR), 1)
    low_t = lane < HEAD_DIM
    within_t = lane % HEAD_DIM
    scale = HEAD_DIM ** -0.5
    nt = (((1,), (1,)), ((), ()))
    tn = (((0,), (0,)), ((), ()))
    for t in range(rows // tile):
        at = pl.ds(t * tile, tile)
        qr = qr_ref[at, :]
        qs = qr * jnp.bfloat16(scale)
        do = do_ref[at, :]
        prod = do.astype(jnp.float32) * o_ref[at, :].astype(jnp.float32)
        lse = lse_ref[at, :]
        lse_other = pltpu.roll(lse, HEAD_DIM, 1)
        qf = qf_ref[at, :].astype(jnp.float32)
        dqs = []
        for h in range(2):
            mine = low_t if h == 0 else ~low_t
            dsum = jnp.sum(jnp.where(mine, prod, 0.0), -1, keepdims=True)
            a, b, c = three_parts(-dsum)
            dfeat = jnp.where(within_t == 0, a, jnp.where(within_t == 1, b, jnp.where(within_t == 2, c, 0.0)))
            doh = jnp.where(mine, do, dfeat.astype(jnp.bfloat16))
            a, b, c = three_parts(-lse_other)
            qfeat = jnp.where(within_t == 3, a, jnp.where(within_t == 4, b, jnp.where(within_t == 5, c, qf)))
            qh = jnp.where(mine, qs, qfeat.astype(jnp.bfloat16))
            st = lax.dot_general(keys[h], qh, nt, preferred_element_type=jnp.float32)
            p = jnp.exp(st)
            dpt = lax.dot_general(vals[h], doh, nt, preferred_element_type=jnp.float32)
            ds = (p * dpt).astype(jnp.bfloat16)
            dv = jnp.dot(p.astype(jnp.bfloat16), do, preferred_element_type=jnp.float32)
            dk = jnp.dot(ds, qs, preferred_element_type=jnp.float32)
            dqs.append(lax.dot_general(ds, kr, tn, preferred_element_type=jnp.float32))
            if t == 0:
                dv_acc[h] = dv
                dk_acc[h] = dk
            else:
                dv_acc[h] += dv
                dk_acc[h] += dk
        dq = jnp.where(low_t, dqs[0], dqs[1]) * scale
        dq_ref[at, :] = (dq * cos_ref[at, :] - swap_halves(dq, lane) * sin_ref[at, :]).astype(jnp.bfloat16)
    dk = jnp.where(low, dk_acc[0], dk_acc[1])
    dk_ref[...] = (dk * cos_ref[...] - swap_halves(dk, lane_all) * sin_ref[...]).astype(jnp.bfloat16)
    dv_ref[...] = jnp.where(low, dv_acc[0], dv_acc[1]).astype(jnp.bfloat16)


def attend(q, k, v, feats, width, tile=512):
    qf, kf, cosine, sine = feats
    rows = q[0].shape[0]

    def from_col(start):
        return pl.BlockSpec((rows, PAIR), lambda j: (0, start // PAIR + j))

    col = from_col(0)
    whole = pl.BlockSpec((rows, PAIR), lambda j: (0, 0))
    bf = jax.ShapeDtypeStruct((rows, width), jnp.bfloat16)
    pairs = width // PAIR
    return pl.pallas_call(
        functools.partial(attend_kernel, tile=min(tile, rows)),
        grid=(pairs,),
        in_specs=[from_col(q[1]), from_col(k[1]), from_col(v[1]), whole, whole, whole, whole],
        out_specs=[col, col, col, col],
        out_shape=[bf, jax.ShapeDtypeStruct((rows, width), jnp.float32), bf, bf],
        cost_estimate=pl.CostEstimate(flops=8 * pairs * rows * rows * PAIR, bytes_accessed=rows * width * 24, transcendentals=2 * pairs * rows * rows),
        name="attend",
    )(q[0], k[0], v[0], qf, kf, cosine, sine)


def attend_back(qr, kr, v, o, do, lse, feats, tile=256):
    qf, kf, cosine, sine = feats
    rows, width = qr.shape
    col = pl.BlockSpec((rows, PAIR), lambda j: (0, j))
    whole = pl.BlockSpec((rows, PAIR), lambda j: (0, 0))
    bf = jax.ShapeDtypeStruct((rows, width), jnp.bfloat16)
    pairs = width // PAIR
    return pl.pallas_call(
        functools.partial(attend_back_kernel, tile=tile),
        grid=(pairs,),
        in_specs=[col] * 6 + [whole] * 4,
        out_specs=[col, col, col],
        out_shape=[bf, bf, bf],
        scratch_shapes=[pltpu.VMEM((2, rows, PAIR), jnp.float32), pltpu.VMEM((2, rows, PAIR), jnp.float32)],
        cost_estimate=pl.CostEstimate(flops=20 * pairs * rows * rows * PAIR, bytes_accessed=rows * width * 20, transcendentals=2 * pairs * rows * rows),
        name="attend_back",
    )(qr, kr, v, o, do, lse, qf, kf, cosine, sine)


def tables(image_sizes, count):
    images = image_sizes.shape[0]
    places = jnp.arange(count, dtype=jnp.int32)
    ends = jnp.cumsum(image_sizes)
    passed = places[:, None] >= ends[None, :]
    segment = jnp.sum(passed.astype(jnp.int32), -1)
    start = jnp.sum(jnp.where(passed, image_sizes[None, :], 0), -1)
    place = (places - start).astype(jnp.float32)
    half = HEAD_DIM // 2
    lane = jnp.arange(PAIR, dtype=jnp.int32)
    freqs = 100.0 ** (-((lane % half).astype(jnp.float32) / half))
    angles = place[:, None] * freqs[None, :]
    sign = jnp.where(lane % HEAD_DIM < half, -1.0, 1.0)
    member = (lane % HEAD_DIM)[None, :] == segment[:, None]
    slot = ((lane % HEAD_DIM) < images)[None, :]
    kf = member.astype(jnp.bfloat16)
    qf = jnp.where(slot & ~member, -FAR, 0.0).astype(jnp.bfloat16)
    return qf, kf, jnp.cos(angles), jnp.sin(angles) * sign[None, :]


norm_epsilon = 1e-06
BF = jnp.bfloat16
F32 = jnp.float32


def mm(a, b):
    return jnp.dot(a, b, preferred_element_type=F32)


def mm_t(a, b):
    return lax.dot_general(a, b, (((1,), (1,)), ((), ())), preferred_element_type=F32)


def t_mm(a, b):
    return lax.dot_general(a, b, (((0,), (0,)), ((), ())), preferred_element_type=F32)


def norm(rows, gain, shift):
    centre = jnp.mean(rows, -1, keepdims=True)
    centred = rows - centre
    spread = jnp.mean(centred * centred, -1, keepdims=True)
    scale = lax.rsqrt(spread + norm_epsilon)
    hat = centred * scale
    return (hat * gain + shift).astype(BF), (centre, scale)


def norm_back(grad, rows, stats, gain):
    centre, scale = stats
    hat = (rows - centre) * scale
    w = grad * gain
    back = scale * (w - jnp.mean(w, -1, keepdims=True) - hat * jnp.mean(w * hat, -1, keepdims=True))
    return back, jnp.sum(grad * hat, 0), jnp.sum(grad, 0)


def body(tokens, cotangent, lengths, norm1_gain, norm1_shift, qkv_w, qkv_b, out_w, out_b, norm2_gain, norm2_shift,
         normy_gain, normy_shift, cq_w, cq_b, ckv_w, ckv_b, cout_w, cout_b, norm3_gain, norm3_shift, up_w, up_b, down_w, down_b):
    batches = tokens.shape[0]
    members = lax.axis_size("mp")
    n_dp = lax.axis_size("dp")
    assert members == 2 * batches
    me = lax.axis_index("mp")
    view = me // batches
    batch = me % batches
    local = tokens.shape[2]
    rows = local * members
    width = tokens.shape[3]
    r = qkv_w.shape[1]
    hw = cq_w.shape[2]
    fw = up_w.shape[2]
    partner = [(i, (i + batches) % members) for i in range(members)]
    groups = [[d * members + v * batches + b for d in range(n_dp) for b in range(batches)] for v in range(2)]
    both = ("dp", "mp")

    def of_view(a, which):
        return lax.dynamic_index_in_dim(a, which, 0, keepdims=False)

    def swap_view(a):
        return jnp.stack([of_view(a, view), lax.ppermute(of_view(a, 1 - view), "mp", partner)], 0)

    def gather(pack):
        return lax.all_gather(swap_view(pack), both, axis=0, axis_index_groups=groups)

    def placed(g, start, parts, w):
        piece = g[..., start : start + parts * w].reshape(n_dp, batches, 2, r, parts, w)
        return piece.transpose(0, 3, 4, 2, 1, 5).reshape(n_dp * r, parts * members * w)

    pack_a = jnp.concatenate(
        [qkv_w.reshape(2, r, -1), out_w.swapaxes(1, 2), cq_w, ckv_w.reshape(2, r, -1), cout_w.swapaxes(1, 2)], -1)
    pack_f = jnp.concatenate([up_w, down_w.swapaxes(1, 2)], -1)
    got_a = gather(pack_a)
    got_f = gather(pack_f)

    bias_pack = jnp.concatenate([qkv_b.reshape(2, -1), cq_b, ckv_b.reshape(2, -1), up_b], -1)
    bias_len = bias_pack.shape[-1]
    bias_rows = -(-bias_len // width)
    bias_pack = jnp.pad(bias_pack, ((0, 0), (0, bias_rows * width - bias_len))).reshape(2, 1, bias_rows, width)
    bias_pack = jnp.broadcast_to(bias_pack, (2, batches, bias_rows, width))
    by_view = tokens.swapaxes(0, 1)
    sent_x = jnp.concatenate([by_view, bias_pack], 2).reshape(members, local + bias_rows, width)
    got_x = lax.all_to_all(sent_x, "mp", 0, 0, tiled=True)
    got_y = lax.all_to_all(by_view[::-1].reshape(members, local, width), "mp", 0, 0, tiled=True)
    got_z = lax.all_to_all(cotangent.swapaxes(0, 1).reshape(members, local, width), "mp", 0, 0, tiled=True)
    x_low = got_x[:, :local].reshape(rows, width)
    bias_all = got_x[:, local:].reshape(2, batches, bias_rows * width).astype(F32)
    bias_all = jnp.where(view == 0, bias_all, bias_all[::-1]).reshape(members, -1)
    x = x_low.astype(F32)
    y = got_y.reshape(rows, width).astype(F32)
    dz_low = got_z.reshape(rows, width)
    dz = dz_low.astype(F32)

    def bias_of(start, parts, w):
        return bias_all[:, start : start + parts * w].reshape(members, parts, w).swapaxes(0, 1).reshape(1, -1)

    qkv_bias = bias_of(0, 3, hw)
    cq_bias = bias_of(3 * hw, 1, hw)
    ckv_bias = bias_of(4 * hw, 2, hw)
    up_bias = bias_of(6 * hw, 1, fw)

    def mine(a):
        return of_view(a, view).astype(F32)[None]

    g1, s1, ob, g2, s2, gy, sy, cob, g3, s3, db = [
        mine(a) for a in (norm1_gain, norm1_shift, out_b, norm2_gain, norm2_shift, normy_gain, normy_shift, cout_b, norm3_gain, norm3_shift, down_b)]

    feats = tables(of_view(lengths[:, 0], batch), rows)

    w_qkv = placed(got_a, 0, 3, hw)
    w_out = placed(got_a, 3 * hw, 1, hw)
    w_cq = placed(got_a, 4 * hw, 1, hw)
    w_ckv = placed(got_a, 5 * hw, 2, hw)
    w_cout = placed(got_a, 7 * hw, 1, hw)
    w_up = placed(got_f, 0, 1, fw)
    w_down = placed(got_f, fw, 1, fw)

    n1, st1 = norm(x, g1, s1)
    side, sty = norm(y, gy, sy)
    qkv = mm(n1, w_qkv) + qkv_bias
    att, lse, q_rot, k_rot = attend((qkv, 0), (qkv, width), (qkv, 2 * width), feats, width)
    v_low = qkv[:, 2 * width :].astype(BF)
    middle = x + mm_t(att, w_out) + ob
    n2, st2 = norm(middle, g2, s2)
    cq = mm(n2, w_cq) + cq_bias
    ckv = mm(side, w_ckv) + ckv_bias
    catt, clse, cq_rot, ck_rot = attend((cq, 0), (ckv, 0), (ckv, width), feats, width)
    cv_low = ckv[:, width:].astype(BF)
    middle2 = middle + mm_t(catt, w_cout) + cob
    n3, st3 = norm(middle2, g3, s3)
    hidden_in = mm(n3, w_up) + up_bias
    phi = 0.5 * (1.0 + lax.erf(hidden_in * (0.5 ** 0.5)))
    slope = (phi + hidden_in * jnp.exp(-0.5 * hidden_in * hidden_in) * (0.5 / math.pi) ** 0.5).astype(BF)
    hidden = (hidden_in * phi).astype(BF)
    hidden, slope = lax.optimization_barrier((hidden, slope))
    output = (middle2 + mm_t(hidden, w_down) + db).astype(BF)

    d_hidden = (mm(dz_low, w_down) * slope.astype(F32)).astype(BF)
    grad_up = t_mm(n3, d_hidden)
    grad_down = t_mm(dz_low, hidden)
    part, gg3, gs3 = norm_back(mm_t(d_hidden, w_up), middle2, st3, g3)
    d_mid2 = dz + part
    d_cross = d_mid2.astype(BF)
    grad_cout = t_mm(d_cross, catt)
    d_catt = mm(d_cross, w_cout).astype(BF)
    dcq, dck, dcv = attend_back(cq_rot, ck_rot, cv_low, catt, d_catt, clse, feats)
    grad_cq = t_mm(n2, dcq)
    grad_ckv = jnp.concatenate([t_mm(side, dck), t_mm(side, dcv)], -1)
    part, gg2, gs2 = norm_back(mm_t(dcq, w_cq), middle, st2, g2)
    d_mid = d_mid2 + part
    other, ggy, gsy = norm_back(mm_t(dck, w_ckv[:, :width]) + mm_t(dcv, w_ckv[:, width:]), y, sty, gy)
    d_branch = d_mid.astype(BF)
    grad_out = t_mm(d_branch, att)
    d_att = mm(d_branch, w_out).astype(BF)
    dq, dk, dv = attend_back(q_rot, k_rot, v_low, att, d_att, lse, feats)
    grad_qkv = jnp.concatenate([t_mm(n1, dq), t_mm(n1, dk), t_mm(n1, dv)], -1)
    part, gg1, gs1 = norm_back(mm_t(dq, w_qkv[:, :width]) + mm_t(dk, w_qkv[:, width : 2 * width]) + mm_t(dv, w_qkv[:, 2 * width :]), x, st1, g1)
    own = d_mid + part

    def packed(g, parts, w):
        piece = g.astype(BF).reshape(n_dp, r, parts, 2, batches, w)
        return piece.transpose(0, 4, 3, 1, 2, 5).reshape(n_dp * batches, 2, r, parts * w)

    def settle(pieces):
        whole = jnp.concatenate(pieces, -1)
        mine = lax.psum_scatter(whole, both, scatter_dimension=0, axis_index_groups=groups)
        theirs = lax.ppermute(mine[1], "mp", partner)
        keep = mine[0].astype(F32)
        theirs = theirs.astype(F32)
        return jnp.stack([jnp.where(view == 0, keep, theirs), jnp.where(view == 0, theirs, keep)], 0)

    sum_f = settle([packed(grad_up, 1, fw), packed(grad_down, 1, fw)])
    sum_a = settle([packed(grad_qkv, 3, hw), packed(grad_out, 1, hw), packed(grad_cq, 1, hw), packed(grad_ckv, 2, hw), packed(grad_cout, 1, hw)])

    def bias_sum(g, parts, w):
        total = jnp.sum(g.astype(F32), 0).reshape(parts, 2, batches, w)
        return jnp.where(view == 0, total, total[:, ::-1]).reshape(-1)

    small = [gg1, gs1, jnp.sum(d_branch.astype(F32), 0), gg2, gs2, ggy, gsy, jnp.sum(d_cross.astype(F32), 0), gg3, gs3, jnp.sum(dz, 0)]
    bias_q = jnp.concatenate([bias_sum(dq, 1, hw), bias_sum(dk, 1, hw), bias_sum(dv, 1, hw)])
    bias_ckv = jnp.concatenate([bias_sum(dck, 1, hw), bias_sum(dcv, 1, hw)])
    flat = jnp.concatenate(small + [bias_q, bias_sum(dcq, 1, hw), bias_ckv, bias_sum(d_hidden, 1, fw)])
    flat = jnp.stack([jnp.where(view == 0, flat, 0.0), jnp.where(view == 1, flat, 0.0)], 0)
    total = lax.psum(flat, both)
    sm = [total[:, i * width : (i + 1) * width] for i in range(11)]
    at = 11 * width

    def bias_out(start, parts, w):
        piece = total[:, start : start + parts * members * w].reshape(2, parts, members, w)
        piece = lax.dynamic_index_in_dim(piece, me, 2, keepdims=False)
        return piece if parts > 1 else piece[:, 0]

    qkv_bias_grad = bias_out(at, 3, hw)
    cq_bias_grad = bias_out(at + 3 * width, 1, hw)
    ckv_bias_grad = bias_out(at + 4 * width, 2, hw)
    up_bias_grad = bias_out(at + 6 * width, 1, fw)

    back = lax.all_to_all(output.reshape(members, local, width), "mp", 0, 0, tiled=True)
    block_output = back.reshape(2, batches, local, width).swapaxes(0, 1)
    sent = jnp.stack([own.astype(BF).reshape(members, local, width), other.astype(BF).reshape(members, local, width)], 1)
    got = lax.all_to_all(sent, "mp", 0, 0, tiled=True).astype(F32).reshape(2, batches, 2, local, width)
    input_grad = (got[:, :, 0] + got[::-1, :, 1]).swapaxes(0, 1)

    qkv_wg = sum_a[..., : 3 * hw].reshape(2, r, 3, hw)
    out_wg = sum_a[..., 3 * hw : 4 * hw].swapaxes(1, 2)
    cq_wg = sum_a[..., 4 * hw : 5 * hw]
    ckv_wg = sum_a[..., 5 * hw : 7 * hw].reshape(2, r, 2, hw)
    cout_wg = sum_a[..., 7 * hw :].swapaxes(1, 2)
    up_wg = sum_f[..., :fw]
    down_wg = sum_f[..., fw:].swapaxes(1, 2)
    return (block_output, input_grad, sm[0], sm[1], qkv_wg, qkv_bias_grad, out_wg, sm[2], sm[3], sm[4], sm[5], sm[6], cq_wg, cq_bias_grad,
            ckv_wg, ckv_bias_grad, cout_wg, sm[7], sm[8], sm[9], up_wg, up_bias_grad, down_wg, sm[10])


def solution(mesh):
    rows = P(None, None, ("dp", "mp"), None)
    wide = P(None, "dp", None, "mp")
    by_rows = P(None, "dp", "mp")
    by_cols = P(None, "mp", "dp")
    parts = P(None, None, "mp")
    flat = P(None, "mp")
    whole = P()
    in_specs = (rows, rows, P(None, "dp", None), whole, whole, wide, parts, by_cols, whole, whole, whole, whole, whole, by_rows, flat, wide, parts,
                by_cols, whole, whole, whole, by_rows, flat, by_cols, whole)
    out_specs = (rows, rows, whole, whole, wide, parts, by_cols, whole, whole, whole, whole, whole, by_rows, flat, wide, parts, by_cols, whole,
                 whole, whole, by_rows, flat, by_cols, whole)
    return jax.shard_map(body, mesh=mesh, in_specs=in_specs, out_specs=out_specs, check_vma=False)
```

```python
import functools
import math

import jax
import jax.numpy as jnp
from jax import lax
from jax.experimental import pallas as pl
from jax.experimental.pallas import tpu as pltpu
from jax.sharding import PartitionSpec as P

HEAD_DIM = 64
PAIR = 2 * HEAD_DIM
FAR = 1e30
BF = jnp.bfloat16
F32 = jnp.float32
LONGEST = 768
ROWS = 256
TALL = 1024
CHEAP = 16
FFN_ROWS = 1024
PART = 768
norm_epsilon = 1e-06


def mm(a, b):
    return jnp.dot(a, b, preferred_element_type=F32)


def mm_t(a, b):
    return lax.dot_general(a, b, (((1,), (1,)), ((), ())), preferred_element_type=F32)


def t_mm(a, b):
    return lax.dot_general(a, b, (((0,), (0,)), ((), ())), preferred_element_type=F32)


def each(count, size, step, carry=None):
    def go(i, c):
        return step(i, pl.ds(pl.multiple_of(i * size, size), size), c)

    return lax.fori_loop(0, count // size, go, carry)


def normed(rows, gain, shift):
    centred = rows - jnp.mean(rows, -1, keepdims=True)
    spread = jnp.mean(centred * centred, -1, keepdims=True)
    return (centred * lax.rsqrt(spread + norm_epsilon) * gain + shift).astype(BF)


def norm_back(grad, rows, gain):
    centred = rows - jnp.mean(rows, -1, keepdims=True)
    scale = lax.rsqrt(jnp.mean(centred * centred, -1, keepdims=True) + norm_epsilon)
    hat = centred * scale
    w = grad * gain
    back = scale * (w - jnp.mean(w, -1, keepdims=True) - hat * jnp.mean(w * hat, -1, keepdims=True))
    return back, col_sum(grad * hat), col_sum(grad)


def col_sum(a):
    return jnp.sum(a, 0, keepdims=True)


def swap_halves(u):
    lane = lax.broadcasted_iota(jnp.int32, u.shape, 1)
    half = HEAD_DIM // 2
    return jnp.where(lane % HEAD_DIM < half, pltpu.roll(u, PAIR - half, 1), pltpu.roll(u, half, 1))


def turn(u, cosine, sine):
    return u * cosine + swap_halves(u) * sine


def turn_back(u, cosine, sine):
    return u * cosine - swap_halves(u) * sine


def other_half(u):
    return pltpu.roll(u.astype(F32), HEAD_DIM, 1).astype(u.dtype)


def is_low(count):
    return lax.broadcasted_iota(jnp.int32, (count, PAIR), 1) < HEAD_DIM


def matrix(ref, start=0, stop=None):
    stop = ref.shape[4] if stop is None else stop
    return ref[:, 0, 0, :, start:stop].reshape(ref.shape[0] * ref.shape[3], stop - start)


def put_rows(ref, i, value, cols=None):
    blocks, rows = ref.shape[0], ref.shape[3]
    cols = slice(None) if cols is None else cols
    value = value.astype(ref.dtype)
    if blocks == 1:
        ref[0, 0, 0, pl.ds(pl.multiple_of(i * PART, PART), PART), cols] = value
    else:
        k = PART // rows
        ref[pl.ds(i * k, k), 0, 0, :, cols] = value.reshape(k, rows, value.shape[-1])


def store_heads(ref, at, tiles, cosine, sine):
    low = is_low(tiles[0].shape[0])
    scale = HEAD_DIM ** -0.5
    mixed = turn(tiles[1], cosine, sine)
    done = (turn(tiles[0], cosine, sine) * scale, jnp.where(low, mixed * scale, mixed), turn(tiles[2], cosine, sine), tiles[3], tiles[4])
    for i, tile in enumerate(done):
        ref[0, at, i * PAIR : (i + 1) * PAIR] = tile.astype(BF)


def split_tiles(a):
    return [a[:, i * PAIR : (i + 1) * PAIR] for i in range(a.shape[1] // PAIR)]


def norm_kernel(x_ref, gain_ref, shift_ref, n_ref):
    n_ref[...] = normed(x_ref[...].astype(F32), gain_ref[...], shift_ref[...])


def self_in_kernel(n_ref, w_ref, bias_ref, cos_ref, sin_ref, heads_ref):
    w = matrix(w_ref, 0, 5 * PAIR)
    bias = bias_ref[0, :, : 5 * PAIR]

    def one(i, at, c):
        store_heads(heads_ref, at, split_tiles(mm(n_ref[at, :], w) + bias), cos_ref[at, :], sin_ref[at, :])

    each(n_ref.shape[0], TALL, one)


def cross_in_kernel(n_ref, side_ref, w_ref, bias_ref, cos_ref, sin_ref, heads_ref):
    wq = matrix(w_ref, 0, 2 * PAIR)
    wkv = matrix(w_ref, PAIR, 5 * PAIR)
    bias = split_tiles(bias_ref[0, :, : 5 * PAIR])
    low = is_low(TALL)

    def one(i, at, c):
        q0, q2 = split_tiles(mm(n_ref[at, :], wq))
        k2, k0, v0, v2 = split_tiles(mm(side_ref[at, :], wkv))
        tiles = [q0, jnp.where(low, q2, k2), k0, v0, v2]
        store_heads(heads_ref, at, [t + b for t, b in zip(tiles, bias)], cos_ref[at, :], sin_ref[at, :])

    each(n_ref.shape[0], TALL, one)


def spans(rows):
    return ((0, LONGEST), (LONGEST, rows - LONGEST))


def attend_kernel(heads_ref, qf_ref, kf_ref, o_ref, lse_ref, *, tile):
    rows = heads_ref.shape[1]
    for start, size in spans(rows):
        near = pl.ds(start, size)
        low = is_low(size)
        t3, t1, t2, t4 = [heads_ref[0, near, i * PAIR : (i + 1) * PAIR] for i in range(1, 5)]
        kf = kf_ref[near, :]
        one = jnp.ones_like(t2)
        keys = (jnp.where(low, t1, kf), jnp.where(low, kf, t1), jnp.where(low, other_half(t3), kf))
        vals = (jnp.where(low, t2, one), jnp.where(low, one, t2), jnp.where(low, one, other_half(t4)))
        step = min(tile, size)
        low_t = is_low(step)
        for t in range(size // step):
            at = pl.ds(start + t * step, step)
            qf = qf_ref[at, :]
            q0 = heads_ref[0, at, :PAIR]
            queries = (jnp.where(low_t, q0, qf), jnp.where(low_t, qf, q0), jnp.where(low_t, heads_ref[0, at, PAIR : 2 * PAIR], qf))
            outs, lses = [], []
            for h in range(3):
                s = mm_t(queries[h], keys[h])
                top = jnp.max(s, -1, keepdims=True)
                o = mm(jnp.exp(s - top).astype(BF), vals[h])
                total = pltpu.roll(o, HEAD_DIM, 1)
                outs.append(o / total)
                lses.append(top + jnp.log(total))
            o_ref[0, at, :PAIR] = jnp.where(low_t, 0.0, outs[2]).astype(BF)
            o_ref[0, at, PAIR:] = jnp.where(low_t, outs[0], outs[1]).astype(BF)
            lse_ref[0, at, :PAIR] = jnp.where(low_t, 0.0, lses[2])
            lse_ref[0, at, PAIR:] = jnp.where(low_t, lses[0], lses[1])


def three_parts(u):
    a = u.astype(BF).astype(F32)
    b = (u - a).astype(BF).astype(F32)
    return a, b, u - a - b


def attend_back_kernel(heads_ref, o_ref, do_ref, lse_ref, qf_ref, kf_ref, cos_ref, sin_ref, out_ref, dq2_acc, dk_acc, dv_acc, *, tile):
    rows = heads_ref.shape[1]
    scale = HEAD_DIM ** -0.5
    for start, size in spans(rows):
        near = pl.ds(start, size)
        low = is_low(size)
        within = lax.broadcasted_iota(jnp.int32, (size, PAIR), 1) % HEAD_DIM
        t3, t1, t2, t4 = [heads_ref[0, near, i * PAIR : (i + 1) * PAIR] for i in range(1, 5)]
        ones3 = jnp.where(within < 3, 1.0, 0.0).astype(BF)
        kf = kf_ref[near, :] + jnp.where((within >= 3) & (within < 6), 1.0, 0.0).astype(BF)
        k2 = other_half(t3)
        raw_keys = (t1, t1, k2)
        keys = (jnp.where(low, t1, kf), jnp.where(low, kf, t1), jnp.where(low, k2, kf))
        vals = (jnp.where(low, t2, ones3), jnp.where(low, ones3, t2), jnp.where(low, t4, ones3))
        step = min(tile, size)
        low_t = is_low(step)
        high_t = ~low_t
        within_t = lax.broadcasted_iota(jnp.int32, (step, PAIR), 1) % HEAD_DIM
        for t in range(size // step):
            at = pl.ds(start + t * step, step)
            q0, q2 = heads_ref[0, at, :PAIR], heads_ref[0, at, PAIR : 2 * PAIR]
            do2, do0 = do_ref[0, at, :PAIR], do_ref[0, at, PAIR:]
            prod2 = do2.astype(F32) * o_ref[0, at, :PAIR].astype(F32)
            prod0 = do0.astype(F32) * o_ref[0, at, PAIR:].astype(F32)
            lse2, lse0 = lse_ref[0, at, :PAIR], lse_ref[0, at, PAIR:]
            qf = qf_ref[at, :].astype(F32)
            lse_swapped = pltpu.roll(lse0, HEAD_DIM, 1)
            items = ((q0, do0, low_t, low_t, prod0, lse_swapped), (q0, do0, high_t, high_t, prod0, lse_swapped), (q2, other_half(do2), low_t, high_t, prod2, lse2))
            dqs = []
            for h, (q, do, mine, where_o, prod, lse) in enumerate(items):
                a, b, c = three_parts(-jnp.sum(jnp.where(where_o, prod, 0.0), -1, keepdims=True))
                feat = jnp.where(within_t == 0, a, jnp.where(within_t == 1, b, jnp.where(within_t == 2, c, 0.0)))
                doh = jnp.where(mine, do, feat.astype(BF))
                a, b, c = three_parts(-lse)
                feat = jnp.where(within_t == 3, a, jnp.where(within_t == 4, b, jnp.where(within_t == 5, c, qf)))
                qh = jnp.where(mine, q, feat.astype(BF))
                p = jnp.exp(mm_t(keys[h], qh))
                ds = (p * mm_t(vals[h], doh)).astype(BF)
                dv = mm(p.astype(BF), do)
                dk = mm(ds, q)
                dqs.append(t_mm(ds, raw_keys[h]) * scale)
                if t == 0:
                    dv_acc[h, near, :] = dv
                    dk_acc[h, near, :] = dk
                else:
                    dv_acc[h, near, :] += dv
                    dk_acc[h, near, :] += dk
            dq = jnp.where(low_t, dqs[0], dqs[1])
            out_ref[0, at, :PAIR] = turn_back(dq, cos_ref[at, :], sin_ref[at, :]).astype(BF)
            dq2_acc[at, :] = dqs[2]

    def finish(i, at, c):
        low_r = is_low(ROWS)
        cosine, sine = cos_ref[at, :], sin_ref[at, :]
        out_ref[0, at, 2 * PAIR : 3 * PAIR] = turn_back(jnp.where(low_r, dk_acc[0, at, :], dk_acc[1, at, :]), cosine, sine).astype(BF)
        out_ref[0, at, 3 * PAIR : 4 * PAIR] = jnp.where(low_r, dv_acc[0, at, :], dv_acc[1, at, :]).astype(BF)
        last = jnp.where(low_r, dq2_acc[at, :], pltpu.roll(dk_acc[2, at, :], HEAD_DIM, 1))
        out_ref[0, at, PAIR : 2 * PAIR] = turn_back(last, cosine, sine).astype(BF)
        out_ref[0, at, 4 * PAIR :] = jnp.where(low_r, dv_acc[2, at, :], 0.0).astype(BF)

    each(rows, ROWS, finish)


def out_kernel(att_ref, w_ref, res_ref, bias_ref, gain_ref, shift_ref, mid_ref, n_ref):
    blocks, batches, two, deep, cols = w_ref.shape
    total = None
    for b in range(batches):
        for t in range(two):
            part = mm_t(att_ref[2 * b + t], w_ref[:, b, t].reshape(blocks * deep, cols))
            total = part if total is None else total + part
    mid = res_ref[...].astype(F32) + total + bias_ref[...]
    mid_ref[...] = mid
    n_ref[...] = normed(mid, gain_ref[...], shift_ref[...])


def clear(*refs):
    @pl.when(pl.program_id(0) == 0)
    def _():
        def zero(i, at, c):
            for ref in refs:
                ref[at, :] = jnp.zeros((ROWS, ref.shape[1]), F32)

        each(refs[0].shape[0], ROWS, zero)


def ffn_kernel(mid_ref, n_ref, dz_ref, up_ref, down_ref, upb_ref, downb_ref, gain_ref,
               out_ref, dmid_ref, dlow_ref, dw_ref, dupb_ref, dgain_ref, dshift_ref, ddownb_ref, dcob_ref,
               acc_out, acc_dn, hid, dhid):
    j = pl.program_id(0)
    rows = mid_ref.shape[0]
    width = mid_ref.shape[1]
    up = matrix(up_ref)
    down = matrix(down_ref)
    bias = upb_ref[0]
    clear(acc_out, acc_dn)

    def one(i, at, total):
        h = mm(n_ref[at, :], up) + bias
        phi = 0.5 * (1.0 + lax.erf(h * (0.5 ** 0.5)))
        slope = phi + h * jnp.exp(-0.5 * h * h) * (0.5 / math.pi) ** 0.5
        low = (h * phi).astype(BF)
        hid[at, :] = low
        acc_out[at, :] += mm_t(low, down)
        d = (mm(dz_ref[at, :], down) * slope).astype(BF)
        dhid[at, :] = d
        acc_dn[at, :] += mm_t(d, up)
        return total + col_sum(d.astype(F32))

    dupb_ref[0] = each(rows, FFN_ROWS, one, jnp.zeros((1, up.shape[1]), F32))

    def weight(i, at, c):
        put_rows(dw_ref, i, t_mm(n_ref[:, at], dhid[...]), slice(0, dhid.shape[1]))
        put_rows(dw_ref, i, t_mm(dz_ref[:, at], hid[...]), slice(dhid.shape[1], None))

    each(width, PART, weight)

    @pl.when(j == pl.num_programs(0) - 1)
    def _():
        def last(i, at, sums):
            mid = mid_ref[at, :]
            out_ref[at, :] = (mid + acc_out[at, :] + downb_ref[...]).astype(BF)
            back, dg, ds = norm_back(acc_dn[at, :], mid, gain_ref[...])
            dz = dz_ref[at, :].astype(F32)
            total = dz + back
            dmid_ref[at, :] = total
            low = total.astype(BF)
            dlow_ref[at, :] = low
            return tuple(s + a for s, a in zip(sums, (dg, ds, col_sum(dz), col_sum(low.astype(F32)))))

        sums = each(rows, ROWS, last, (jnp.zeros((1, width), F32),) * 4)
        dgain_ref[...], dshift_ref[...], ddownb_ref[...], dcob_ref[...] = sums


def out_back_kernel(d_ref, w_ref, datt_ref):
    datt_ref[0] = mm(d_ref[...], matrix(w_ref)).astype(BF)


def cross_back_kernel(dh_ref, w_ref, n_ref, side_ref, dlow_ref, att_ref, mid_ref, y_ref, dmid_ref, gain_ref, gainy_ref,
                      dw_ref, dbias_ref, dout_ref, dbranch_ref, other_ref, dg_ref, ds_ref, dgy_ref, dsy_ref, dob_ref,
                      acc_n, acc_side):
    j = pl.program_id(0)
    rows, width = mid_ref.shape
    wq = matrix(w_ref, 0, 2 * PAIR)
    wkv = matrix(w_ref, PAIR, 5 * PAIR)
    low = is_low(TALL)
    nought = jnp.zeros((TALL, PAIR), BF)
    clear(acc_n, acc_side)

    def one(i, at, total):
        d = dh_ref[0, at, :]
        t0, t1, t2, t3, t4 = split_tiles(d)
        acc_n[at, :] += mm_t(jnp.concatenate([t0, jnp.where(low, t1, nought)], 1), wq)
        acc_side[at, :] += mm_t(jnp.concatenate([jnp.where(low, nought, t1), t2, t3, t4], 1), wkv)
        return total + col_sum(d.astype(F32))

    dbias_ref[0] = each(rows, TALL, one, jnp.zeros((1, 5 * PAIR), F32))
    low_p = is_low(PART)

    def weight(i, at, c):
        dq = t_mm(n_ref[:, at], dh_ref[0, :, : 2 * PAIR])
        dkv = t_mm(side_ref[:, at], dh_ref[0, :, PAIR:])
        do = t_mm(dlow_ref[:, at], att_ref[0])
        put_rows(dw_ref, i, dq[:, :PAIR], slice(0, PAIR))
        put_rows(dw_ref, i, jnp.where(low_p, dq[:, PAIR:], dkv[:, :PAIR]), slice(PAIR, 2 * PAIR))
        put_rows(dw_ref, i, dkv[:, PAIR : 3 * PAIR], slice(2 * PAIR, 4 * PAIR))
        put_rows(dw_ref, i, dkv[:, 3 * PAIR :] + do[:, :PAIR], slice(4 * PAIR, 5 * PAIR))
        put_rows(dw_ref, i, do[:, PAIR:], slice(5 * PAIR, 6 * PAIR))

    each(width, PART, weight)

    @pl.when(j == pl.num_programs(0) - 1)
    def _():
        def last(i, at, sums):
            back, dg, ds = norm_back(acc_n[at, :], mid_ref[at, :], gain_ref[...])
            total = dmid_ref[at, :] + back
            dout_ref[at, :] = total
            branch = total.astype(BF)
            dbranch_ref[at, :] = branch
            other, dgy, dsy = norm_back(acc_side[at, :], y_ref[at, :].astype(F32), gainy_ref[...])
            other_ref[at, :] = other.astype(BF)
            return tuple(s + a for s, a in zip(sums, (dg, ds, dgy, dsy, col_sum(branch.astype(F32)))))

        sums = each(rows, ROWS, last, (jnp.zeros((1, width), F32),) * 5)
        dg_ref[...], ds_ref[...], dgy_ref[...], dsy_ref[...], dob_ref[...] = sums


def self_back_part(dh_ref, w_ref, n_ref, dlow_ref, att_ref, dw_ref, dbias_ref, acc_ref):
    rows, width = n_ref.shape
    w = matrix(w_ref, 0, 5 * PAIR)
    clear(acc_ref)

    def one(i, at, total):
        d = dh_ref[0, at, :]
        acc_ref[at, :] += mm_t(d, w)
        return total + col_sum(d.astype(F32))

    dbias_ref[0] = each(rows, TALL, one, jnp.zeros((1, 5 * PAIR), F32))

    def weight(i, at, c):
        dqkv = t_mm(n_ref[:, at], dh_ref[0])
        do = t_mm(dlow_ref[:, at], att_ref[0])
        put_rows(dw_ref, i, dqkv[:, : 4 * PAIR], slice(0, 4 * PAIR))
        put_rows(dw_ref, i, dqkv[:, 4 * PAIR :] + do[:, :PAIR], slice(4 * PAIR, 5 * PAIR))
        put_rows(dw_ref, i, do[:, PAIR:], slice(5 * PAIR, 6 * PAIR))

    each(width, PART, weight)


def self_back_first_kernel(dh_ref, w_ref, n_ref, dlow_ref, att_ref, dw_ref, dbias_ref, acc_ref):
    self_back_part(dh_ref, w_ref, n_ref, dlow_ref, att_ref, dw_ref, dbias_ref, acc_ref)


def self_back_last_kernel(dh_ref, w_ref, n_ref, dlow_ref, att_ref, x_ref, dmid_ref, before_ref, gain_ref,
                          dw_ref, dbias_ref, own_ref, dg_ref, ds_ref, acc_ref):
    j = pl.program_id(0)
    rows, width = x_ref.shape
    self_back_part(dh_ref, w_ref, n_ref, dlow_ref, att_ref, dw_ref, dbias_ref, acc_ref)

    @pl.when(j == pl.num_programs(0) - 1)
    def _():
        def last(i, at, sums):
            back, dg, ds = norm_back(acc_ref[at, :] + before_ref[at, :], x_ref[at, :].astype(F32), gain_ref[...])
            own_ref[at, :] = (dmid_ref[at, :] + back).astype(BF)
            return sums[0] + dg, sums[1] + ds

        dg_ref[...], ds_ref[...] = each(rows, ROWS, last, (jnp.zeros((1, width), F32),) * 2)


def tables(image_sizes, count):
    images = image_sizes.shape[0]
    ends = jnp.cumsum(image_sizes)
    first = jnp.sum(jnp.where(image_sizes == LONGEST, ends - image_sizes, 0))
    places = (jnp.arange(count, dtype=jnp.int32) + first) % count
    passed = places[:, None] >= ends[None, :]
    segment = jnp.sum(passed.astype(jnp.int32), -1)
    start = jnp.sum(jnp.where(passed, image_sizes[None, :], 0), -1)
    place = (places - start).astype(F32)
    half = HEAD_DIM // 2
    lane = jnp.arange(PAIR, dtype=jnp.int32)
    freqs = 100.0 ** (-((lane % half).astype(F32) / half))
    angles = place[:, None] * freqs[None, :]
    sign = jnp.where(lane % HEAD_DIM < half, -1.0, 1.0)
    member = (lane % HEAD_DIM)[None, :] == segment[:, None]
    slot = ((lane % HEAD_DIM) < images)[None, :]
    kf = member.astype(BF)
    qf = jnp.where(slot & ~member, -FAR, 0.0).astype(BF)
    return first, qf, kf, jnp.cos(angles), jnp.sin(angles) * sign[None, :]


def whole(a):
    return pl.BlockSpec(a.shape, lambda j: (0,) * a.ndim)


def per_step(a, side=None):
    return pl.BlockSpec((1,) + a.shape[1:], lambda j: (j if side is None else 2 * j + side,) + (0,) * (a.ndim - 1))


def weight_block(g, cols, at, side=None):
    return pl.BlockSpec((g.shape[0], 1, 1, g.shape[3], cols), lambda j: (0, j // 2, j % 2, 0, at) if side is None else (0, j, side, 0, at))


def sds(shape, dtype):
    return jax.ShapeDtypeStruct(shape, dtype)


def call(kernel, name, steps, ins, outs, scratch=(), flops=0, moved=0, exps=0):
    return pl.pallas_call(
        kernel,
        grid=(steps,),
        in_specs=[s for _, s in ins],
        out_specs=[s for _, s in outs],
        out_shape=[o for o, _ in outs],
        scratch_shapes=list(scratch),
        cost_estimate=pl.CostEstimate(flops=int(flops) // CHEAP, bytes_accessed=int(moved) // CHEAP, transcendentals=int(exps) // CHEAP),
        name=name,
    )(*[a for a, _ in ins])


def body(tokens, cotangent, lengths, norm1_gain, norm1_shift, qkv_w, qkv_b, out_w, out_b, norm2_gain, norm2_shift,
         normy_gain, normy_shift, cq_w, cq_b, ckv_w, ckv_b, cout_w, cout_b, norm3_gain, norm3_shift, up_w, up_b, down_w, down_b):
    batches = tokens.shape[0]
    members = lax.axis_size("mp")
    n_dp = lax.axis_size("dp")
    assert members == 2 * batches
    me = lax.axis_index("mp")
    view = me // batches
    batch = me % batches
    local = tokens.shape[2]
    rows = local * members
    width = tokens.shape[3]
    r = qkv_w.shape[1]
    hw = cq_w.shape[2]
    fw = up_w.shape[2]
    partner = [(i, (i + batches) % members) for i in range(members)]
    groups = [[d * members + v * batches + b for d in range(n_dp) for b in range(batches)] for v in range(2)]
    both = ("dp", "mp")
    split = r % 16 == 0
    blocks, deep = (n_dp, r) if split else (1, n_dp * r)

    def of_view(a, which):
        return lax.dynamic_index_in_dim(a, which, 0, keepdims=False)

    def cols(q, k, v, o):
        return jnp.concatenate([q, k[..., PAIR:], k[..., :PAIR], v, o[..., PAIR:], o[..., :PAIR]], -1)

    def uncols(a):
        t = [a[..., i * PAIR : (i + 1) * PAIR] for i in range(a.shape[-1] // PAIR)]
        h = HEAD_DIM
        join = lambda x, y: jnp.concatenate([x, y], -1)
        heads = (join(t[0], t[1][..., :h]), join(t[2], t[1][..., h:]), join(t[3], t[4][..., :h]))
        return heads + ((join(t[5], t[4][..., h:]),) if len(t) > 5 else ())

    def gather(pack):
        pair = jnp.stack([of_view(pack, view), lax.ppermute(of_view(pack, 1 - view), "mp", partner)], 0)
        got = lax.all_gather(pair, both, axis=0, axis_index_groups=groups).reshape(n_dp, batches, 2, r, -1)
        return got if split else got.transpose(1, 2, 0, 3, 4).reshape(1, batches, 2, deep, -1)

    flip = lambda a: a.swapaxes(-1, -2)
    pack_self = cols(qkv_w[:, :, 0], qkv_w[:, :, 1], qkv_w[:, :, 2], flip(out_w))
    pack_cross = cols(cq_w, ckv_w[:, :, 0], ckv_w[:, :, 1], flip(cout_w))
    w_att = gather(jnp.concatenate([pack_self, pack_cross], -1))
    w_ffn = gather(jnp.concatenate([up_w, flip(down_w)], -1))

    none = jnp.zeros_like(cq_b)
    bias_pack = jnp.concatenate([cols(qkv_b[:, 0], qkv_b[:, 1], qkv_b[:, 2], none), cols(cq_b, ckv_b[:, 0], ckv_b[:, 1], none), up_b], -1)
    bias_rows = bias_pack.shape[-1] // width
    bias_pack = jnp.broadcast_to(bias_pack.reshape(2, 1, bias_rows, width), (2, batches, bias_rows, width))
    by_view = tokens.swapaxes(0, 1)
    sent_x = jnp.concatenate([by_view, bias_pack], 2).reshape(members, local + bias_rows, width)
    got_x = lax.all_to_all(sent_x, "mp", 0, 0, tiled=True)
    got_y = lax.all_to_all(by_view[::-1].reshape(members, local, width), "mp", 0, 0, tiled=True)
    got_z = lax.all_to_all(cotangent.swapaxes(0, 1).reshape(members, local, width), "mp", 0, 0, tiled=True)
    first, qf, kf, cosine, sine = tables(of_view(lengths[:, 0], batch), rows)

    def from_row(a, at):
        return lax.dynamic_slice_in_dim(jnp.concatenate([a, a], 0), at, rows, 0)

    x = from_row(got_x[:, :local].reshape(rows, width), first)
    y = from_row(got_y.reshape(rows, width), first)
    dz = from_row(got_z.reshape(rows, width), first)

    def by_step(a):
        a = a.reshape((2, batches) + a.shape[1:])
        return jnp.where(view == 0, a, a[::-1]).swapaxes(0, 1).reshape((members,) + a.shape[2:])

    def by_member(a):
        a = a.reshape((batches, 2) + a.shape[1:]).swapaxes(0, 1)
        return jnp.where(view == 0, a, a[::-1]).reshape((members,) + a.shape[2:])

    biases = by_step(got_x[:, local:]).astype(F32)
    self_bias, cross_bias, up_bias = biases[:, 0:1], biases[:, 1:2], biases[:, 2:]
    up_bias = up_bias.reshape(members, 1, fw)

    def mine(a):
        return of_view(a, view).astype(F32)[None]

    g1, s1, ob, g2, s2, gy, sy, cob, g3, s3, db = [
        mine(a) for a in (norm1_gain, norm1_shift, out_b, norm2_gain, norm2_shift, normy_gain, normy_shift, cout_b, norm3_gain, norm3_shift, down_b)]
    def given(*arrays):
        return [(a, whole(a)) for a in arrays]

    def steps(*arrays):
        return [(a, per_step(a)) for a in arrays]

    def full(*shape_types):
        return [(s, whole(s)) for s in shape_types]

    low = sds((rows, width), BF)
    high = sds((rows, width), F32)
    line = sds((1, width), F32)
    heads = sds((members, rows, 5 * PAIR), BF)
    att_low = sds((members, rows, 2 * PAIR), BF)
    att_high = sds((members, rows, 2 * PAIR), F32)
    bias_out = sds((members, 1, 5 * PAIR), F32)
    gemm = 2 * rows * width * width * members

    def attend(h):
        return call(functools.partial(attend_kernel, tile=384), "attend", members, steps(h) + given(qf, kf), [(s, per_step(s)) for s in (att_low, att_high)],
                    flops=12 * members * rows * rows * PAIR, moved=members * rows * PAIR * 22, exps=3 * members * rows * rows)

    def attend_back(h, o, do, lse, side=None):
        count = members if side is None else batches
        out = sds((count, rows, 5 * PAIR), BF)
        acc = pltpu.VMEM((3, rows, PAIR), F32)
        ins = [(a, per_step(a, side)) for a in (h, o, do, lse)]
        return call(functools.partial(attend_back_kernel, tile=256), "attend_back", count, ins + given(qf, kf, cosine, sine), [(out, per_step(out))],
                    [pltpu.VMEM((rows, PAIR), F32), acc, acc], flops=30 * count * rows * rows * PAIR, moved=count * rows * PAIR * 40,
                    exps=3 * count * rows * rows)[0]

    def project(att, at, res, bias, gain, shift):
        tall = 512
        part = lambda cols: pl.BlockSpec((tall, cols), lambda i: (i, 0))
        att_spec = pl.BlockSpec((members, tall, 2 * PAIR), lambda i: (0, i, 0))
        w_spec = pl.BlockSpec((blocks, batches, 2, deep, 2 * PAIR), lambda i: (0, 0, 0, 0, at))
        return call(out_kernel, "project", rows // tall, [(att, att_spec), (w_att, w_spec), (res, part(width))] + given(bias, gain, shift),
                    [(high, part(width)), (low, part(width))], flops=gemm / 3, moved=rows * width * 14)

    def project_back(d, at):
        return call(out_back_kernel, "project_back", members, given(d) + [(w_att, weight_block(w_att, 2 * PAIR, at))], [(att_low, per_step(att_low))],
                    flops=gemm / 3, moved=rows * width * 8)[0]

    def norm(a, gain, shift):
        spec = pl.BlockSpec((ROWS, width), lambda i: (i, 0))
        return call(norm_kernel, "norm", rows // ROWS, [(a, spec)] + given(gain, shift), [(low, spec)], moved=rows * width * 4)[0]

    def by_owner(piece):
        if not split:
            piece = piece.reshape(batches, piece.shape[2], n_dp, r, -1).transpose(2, 0, 1, 3, 4)
        return piece

    def scatter(piece):
        return lax.psum_scatter(by_owner(piece).reshape(n_dp * batches, 2, r, -1), both, scatter_dimension=0, axis_index_groups=groups)

    core_pairs = [(i, i ^ 1) for i in range(members)]
    x_pairs = [(i, i ^ 1) for i in range(n_dp)]
    place = lax.axis_index("dp")
    lines = n_dp // 2

    def pick(a, i, axis):
        return lax.dynamic_index_in_dim(a, i, axis, keepdims=False)

    by_hand = batches == 2 and n_dp <= 8

    def over_cores(piece):
        got = lax.ppermute(pick(piece, 1 - batch, 1), "mp", core_pairs)
        return (pick(piece, batch, 1).astype(F32) + got.astype(F32)).astype(BF)

    def over_x(piece):
        piece = piece.reshape((piece.shape[0] // 2, 2) + piece.shape[1:])
        got = lax.ppermute(pick(piece, 1 - place % 2, 1), "dp", x_pairs)
        return (pick(piece, place % 2, 1).astype(F32) + got.astype(F32)).astype(BF)

    def over_z(piece):
        total = pick(piece, place // 2, 0).astype(F32)
        for s in range(1, lines):
            perm = [(i, (i + 2 * s) % n_dp) for i in range(n_dp)]
            total = total + lax.ppermute(pick(piece, (place // 2 + s) % lines, 0), "dp", perm).astype(F32)
        return total.astype(BF)

    def settle(total):
        theirs = lax.ppermute(total[1], "mp", partner).astype(F32)
        keep = total[0].astype(F32)
        return jnp.stack([jnp.where(view == 0, keep, theirs), jnp.where(view == 0, theirs, keep)], 0)

    n1 = norm(x, g1, s1)
    side = norm(y, gy, sy)
    hs = call(self_in_kernel, "self_in", members, given(n1) + [(w_att, weight_block(w_att, 6 * PAIR, 0))] + steps(self_bias) + given(cosine, sine),
              [(heads, per_step(heads))], flops=gemm, moved=rows * width * 16)[0]
    att, lse = attend(hs)
    middle, n2 = project(att, 2, x, ob, g2, s2)
    hc = call(cross_in_kernel, "cross_in", members, given(n2, side) + [(w_att, weight_block(w_att, 6 * PAIR, 1))] + steps(cross_bias) + given(cosine, sine),
              [(heads, per_step(heads))], flops=gemm, moved=rows * width * 16)[0]
    catt, clse = attend(hc)
    middle2, n3 = project(catt, 5, middle, cob, g3, s3)

    dw_ffn = sds((blocks, batches, 2, deep, 2 * fw), BF)
    dw_ffn_spec = pl.BlockSpec((blocks, 1, 1, deep, 2 * fw), lambda j: (0, j // 2, j % 2, 0, 0))
    up_line = sds((members, 1, fw), F32)
    output, d_mid2, d_cross, dw_f, d_upb, gg3, gs3, d_db, d_cob = call(
        ffn_kernel, "ffn", members,
        given(middle2, n3, dz) + [(w_ffn, weight_block(w_ffn, fw, 0)), (w_ffn, weight_block(w_ffn, fw, 1))] + steps(up_bias) + given(db, g3),
        full(low, high, low) + [(dw_ffn, dw_ffn_spec), (up_line, per_step(up_line))] + full(line, line, line, line),
        [pltpu.VMEM((rows, width), F32)] * 2 + [pltpu.VMEM((rows, fw), BF)] * 2,
        flops=6 * gemm, moved=rows * width * 60, exps=rows * fw * members * 2)

    total_ffn = scatter(dw_f)
    d_catt = project_back(d_cross, 5)
    d_hc = attend_back(hc, catt, d_catt, clse)
    dw_att = sds((blocks, batches, 2, deep, 6 * PAIR), BF)
    dw_spec = pl.BlockSpec((blocks, 1, 1, deep, 6 * PAIR), lambda j: (0, j // 2, j % 2, 0, 0))
    dw_cross, d_crossb, d_mid, d_branch, other, gg2, gs2, ggy, gsy, d_ob = call(
        cross_back_kernel, "cross_back", members,
        steps(d_hc) + [(w_att, weight_block(w_att, 6 * PAIR, 1))] + given(n2, side, d_cross) + steps(catt) + given(middle, y, d_mid2, g2, gy),
        [(dw_att, dw_spec), (bias_out, per_step(bias_out))] + full(high, low, low, line, line, line, line, line),
        [pltpu.VMEM((rows, width), F32)] * 2, flops=3 * gemm, moved=rows * width * 40)
    d_att = project_back(d_branch, 2)
    if by_hand:
        cross = over_cores(by_owner(dw_cross))
        d_att, cross = lax.optimization_barrier((d_att, cross))
        cross_a = over_x(cross[: n_dp // 2])

    dw_part = sds((blocks, batches, 1, deep, 6 * PAIR), BF)
    dw_part_spec = pl.BlockSpec((blocks, 1, 1, deep, 6 * PAIR), lambda j: (0, j, 0, 0, 0))
    bias_part = sds((batches, 1, 5 * PAIR), F32)

    def self_back(t, dh, *more):
        ins = steps(dh) + [(w_att, weight_block(w_att, 6 * PAIR, 0, t))] + given(n1, d_branch) + [(att, per_step(att, t))]
        outs = [(dw_part, dw_part_spec), (bias_part, per_step(bias_part))]
        if more:
            return call(self_back_last_kernel, "self_back_last", batches, ins + given(*more), outs + full(low, line, line),
                        [pltpu.VMEM((rows, width), F32)], flops=1.5 * gemm, moved=rows * width * 30)
        return call(self_back_first_kernel, "self_back_first", batches, ins, outs + full(high), flops=1.5 * gemm, moved=rows * width * 24)

    d_h1 = attend_back(hs, att, d_att, lse, 1)
    if by_hand:
        d_h1, cross, cross_a = lax.optimization_barrier((d_h1, cross, cross_a))
        cross_b = over_x(cross[n_dp // 2 :])
    dw_self1, d_selfb1, acc = self_back(1, d_h1)
    if by_hand:
        d_att, acc, cross_a, cross_b, dw_self1 = lax.optimization_barrier((d_att, acc, cross_a, cross_b, dw_self1))
        cross = over_z(jnp.concatenate([cross_a, cross_b], 0))
        self1 = over_cores(by_owner(dw_self1))
    d_h0 = attend_back(hs, att, d_att, lse, 0)
    if by_hand:
        d_h0, total_ffn, self1, cross = lax.optimization_barrier((d_h0, total_ffn, self1, cross))
        self1 = over_x(self1)
    else:
        d_h0, total_ffn = lax.optimization_barrier((d_h0, total_ffn))
    dw_self0, d_selfb0, own, gg1, gs1 = self_back(0, d_h0, x, d_mid, acc, g1)
    d_selfb = jnp.stack([d_selfb0, d_selfb1], 1).reshape(members, 1, 5 * PAIR)
    sum_ffn = settle(total_ffn)
    if by_hand:
        own, dw_self0, self1 = lax.optimization_barrier((own, dw_self0, self1))
        self0 = over_z(over_x(over_cores(by_owner(dw_self0))))
        self1 = over_z(self1)
        sum_cross = settle(cross)
        sum_self = settle(jnp.concatenate([self0, self1], 0))
    else:
        sum_cross = settle(scatter(dw_cross))
        sum_self = settle(scatter(jnp.concatenate([dw_self0, dw_self1], 2)))

    def over_all(flat):
        for perm in [[(i, i // batches * batches + (i + s) % batches) for i in range(members)] for s in range(1, batches)]:
            flat = flat + lax.ppermute(flat, "mp", perm)
        step = 1
        while step < n_dp:
            flat = flat + lax.ppermute(flat, "dp", [(i, i ^ step) for i in range(n_dp)])
            step *= 2
        theirs = lax.ppermute(flat, "mp", partner)
        return jnp.stack([jnp.where(view == 0, flat, theirs), jnp.where(view == 0, theirs, flat)], 0)

    sums = over_all(jnp.concatenate([gg1, gs1, d_ob, gg2, gs2, ggy, gsy, d_cob, gg3, gs3, d_db] + [by_member(a[:, 0]).reshape(1, -1) for a in (d_selfb, d_crossb, d_upb)], -1)[0])
    g1g, s1g, obg, g2g, s2g, gyg, syg, cobg, g3g, s3g, dbg = [sums[:, i * width : (i + 1) * width] for i in range(11)]
    at_self = 11 * width
    at_cross = at_self + members * 5 * PAIR
    at_up = at_cross + members * 5 * PAIR

    def member_part(flat, size):
        return lax.dynamic_index_in_dim(flat.reshape(2, members, size), me, 1, keepdims=False)

    cross_part = uncols(member_part(sums[:, at_cross:at_up], 5 * PAIR))
    upb_grad = member_part(sums[:, at_up:], fw)
    self_part = uncols(member_part(sums[:, at_self:at_cross], 5 * PAIR))

    output, other, own = [from_row(a, rows - first) for a in (output, other, own)]
    back = lax.all_to_all(output.reshape(members, local, width), "mp", 0, 0, tiled=True)
    block_output = back.reshape(2, batches, local, width).swapaxes(0, 1)
    got_other = lax.all_to_all(other.reshape(members, local, width), "mp", 0, 0, tiled=True).reshape(2, batches, local, width)
    got_own = lax.all_to_all(own.reshape(members, local, width), "mp", 0, 0, tiled=True).reshape(2, batches, local, width)
    input_grad = (got_own.astype(F32) + got_other[::-1].astype(F32)).swapaxes(0, 1)

    q, k, v, o = uncols(sum_self)
    cq, ck, cv, co = uncols(sum_cross)
    return (block_output, input_grad, g1g, s1g, jnp.stack([q, k, v], 2), jnp.stack(self_part, 1), flip(o), obg, g2g, s2g, gyg, syg,
            cq, cross_part[0], jnp.stack([ck, cv], 2), jnp.stack(cross_part[1:], 1), flip(co), cobg, g3g, s3g,
            sum_ffn[..., :fw], upb_grad, flip(sum_ffn[..., fw:]), dbg)


def solution(mesh):
    rows = P(None, None, ("dp", "mp"), None)
    wide = P(None, "dp", None, "mp")
    by_rows = P(None, "dp", "mp")
    by_cols = P(None, "mp", "dp")
    parts = P(None, None, "mp")
    flat = P(None, "mp")
    same = P()
    in_specs = (rows, rows, P(None, "dp", None), same, same, wide, parts, by_cols, same, same, same, same, same, by_rows, flat, wide, parts,
                by_cols, same, same, same, by_rows, flat, by_cols, same)
    out_specs = (rows, rows, same, same, wide, parts, by_cols, same, same, same, same, same, by_rows, flat, wide, parts, by_cols, same,
                 same, same, by_rows, flat, by_cols, same)
    return jax.shard_map(body, mesh=mesh, in_specs=in_specs, out_specs=out_specs, check_vma=False)
```

```python
import functools
import math

import jax
import jax.numpy as jnp
from jax import lax
from jax.experimental import pallas as pl
from jax.experimental.layout import Layout, with_layout_constraint
from jax.experimental.pallas import tpu as pltpu
from jax.sharding import PartitionSpec as P

HEAD_DIM = 64
PAIR = 2 * HEAD_DIM
FAR = 1e30
BF = jnp.bfloat16
F32 = jnp.float32
LONGEST = 768
ROWS = 256
TALL = 1024
CHEAP = 16
FFN_ROWS = 1024
PART = 768
norm_epsilon = 1e-06


def mm(a, b):
    return jnp.dot(a, b, preferred_element_type=F32)


def mm_t(a, b):
    return lax.dot_general(a, b, (((1,), (1,)), ((), ())), preferred_element_type=F32)


def t_mm(a, b):
    return lax.dot_general(a, b, (((0,), (0,)), ((), ())), preferred_element_type=F32)


def each(count, size, step, carry=None):
    def go(i, c):
        return step(i, pl.ds(pl.multiple_of(i * size, size), size), c)

    return lax.fori_loop(0, count // size, go, carry)


def normed(rows, gain, shift):
    centred = rows - jnp.mean(rows, -1, keepdims=True)
    spread = jnp.mean(centred * centred, -1, keepdims=True)
    return (centred * lax.rsqrt(spread + norm_epsilon) * gain + shift).astype(BF)


def norm_back(grad, rows, gain):
    centred = rows - jnp.mean(rows, -1, keepdims=True)
    scale = lax.rsqrt(jnp.mean(centred * centred, -1, keepdims=True) + norm_epsilon)
    hat = centred * scale
    w = grad * gain
    back = scale * (w - jnp.mean(w, -1, keepdims=True) - hat * jnp.mean(w * hat, -1, keepdims=True))
    return back, col_sum(grad * hat), col_sum(grad)


def col_sum(a):
    return jnp.sum(a, 0, keepdims=True)


def swap_halves(u):
    lane = lax.broadcasted_iota(jnp.int32, u.shape, 1)
    half = HEAD_DIM // 2
    return jnp.where(lane % HEAD_DIM < half, pltpu.roll(u, PAIR - half, 1), pltpu.roll(u, half, 1))


def turn(u, cosine, sine):
    return u * cosine + swap_halves(u) * sine


def turn_back(u, cosine, sine):
    return u * cosine - swap_halves(u) * sine


def other_half(u):
    return pltpu.roll(u.astype(F32), HEAD_DIM, 1).astype(u.dtype)


def is_low(count):
    return lax.broadcasted_iota(jnp.int32, (count, PAIR), 1) < HEAD_DIM


def matrix(ref, start=0, stop=None):
    stop = ref.shape[4] if stop is None else stop
    return ref[:, 0, 0, :, start:stop].reshape(ref.shape[0] * ref.shape[3], stop - start)


def put_rows(ref, i, value, cols=None):
    blocks, rows = ref.shape[0], ref.shape[3]
    cols = slice(None) if cols is None else cols
    value = value.astype(ref.dtype)
    if blocks == 1:
        ref[0, 0, 0, pl.ds(pl.multiple_of(i * PART, PART), PART), cols] = value
    else:
        k = PART // rows
        ref[pl.ds(i * k, k), 0, 0, :, cols] = value.reshape(k, rows, value.shape[-1])


def store_heads(ref, at, tiles, cosine, sine):
    low = is_low(tiles[0].shape[0])
    scale = HEAD_DIM ** -0.5
    mixed = turn(tiles[1], cosine, sine)
    done = (turn(tiles[0], cosine, sine) * scale, jnp.where(low, mixed * scale, mixed), turn(tiles[2], cosine, sine), tiles[3], tiles[4])
    for i, tile in enumerate(done):
        ref[0, at, i * PAIR : (i + 1) * PAIR] = tile.astype(BF)


def split_tiles(a):
    return [a[:, i * PAIR : (i + 1) * PAIR] for i in range(a.shape[1] // PAIR)]


def norm_kernel(x_ref, gain_ref, shift_ref, n_ref):
    n_ref[...] = normed(x_ref[...].astype(F32), gain_ref[...], shift_ref[...])


def self_in_kernel(n_ref, w_ref, bias_ref, cos_ref, sin_ref, heads_ref):
    w = matrix(w_ref, 0, 5 * PAIR)
    bias = bias_ref[0, :, : 5 * PAIR]

    def one(i, at, c):
        store_heads(heads_ref, at, split_tiles(mm(n_ref[at, :], w) + bias), cos_ref[at, :], sin_ref[at, :])

    each(n_ref.shape[0], TALL, one)


def cross_in_kernel(n_ref, side_ref, w_ref, bias_ref, cos_ref, sin_ref, heads_ref):
    wq = matrix(w_ref, 0, 2 * PAIR)
    wkv = matrix(w_ref, PAIR, 5 * PAIR)
    bias = split_tiles(bias_ref[0, :, : 5 * PAIR])
    low = is_low(TALL)

    def one(i, at, c):
        q0, q2 = split_tiles(mm(n_ref[at, :], wq))
        k2, k0, v0, v2 = split_tiles(mm(side_ref[at, :], wkv))
        tiles = [q0, jnp.where(low, q2, k2), k0, v0, v2]
        store_heads(heads_ref, at, [t + b for t, b in zip(tiles, bias)], cos_ref[at, :], sin_ref[at, :])

    each(n_ref.shape[0], TALL, one)


def spans(rows):
    return ((0, LONGEST), (LONGEST, rows - LONGEST))


def attend_kernel(heads_ref, qf_ref, kf_ref, o_ref, lse_ref, *, tile):
    rows = heads_ref.shape[1]
    for start, size in spans(rows):
        near = pl.ds(start, size)
        low = is_low(size)
        t3, t1, t2, t4 = [heads_ref[0, near, i * PAIR : (i + 1) * PAIR] for i in range(1, 5)]
        kf = kf_ref[near, :]
        one = jnp.ones_like(t2)
        keys = (jnp.where(low, t1, kf), jnp.where(low, kf, t1), jnp.where(low, other_half(t3), kf))
        vals = (jnp.where(low, t2, one), jnp.where(low, one, t2), jnp.where(low, one, other_half(t4)))
        step = min(tile, size)
        low_t = is_low(step)
        for t in range(size // step):
            at = pl.ds(start + t * step, step)
            qf = qf_ref[at, :]
            q0 = heads_ref[0, at, :PAIR]
            queries = (jnp.where(low_t, q0, qf), jnp.where(low_t, qf, q0), jnp.where(low_t, heads_ref[0, at, PAIR : 2 * PAIR], qf))
            outs, lses = [], []
            for h in range(3):
                s = mm_t(queries[h], keys[h])
                top = jnp.max(s, -1, keepdims=True)
                o = mm(jnp.exp(s - top).astype(BF), vals[h])
                total = pltpu.roll(o, HEAD_DIM, 1)
                outs.append(o / total)
                lses.append(top + jnp.log(total))
            o_ref[0, at, :PAIR] = jnp.where(low_t, 0.0, outs[2]).astype(BF)
            o_ref[0, at, PAIR:] = jnp.where(low_t, outs[0], outs[1]).astype(BF)
            lse_ref[0, at, :PAIR] = jnp.where(low_t, 0.0, lses[2])
            lse_ref[0, at, PAIR:] = jnp.where(low_t, lses[0], lses[1])


def three_parts(u):
    a = u.astype(BF).astype(F32)
    b = (u - a).astype(BF).astype(F32)
    return a, b, u - a - b


def attend_back_kernel(heads_ref, o_ref, do_ref, lse_ref, qf_ref, kf_ref, cos_ref, sin_ref, out_ref, dq2_acc, dk_acc, dv_acc, *, tile):
    rows = heads_ref.shape[1]
    scale = HEAD_DIM ** -0.5
    for start, size in spans(rows):
        near = pl.ds(start, size)
        low = is_low(size)
        within = lax.broadcasted_iota(jnp.int32, (size, PAIR), 1) % HEAD_DIM
        t3, t1, t2, t4 = [heads_ref[0, near, i * PAIR : (i + 1) * PAIR] for i in range(1, 5)]
        ones3 = jnp.where(within < 3, 1.0, 0.0).astype(BF)
        kf = kf_ref[near, :] + jnp.where((within >= 3) & (within < 6), 1.0, 0.0).astype(BF)
        k2 = other_half(t3)
        raw_keys = (t1, t1, k2)
        keys = (jnp.where(low, t1, kf), jnp.where(low, kf, t1), jnp.where(low, k2, kf))
        vals = (jnp.where(low, t2, ones3), jnp.where(low, ones3, t2), jnp.where(low, t4, ones3))
        step = min(tile, size)
        low_t = is_low(step)
        high_t = ~low_t
        within_t = lax.broadcasted_iota(jnp.int32, (step, PAIR), 1) % HEAD_DIM
        for t in range(size // step):
            at = pl.ds(start + t * step, step)
            q0, q2 = heads_ref[0, at, :PAIR], heads_ref[0, at, PAIR : 2 * PAIR]
            do2, do0 = do_ref[0, at, :PAIR], do_ref[0, at, PAIR:]
            prod2 = do2.astype(F32) * o_ref[0, at, :PAIR].astype(F32)
            prod0 = do0.astype(F32) * o_ref[0, at, PAIR:].astype(F32)
            lse2, lse0 = lse_ref[0, at, :PAIR], lse_ref[0, at, PAIR:]
            qf = qf_ref[at, :].astype(F32)
            lse_swapped = pltpu.roll(lse0, HEAD_DIM, 1)
            items = ((q0, do0, low_t, low_t, prod0, lse_swapped), (q0, do0, high_t, high_t, prod0, lse_swapped), (q2, other_half(do2), low_t, high_t, prod2, lse2))
            dqs = []
            for h, (q, do, mine, where_o, prod, lse) in enumerate(items):
                a, b, c = three_parts(-jnp.sum(jnp.where(where_o, prod, 0.0), -1, keepdims=True))
                feat = jnp.where(within_t == 0, a, jnp.where(within_t == 1, b, jnp.where(within_t == 2, c, 0.0)))
                doh = jnp.where(mine, do, feat.astype(BF))
                a, b, c = three_parts(-lse)
                feat = jnp.where(within_t == 3, a, jnp.where(within_t == 4, b, jnp.where(within_t == 5, c, qf)))
                qh = jnp.where(mine, q, feat.astype(BF))
                p = jnp.exp(mm_t(keys[h], qh))
                ds = (p * mm_t(vals[h], doh)).astype(BF)
                dv = mm(p.astype(BF), do)
                dk = mm(ds, q)
                dqs.append(t_mm(ds, raw_keys[h]) * scale)
                if t == 0:
                    dv_acc[h, near, :] = dv
                    dk_acc[h, near, :] = dk
                else:
                    dv_acc[h, near, :] += dv
                    dk_acc[h, near, :] += dk
            dq = jnp.where(low_t, dqs[0], dqs[1])
            out_ref[0, at, :PAIR] = turn_back(dq, cos_ref[at, :], sin_ref[at, :]).astype(BF)
            dq2_acc[at, :] = dqs[2]

    def finish(i, at, c):
        low_r = is_low(ROWS)
        cosine, sine = cos_ref[at, :], sin_ref[at, :]
        out_ref[0, at, 2 * PAIR : 3 * PAIR] = turn_back(jnp.where(low_r, dk_acc[0, at, :], dk_acc[1, at, :]), cosine, sine).astype(BF)
        out_ref[0, at, 3 * PAIR : 4 * PAIR] = jnp.where(low_r, dv_acc[0, at, :], dv_acc[1, at, :]).astype(BF)
        last = jnp.where(low_r, dq2_acc[at, :], pltpu.roll(dk_acc[2, at, :], HEAD_DIM, 1))
        out_ref[0, at, PAIR : 2 * PAIR] = turn_back(last, cosine, sine).astype(BF)
        out_ref[0, at, 4 * PAIR :] = jnp.where(low_r, dv_acc[2, at, :], 0.0).astype(BF)

    each(rows, ROWS, finish)


def out_kernel(att_ref, w_ref, res_ref, bias_ref, gain_ref, shift_ref, mid_ref, n_ref):
    blocks, batches, two, deep, cols = w_ref.shape
    total = None
    for b in range(batches):
        for t in range(two):
            part = mm_t(att_ref[2 * b + t], w_ref[:, b, t].reshape(blocks * deep, cols))
            total = part if total is None else total + part
    mid = res_ref[...].astype(F32) + total + bias_ref[...]
    mid_ref[...] = mid
    n_ref[...] = normed(mid, gain_ref[...], shift_ref[...])


def clear(*refs):
    @pl.when(pl.program_id(0) == 0)
    def _():
        def zero(i, at, c):
            for ref in refs:
                ref[at, :] = jnp.zeros((ROWS, ref.shape[1]), F32)

        each(refs[0].shape[0], ROWS, zero)


def ffn_kernel(mid_ref, n_ref, dz_ref, up_ref, down_ref, upb_ref, downb_ref, gain_ref,
               out_ref, dmid_ref, dlow_ref, dw_ref, dupb_ref, dgain_ref, dshift_ref, ddownb_ref, dcob_ref,
               acc_out, acc_dn, hid, dhid):
    j = pl.program_id(0)
    rows = mid_ref.shape[0]
    width = mid_ref.shape[1]
    up = matrix(up_ref)
    down = matrix(down_ref)
    bias = upb_ref[0]
    clear(acc_out, acc_dn)

    def one(i, at, total):
        h = mm(n_ref[at, :], up) + bias
        phi = 0.5 * (1.0 + lax.erf(h * (0.5 ** 0.5)))
        slope = phi + h * jnp.exp(-0.5 * h * h) * (0.5 / math.pi) ** 0.5
        low = (h * phi).astype(BF)
        hid[at, :] = low
        acc_out[at, :] += mm_t(low, down)
        d = (mm(dz_ref[at, :], down) * slope).astype(BF)
        dhid[at, :] = d
        acc_dn[at, :] += mm_t(d, up)
        return total + col_sum(d.astype(F32))

    dupb_ref[0] = each(rows, FFN_ROWS, one, jnp.zeros((1, up.shape[1]), F32))

    def weight(i, at, c):
        put_rows(dw_ref, i, t_mm(n_ref[:, at], dhid[...]), slice(0, dhid.shape[1]))
        put_rows(dw_ref, i, t_mm(dz_ref[:, at], hid[...]), slice(dhid.shape[1], None))

    each(width, PART, weight)

    @pl.when(j == pl.num_programs(0) - 1)
    def _():
        def last(i, at, sums):
            mid = mid_ref[at, :]
            out_ref[at, :] = (mid + acc_out[at, :] + downb_ref[...]).astype(BF)
            back, dg, ds = norm_back(acc_dn[at, :], mid, gain_ref[...])
            dz = dz_ref[at, :].astype(F32)
            total = dz + back
            dmid_ref[at, :] = total
            low = total.astype(BF)
            dlow_ref[at, :] = low
            return tuple(s + a for s, a in zip(sums, (dg, ds, col_sum(dz), col_sum(low.astype(F32)))))

        sums = each(rows, ROWS, last, (jnp.zeros((1, width), F32),) * 4)
        dgain_ref[...], dshift_ref[...], ddownb_ref[...], dcob_ref[...] = sums


def out_back_kernel(d_ref, w_ref, datt_ref):
    datt_ref[0] = mm(d_ref[...], matrix(w_ref)).astype(BF)


def cross_back_kernel(dh_ref, w_ref, n_ref, side_ref, dlow_ref, att_ref, mid_ref, dmid_ref, gain_ref,
                      dw_ref, dbias_ref, dout_ref, dbranch_ref, dg_ref, ds_ref, dob_ref, acc_n):
    j = pl.program_id(0)
    rows, width = mid_ref.shape
    wq = matrix(w_ref, 0, 2 * PAIR)
    low = is_low(TALL)
    nought = jnp.zeros((TALL, PAIR), BF)
    clear(acc_n)

    def one(i, at, total):
        d = dh_ref[0, at, :]
        acc_n[at, :] += mm_t(jnp.concatenate([d[:, :PAIR], jnp.where(low, d[:, PAIR : 2 * PAIR], nought)], 1), wq)
        return total + col_sum(d.astype(F32))

    dbias_ref[0, :, : 5 * PAIR] = each(rows, TALL, one, jnp.zeros((1, 5 * PAIR), F32))
    dbias_ref[0, :, 5 * PAIR :] = jnp.zeros((1, PAIR), F32)
    low_p = is_low(PART)

    def weight(i, at, c):
        dq = t_mm(n_ref[:, at], dh_ref[0, :, : 2 * PAIR])
        dkv = t_mm(side_ref[:, at], dh_ref[0, :, PAIR:])
        do = t_mm(dlow_ref[:, at], att_ref[0])
        put_rows(dw_ref, i, dq[:, :PAIR], slice(0, PAIR))
        put_rows(dw_ref, i, jnp.where(low_p, dq[:, PAIR:], dkv[:, :PAIR]), slice(PAIR, 2 * PAIR))
        put_rows(dw_ref, i, dkv[:, PAIR : 3 * PAIR], slice(2 * PAIR, 4 * PAIR))
        put_rows(dw_ref, i, dkv[:, 3 * PAIR :] + do[:, :PAIR], slice(4 * PAIR, 5 * PAIR))
        put_rows(dw_ref, i, do[:, PAIR:], slice(5 * PAIR, 6 * PAIR))

    each(width, PART, weight)

    @pl.when(j == pl.num_programs(0) - 1)
    def _():
        def last(i, at, sums):
            back, dg, ds = norm_back(acc_n[at, :], mid_ref[at, :], gain_ref[...])
            total = dmid_ref[at, :] + back
            dout_ref[at, :] = total
            branch = total.astype(BF)
            dbranch_ref[at, :] = branch
            return tuple(s + a for s, a in zip(sums, (dg, ds, col_sum(branch.astype(F32)))))

        sums = each(rows, ROWS, last, (jnp.zeros((1, width), F32),) * 3)
        dg_ref[...], ds_ref[...], dob_ref[...] = sums


def side_back_kernel(dh_ref, w_ref, y_ref, gain_ref, other_ref, dg_ref, ds_ref, acc):
    rows, width = y_ref.shape
    w = matrix(w_ref, PAIR, 5 * PAIR)
    low = is_low(TALL)
    nought = jnp.zeros((TALL, PAIR), BF)
    clear(acc)

    def one(i, at, c):
        d = dh_ref[0, at, :]
        acc[at, :] += mm_t(jnp.concatenate([jnp.where(low, nought, d[:, PAIR : 2 * PAIR]), d[:, 2 * PAIR :]], 1), w)

    each(rows, TALL, one)

    @pl.when(pl.program_id(0) == pl.num_programs(0) - 1)
    def _():
        def last(i, at, sums):
            other, dg, ds = norm_back(acc[at, :], y_ref[at, :].astype(F32), gain_ref[...])
            other_ref[at, :] = other.astype(BF)
            return sums[0] + dg, sums[1] + ds

        dg_ref[...], ds_ref[...] = each(rows, ROWS, last, (jnp.zeros((1, width), F32),) * 2)


def self_back_part(dh_ref, w_ref, n_ref, dlow_ref, att_ref, dw_ref, dbias_ref, acc_ref):
    rows, width = n_ref.shape
    w = matrix(w_ref, 0, 5 * PAIR)
    clear(acc_ref)

    def one(i, at, total):
        d = dh_ref[0, at, :]
        acc_ref[at, :] += mm_t(d, w)
        return total + col_sum(d.astype(F32))

    dbias_ref[0, :, : 5 * PAIR] = each(rows, TALL, one, jnp.zeros((1, 5 * PAIR), F32))
    dbias_ref[0, :, 5 * PAIR :] = jnp.zeros((1, PAIR), F32)

    def weight(i, at, c):
        dqkv = t_mm(n_ref[:, at], dh_ref[0])
        do = t_mm(dlow_ref[:, at], att_ref[0])
        put_rows(dw_ref, i, dqkv[:, : 4 * PAIR], slice(0, 4 * PAIR))
        put_rows(dw_ref, i, dqkv[:, 4 * PAIR :] + do[:, :PAIR], slice(4 * PAIR, 5 * PAIR))
        put_rows(dw_ref, i, do[:, PAIR:], slice(5 * PAIR, 6 * PAIR))

    each(width, PART, weight)


def self_back_first_kernel(dh_ref, w_ref, n_ref, dlow_ref, att_ref, dw_ref, dbias_ref, acc_ref):
    self_back_part(dh_ref, w_ref, n_ref, dlow_ref, att_ref, dw_ref, dbias_ref, acc_ref)


def self_back_last_kernel(dh_ref, w_ref, n_ref, dlow_ref, att_ref, x_ref, dmid_ref, before_ref, gain_ref,
                          dw_ref, dbias_ref, own_ref, dg_ref, ds_ref, acc_ref):
    j = pl.program_id(0)
    rows, width = x_ref.shape
    self_back_part(dh_ref, w_ref, n_ref, dlow_ref, att_ref, dw_ref, dbias_ref, acc_ref)

    @pl.when(j == pl.num_programs(0) - 1)
    def _():
        def last(i, at, sums):
            back, dg, ds = norm_back(acc_ref[at, :] + before_ref[at, :], x_ref[at, :].astype(F32), gain_ref[...])
            own_ref[at, :] = (dmid_ref[at, :] + back).astype(BF)
            return sums[0] + dg, sums[1] + ds

        dg_ref[...], ds_ref[...] = each(rows, ROWS, last, (jnp.zeros((1, width), F32),) * 2)


def collect_kernel(*refs):
    *ins, out_ref = refs
    out_ref[...] = jnp.zeros(out_ref.shape, F32)
    at = 0
    for ref in ins:
        for i in range(ref.shape[0]):
            out_ref[at : at + 1, :] = ref[i] if len(ref.shape) == 3 else ref[...]
            at += 1


def tables(image_sizes, count):
    images = image_sizes.shape[0]
    ends = jnp.cumsum(image_sizes)
    first = jnp.sum(jnp.where(image_sizes == LONGEST, ends - image_sizes, 0))
    places = (jnp.arange(count, dtype=jnp.int32) + first) % count
    passed = places[:, None] >= ends[None, :]
    segment = jnp.sum(passed.astype(jnp.int32), -1)
    start = jnp.sum(jnp.where(passed, image_sizes[None, :], 0), -1)
    place = (places - start).astype(F32)
    half = HEAD_DIM // 2
    lane = jnp.arange(PAIR, dtype=jnp.int32)
    freqs = 100.0 ** (-((lane % half).astype(F32) / half))
    angles = place[:, None] * freqs[None, :]
    sign = jnp.where(lane % HEAD_DIM < half, -1.0, 1.0)
    member = (lane % HEAD_DIM)[None, :] == segment[:, None]
    slot = ((lane % HEAD_DIM) < images)[None, :]
    kf = member.astype(BF)
    qf = jnp.where(slot & ~member, -FAR, 0.0).astype(BF)
    return first, qf, kf, jnp.cos(angles), jnp.sin(angles) * sign[None, :]


def whole(a):
    return pl.BlockSpec(a.shape, lambda j: (0,) * a.ndim)


def per_step(a, side=None):
    return pl.BlockSpec((1,) + a.shape[1:], lambda j: (j if side is None else 2 * j + side,) + (0,) * (a.ndim - 1))


def weight_block(g, cols, at, side=None):
    return pl.BlockSpec((g.shape[0], 1, 1, g.shape[3], cols), lambda j: (0, j // 2, j % 2, 0, at) if side is None else (0, j, side, 0, at))


def sds(shape, dtype):
    return jax.ShapeDtypeStruct(shape, dtype)


def call(kernel, name, steps, ins, outs, scratch=(), flops=0, moved=0, exps=0):
    return pl.pallas_call(
        kernel,
        grid=(steps,),
        in_specs=[s for _, s in ins],
        out_specs=[s for _, s in outs],
        out_shape=[o for o, _ in outs],
        scratch_shapes=list(scratch),
        cost_estimate=pl.CostEstimate(flops=int(flops) // CHEAP, bytes_accessed=int(moved) // CHEAP, transcendentals=int(exps) // CHEAP),
        name=name,
    )(*[a for a, _ in ins])


def body(tokens, cotangent, lengths, norm1_gain, norm1_shift, qkv_w, qkv_b, out_w, out_b, norm2_gain, norm2_shift,
         normy_gain, normy_shift, cq_w, cq_b, ckv_w, ckv_b, cout_w, cout_b, norm3_gain, norm3_shift, up_w, up_b, down_w, down_b):
    batches = tokens.shape[0]
    members = lax.axis_size("mp")
    n_dp = lax.axis_size("dp")
    assert members == 2 * batches
    me = lax.axis_index("mp")
    view = me // batches
    batch = me % batches
    local = tokens.shape[2]
    rows = local * members
    width = tokens.shape[3]
    r = qkv_w.shape[1]
    hw = cq_w.shape[2]
    fw = up_w.shape[2]
    partner = [(i, (i + batches) % members) for i in range(members)]
    groups = [[d * members + v * batches + b for d in range(n_dp) for b in range(batches)] for v in range(2)]
    both = ("dp", "mp")
    split = r % 16 == 0
    blocks, deep = (n_dp, r) if split else (1, n_dp * r)

    def of_view(a, which):
        return lax.dynamic_index_in_dim(a, which, 0, keepdims=False)

    def cols(q, k, v, o):
        return jnp.concatenate([q, k[..., PAIR:], k[..., :PAIR], v, o[..., PAIR:], o[..., :PAIR]], -1)

    def uncols(a):
        t = [a[..., i * PAIR : (i + 1) * PAIR] for i in range(a.shape[-1] // PAIR)]
        h = HEAD_DIM
        join = lambda x, y: jnp.concatenate([x, y], -1)
        heads = (join(t[0], t[1][..., :h]), join(t[2], t[1][..., h:]), join(t[3], t[4][..., :h]))
        return heads + ((join(t[5], t[4][..., h:]),) if len(t) > 5 else ())

    def pair_of(pack):
        return jnp.stack([of_view(pack, view), lax.ppermute(of_view(pack, 1 - view), "mp", partner)], 0)

    def gather(pair):
        got = lax.all_gather(pair, both, axis=0, axis_index_groups=groups).reshape(n_dp, batches, 2, r, -1)
        return got if split else got.transpose(1, 2, 0, 3, 4).reshape(1, batches, 2, deep, -1)

    flip = lambda a: a.swapaxes(-1, -2)
    pack_self = cols(qkv_w[:, :, 0], qkv_w[:, :, 1], qkv_w[:, :, 2], flip(out_w))
    pack_cross = cols(cq_w, ckv_w[:, :, 0], ckv_w[:, :, 1], flip(cout_w))
    w_att = gather(pair_of(jnp.concatenate([pack_self, pack_cross], -1)))
    pair_ffn = pair_of(jnp.concatenate([up_w, flip(down_w)], -1))

    none = jnp.zeros_like(cq_b)
    bias_pack = jnp.concatenate([cols(qkv_b[:, 0], qkv_b[:, 1], qkv_b[:, 2], none), cols(cq_b, ckv_b[:, 0], ckv_b[:, 1], none), up_b], -1)
    bias_rows = bias_pack.shape[-1] // width
    bias_pack = jnp.broadcast_to(bias_pack.reshape(2, 1, bias_rows, width), (2, batches, bias_rows, width))
    by_view = tokens.swapaxes(0, 1)
    sent_x = jnp.concatenate([by_view, bias_pack], 2).reshape(members, local + bias_rows, width)
    got_x = lax.all_to_all(sent_x, "mp", 0, 0, tiled=True)
    got_y = lax.all_to_all(by_view[::-1].reshape(members, local, width), "mp", 0, 0, tiled=True)
    got_z = lax.all_to_all(cotangent.swapaxes(0, 1).reshape(members, local, width), "mp", 0, 0, tiled=True)
    first, qf, kf, cosine, sine = tables(of_view(lengths[:, 0], batch), rows)

    def from_row(a, at):
        return lax.dynamic_slice_in_dim(jnp.concatenate([a, a], 0), at, rows, 0)

    x = from_row(got_x[:, :local].reshape(rows, width), first)
    y = from_row(got_y.reshape(rows, width), first)
    dz = from_row(got_z.reshape(rows, width), first)

    def by_step(a):
        a = a.reshape((2, batches) + a.shape[1:])
        return jnp.where(view == 0, a, a[::-1]).swapaxes(0, 1).reshape((members,) + a.shape[2:])

    def by_member(a):
        a = a.reshape((batches, 2) + a.shape[1:]).swapaxes(0, 1)
        return jnp.where(view == 0, a, a[::-1]).reshape((members,) + a.shape[2:])

    biases = by_step(got_x[:, local:]).astype(F32)
    self_bias, cross_bias, up_bias = biases[:, 0:1], biases[:, 1:2], biases[:, 2:]
    up_bias = up_bias.reshape(members, 1, fw)

    def mine(a):
        return of_view(a, view).astype(F32)[None]

    g1, s1, ob, g2, s2, gy, sy, cob, g3, s3, db = [
        mine(a) for a in (norm1_gain, norm1_shift, out_b, norm2_gain, norm2_shift, normy_gain, normy_shift, cout_b, norm3_gain, norm3_shift, down_b)]
    def given(*arrays):
        return [(a, whole(a)) for a in arrays]

    def steps(*arrays):
        return [(a, per_step(a)) for a in arrays]

    def full(*shape_types):
        return [(s, whole(s)) for s in shape_types]

    low = sds((rows, width), BF)
    high = sds((rows, width), F32)
    line = sds((1, width), F32)
    heads = sds((members, rows, 5 * PAIR), BF)
    att_low = sds((members, rows, 2 * PAIR), BF)
    att_high = sds((members, rows, 2 * PAIR), F32)
    bias_out = sds((members, 1, 6 * PAIR), F32)
    gemm = 2 * rows * width * width * members

    def attend(h):
        return call(functools.partial(attend_kernel, tile=384), "attend", members, steps(h) + given(qf, kf), [(s, per_step(s)) for s in (att_low, att_high)],
                    flops=12 * members * rows * rows * PAIR, moved=members * rows * PAIR * 22, exps=3 * members * rows * rows)

    def attend_back(h, o, do, lse, side=None):
        count = members if side is None else batches
        out = sds((count, rows, 5 * PAIR), BF)
        acc = pltpu.VMEM((3, rows, PAIR), F32)
        ins = [(a, per_step(a, side)) for a in (h, o, do, lse)]
        return call(functools.partial(attend_back_kernel, tile=256), "attend_back", count, ins + given(qf, kf, cosine, sine), [(out, per_step(out))],
                    [pltpu.VMEM((rows, PAIR), F32), acc, acc], flops=30 * count * rows * rows * PAIR, moved=count * rows * PAIR * 40,
                    exps=3 * count * rows * rows)[0]

    def project(att, at, res, bias, gain, shift):
        tall = 512
        part = lambda cols: pl.BlockSpec((tall, cols), lambda i: (i, 0))
        att_spec = pl.BlockSpec((members, tall, 2 * PAIR), lambda i: (0, i, 0))
        w_spec = pl.BlockSpec((blocks, batches, 2, deep, 2 * PAIR), lambda i: (0, 0, 0, 0, at))
        return call(out_kernel, "project", rows // tall, [(att, att_spec), (w_att, w_spec), (res, part(width))] + given(bias, gain, shift),
                    [(high, part(width)), (low, part(width))], flops=gemm / 3, moved=rows * width * 14)

    def project_back(d, at):
        return call(out_back_kernel, "project_back", members, given(d) + [(w_att, weight_block(w_att, 2 * PAIR, at))], [(att_low, per_step(att_low))],
                    flops=gemm / 3, moved=rows * width * 8)[0]

    def norm(a, gain, shift):
        spec = pl.BlockSpec((ROWS, width), lambda i: (i, 0))
        return call(norm_kernel, "norm", rows // ROWS, [(a, spec)] + given(gain, shift), [(low, spec)], moved=rows * width * 4)[0]

    def by_owner(piece):
        if not split:
            piece = piece.reshape(batches, piece.shape[2], n_dp, r, -1).transpose(2, 0, 1, 3, 4)
        return piece

    def scatter(piece):
        whole_piece = by_owner(piece).reshape(n_dp * batches, 2, r, -1)
        total = lax.psum_scatter(whole_piece, both, scatter_dimension=0, axis_index_groups=groups)
        return with_layout_constraint(total, Layout(major_to_minor=(0, 1, 2)))

    core_pairs = [(i, i ^ 1) for i in range(members)]
    x_pairs = [(i, i ^ 1) for i in range(n_dp)]
    place = lax.axis_index("dp")
    lines = n_dp // 2

    def pick(a, i, axis):
        return lax.dynamic_index_in_dim(a, i, axis, keepdims=False)

    by_hand = batches == 2 and n_dp <= 8
    x_place, z_place = place % 2, place // 2

    def added(terms):
        total = terms[0].astype(F32)
        for term in terms[1:]:
            total = total + term.astype(F32)
        return total

    def hop(terms, axis, other, mine, name, perm):
        got = lax.ppermute(added([pick(t, other, axis) for t in terms]).astype(BF), name, perm)
        return [pick(t, mine, axis) for t in terms] + [got]

    def over_cores(piece):
        return hop([piece], 1, 1 - batch, batch, "mp", core_pairs)

    def over_x(terms):
        terms = [t.reshape((t.shape[0] // 2, 2) + t.shape[1:]) for t in terms]
        return hop(terms, 1, 1 - x_place, x_place, "dp", x_pairs)

    def over_z(terms):
        total = added([pick(t, z_place, 0) for t in terms])
        for s in range(1, lines):
            perm = [(i, (i + 2 * s) % n_dp) for i in range(n_dp)]
            total = total + lax.ppermute(added([pick(t, (z_place + s) % lines, 0) for t in terms]).astype(BF), "dp", perm).astype(F32)
        return total.astype(BF)

    def to_partner(a):
        return lax.ppermute(a, "mp", partner)

    def both_views(keep, theirs):
        keep, theirs = keep.astype(F32), theirs.astype(F32)
        return jnp.stack([jnp.where(view == 0, keep, theirs), jnp.where(view == 0, theirs, keep)], 0)

    n1 = norm(x, g1, s1)
    side = norm(y, gy, sy)
    pair_ffn, n1, side, qf, kf, cosine, sine = lax.optimization_barrier((pair_ffn, n1, side, qf, kf, cosine, sine))
    w_ffn = gather(pair_ffn)
    hs = call(self_in_kernel, "self_in", members, given(n1) + [(w_att, weight_block(w_att, 6 * PAIR, 0))] + steps(self_bias) + given(cosine, sine),
              [(heads, per_step(heads))], flops=gemm, moved=rows * width * 16)[0]
    att, lse = attend(hs)
    middle, n2 = project(att, 2, x, ob, g2, s2)
    hc = call(cross_in_kernel, "cross_in", members, given(n2, side) + [(w_att, weight_block(w_att, 6 * PAIR, 1))] + steps(cross_bias) + given(cosine, sine),
              [(heads, per_step(heads))], flops=gemm, moved=rows * width * 16)[0]
    catt, clse = attend(hc)
    middle2, n3 = project(catt, 5, middle, cob, g3, s3)

    dw_ffn = sds((blocks, batches, 2, deep, 2 * fw), BF)
    dw_ffn_spec = pl.BlockSpec((blocks, 1, 1, deep, 2 * fw), lambda j: (0, j // 2, j % 2, 0, 0))
    up_line = sds((members, 1, fw), F32)
    output, d_mid2, d_cross, dw_f, d_upb, gg3, gs3, d_db, d_cob = call(
        ffn_kernel, "ffn", members,
        given(middle2, n3, dz) + [(w_ffn, weight_block(w_ffn, fw, 0)), (w_ffn, weight_block(w_ffn, fw, 1))] + steps(up_bias) + given(db, g3),
        full(low, high, low) + [(dw_ffn, dw_ffn_spec), (up_line, per_step(up_line))] + full(line, line, line, line),
        [pltpu.VMEM((rows, width), F32)] * 2 + [pltpu.VMEM((rows, fw), BF)] * 2,
        flops=6 * gemm, moved=rows * width * 60, exps=rows * fw * members * 2)

    total_ffn = scatter(dw_f)
    d_catt = project_back(d_cross, 5)
    d_hc = attend_back(hc, catt, d_catt, clse)
    dw_att = sds((blocks, batches, 2, deep, 6 * PAIR), BF)
    dw_spec = pl.BlockSpec((blocks, 1, 1, deep, 6 * PAIR), lambda j: (0, j // 2, j % 2, 0, 0))
    dw_cross, d_crossb, d_mid, d_branch, gg2, gs2, d_ob = call(
        cross_back_kernel, "cross_back", members,
        steps(d_hc) + [(w_att, weight_block(w_att, 6 * PAIR, 1))] + given(n2, side, d_cross) + steps(catt) + given(middle, d_mid2, g2),
        [(dw_att, dw_spec), (bias_out, per_step(bias_out))] + full(high, low, line, line, line),
        [pltpu.VMEM((rows, width), F32)], flops=2 * gemm, moved=rows * width * 30)

    def side_back(dh):
        return call(side_back_kernel, "side_back", members, steps(dh) + [(w_att, weight_block(w_att, 6 * PAIR, 1))] + given(y, gy),
                    full(low, line, line), [pltpu.VMEM((rows, width), F32)], flops=gemm, moved=rows * width * 16)

    d_att = project_back(d_branch, 2)
    total_cross = scatter(dw_cross)

    dw_part = sds((blocks, batches, 1, deep, 6 * PAIR), BF)
    dw_part_spec = pl.BlockSpec((blocks, 1, 1, deep, 6 * PAIR), lambda j: (0, j, 0, 0, 0))
    bias_part = sds((batches, 1, 6 * PAIR), F32)

    def self_back(t, dh, *more):
        ins = steps(dh) + [(w_att, weight_block(w_att, 6 * PAIR, 0, t))] + given(n1, d_branch) + [(att, per_step(att, t))]
        outs = [(dw_part, dw_part_spec), (bias_part, per_step(bias_part))]
        if more:
            return call(self_back_last_kernel, "self_back_last", batches, ins + given(*more), outs + full(low, line, line),
                        [pltpu.VMEM((rows, width), F32)], flops=1.5 * gemm, moved=rows * width * 30)
        return call(self_back_first_kernel, "self_back_first", batches, ins, outs + full(high), flops=1.5 * gemm, moved=rows * width * 24)

    def home(a):
        return lax.all_to_all(a.reshape(members, local, width), "mp", 0, 0, tiled=True).reshape(2, batches, local, width)

    d_h1 = attend_back(hs, att, d_att, lse, 1)
    dw_self1, d_selfb1, acc = self_back(1, d_h1)
    d_att, acc, dw_self1 = lax.optimization_barrier((d_att, acc, dw_self1))
    output = from_row(output, rows - first)
    if by_hand:
        self1 = over_cores(by_owner(dw_self1))
        d_att, output, got = lax.optimization_barrier((d_att, output, self1[1]))
        self1 = over_x([self1[0], got])
    got_output = home(output)
    d_h0 = attend_back(hs, att, d_att, lse, 0)
    d_h0, total_ffn, got_output = lax.optimization_barrier((d_h0, total_ffn, got_output))
    their_ffn = to_partner(total_ffn[1])
    if by_hand:
        d_h0, got = lax.optimization_barrier((d_h0, self1[2]))
        total1 = over_z(self1[:2] + [got])
    dw_self0, d_selfb0, own, gg1, gs1 = self_back(0, d_h0, x, d_mid, acc, g1)
    if by_hand:
        own, dw_self0, gg1, their_ffn, total1 = lax.optimization_barrier((own, dw_self0, gg1, their_ffn, total1))
        self0 = over_cores(by_owner(dw_self0))
        own = from_row(own, rows - first)
        own, got, gg1 = lax.optimization_barrier((own, self0[1], gg1))
        self0 = [t.reshape((lines, 2) + t.shape[1:]) for t in (self0[0], got)]
        send = added([pick(t, 1 - x_place, 1) for t in self0]).astype(BF)
        own, send, d_hc = lax.optimization_barrier((own, send, d_hc))
        self0 = [pick(t, x_place, 1) for t in self0] + [lax.ppermute(send, "dp", x_pairs)]
    else:
        own = from_row(own, rows - first)
    got_own = home(own)
    other, ggy, gsy = side_back(d_hc)
    if by_hand:
        other, x_sum = lax.optimization_barrier((other, self0[2]))
        self0 = self0[:2] + [x_sum]
    lines_out = [gg1, gs1, d_ob, gg2, gs2, ggy, gsy, d_cob, gg3, gs3, d_db, d_selfb0, d_selfb1, d_crossb, d_upb]
    count = 11 + 3 * members
    collected = sds((-(-count // 8) * 8, width), F32)
    small = call(collect_kernel, "collect", 1, given(*lines_out), full(collected))[0]
    if by_hand:
        small = small + lax.ppermute(small, "mp", core_pairs)
        sum_ffn = both_views(total_ffn[0], their_ffn)
        up_wg, down_wg = sum_ffn[..., :fw], flip(sum_ffn[..., fw:])
        their1 = to_partner(total1)
        flat = small + lax.ppermute(small, "dp", x_pairs)
        flat, got, their1, got_own, other, up_wg, down_wg, total_cross = lax.optimization_barrier((flat, self0[2], their1, got_own, other, up_wg, down_wg, total_cross))
        other = from_row(other, rows - first)
        got_other = home(other)
        their_cross = to_partner(total_cross[1])
        flat = lax.reduce_precision(flat, 8, 7)
        self0 = self0[:2] + [got]
        total0 = added([pick(t, z_place, 0) for t in self0])
        on_line = [flat]
        for s in range(1, lines):
            send = added([pick(t, (z_place + s) % lines, 0) for t in self0]).astype(BF)
            got = lax.ppermute(jnp.concatenate([send.reshape(-1, width), flat.astype(BF)], 0), "dp", [(i, (i + 2 * s) % n_dp) for i in range(n_dp)])
            total0 = total0 + got[: send.size // width].reshape(total0.shape).astype(F32)
            on_line.append(got[send.size // width :].astype(F32))
        on_line = jnp.stack(on_line, 0)
        flat = sum(pick(on_line, (z_place - p) % lines, 0) for p in range(lines))
        flat_in = to_partner(flat)
        sum_self = both_views(total0[0], their1[0])
    else:
        got_other = home(from_row(other, rows - first))
        total_self = scatter(jnp.concatenate([dw_self0, dw_self1], 2))
        their_cross = to_partner(total_cross[1])
        sum_self = both_views(total_self[0], to_partner(total_self[1]))
        sums = lax.psum(jnp.stack([jnp.where(view == 0, small, 0.0), jnp.where(view == 1, small, 0.0)], 0), both)
        flat, flat_in = pick(sums, view, 0), pick(sums, 1 - view, 0)
        sum_ffn = both_views(total_ffn[0], their_ffn)
        up_wg, down_wg = sum_ffn[..., :fw], flip(sum_ffn[..., fw:])
    sum_cross = both_views(total_cross[0], their_cross)

    sums = both_views(flat[:11].reshape(-1), flat_in[:11].reshape(-1))
    g1g, s1g, obg, g2g, s2g, gyg, syg, cobg, g3g, s3g, dbg = [sums[:, i * width : (i + 1) * width] for i in range(11)]

    def member_row(own_row, other_row):
        return both_views(pick(flat, own_row, 0), pick(flat_in, other_row, 0))

    self_part = uncols(member_row(11 + batch, 11 + batches + batch)[:, : 5 * PAIR])
    start = 11 + members + 2 * batch
    cross_part = uncols(member_row(start, start + 1)[:, : 5 * PAIR])
    upb_grad = member_row(start + members, start + members + 1)

    block_output = got_output.swapaxes(0, 1)
    input_grad = (got_own.astype(F32) + got_other[::-1].astype(F32)).swapaxes(0, 1)

    q, k, v, o = uncols(sum_self)
    cq, ck, cv, co = uncols(sum_cross)
    return (block_output, input_grad, g1g, s1g, jnp.stack([q, k, v], 2), jnp.stack(self_part, 1), flip(o), obg, g2g, s2g, gyg, syg,
            cq, cross_part[0], jnp.stack([ck, cv], 2), jnp.stack(cross_part[1:], 1), flip(co), cobg, g3g, s3g,
            up_wg, upb_grad, down_wg, dbg)


def solution(mesh):
    rows = P(None, None, ("dp", "mp"), None)
    wide = P(None, "dp", None, "mp")
    by_rows = P(None, "dp", "mp")
    by_cols = P(None, "mp", "dp")
    parts = P(None, None, "mp")
    flat = P(None, "mp")
    same = P()
    in_specs = (rows, rows, P(None, "dp", None), same, same, wide, parts, by_cols, same, same, same, same, same, by_rows, flat, wide, parts,
                by_cols, same, same, same, by_rows, flat, by_cols, same)
    out_specs = (rows, rows, same, same, wide, parts, by_cols, same, same, same, same, same, by_rows, flat, wide, parts, by_cols, same,
                 same, same, by_rows, flat, by_cols, same)
    return jax.shard_map(body, mesh=mesh, in_specs=in_specs, out_specs=out_specs, check_vma=False)
```

```python
import functools
import math

import jax
import jax.numpy as jnp
from jax import lax
from jax.experimental import pallas as pl
from jax.experimental.layout import Layout, with_layout_constraint
from jax.experimental.pallas import tpu as pltpu
from jax.sharding import PartitionSpec as P

HEAD_DIM = 64
PAIR = 2 * HEAD_DIM
FAR = 1e30
BF = jnp.bfloat16
F32 = jnp.float32
LONGEST = 768
ROWS = 256
TALL = 1024
CHEAP = 16
FFN_ROWS = 1024
PART = 768
norm_epsilon = 1e-06


def mm(a, b):
    return jnp.dot(a, b, preferred_element_type=F32)


def mm_t(a, b):
    return lax.dot_general(a, b, (((1,), (1,)), ((), ())), preferred_element_type=F32)


def t_mm(a, b):
    return lax.dot_general(a, b, (((0,), (0,)), ((), ())), preferred_element_type=F32)


def each(count, size, step, carry=None):
    def go(i, c):
        return step(i, pl.ds(pl.multiple_of(i * size, size), size), c)

    return lax.fori_loop(0, count // size, go, carry)


def normed(rows, gain, shift):
    centred = rows - jnp.mean(rows, -1, keepdims=True)
    spread = jnp.mean(centred * centred, -1, keepdims=True)
    return (centred * lax.rsqrt(spread + norm_epsilon) * gain + shift).astype(BF)


def norm_back(grad, rows, gain):
    centred = rows - jnp.mean(rows, -1, keepdims=True)
    scale = lax.rsqrt(jnp.mean(centred * centred, -1, keepdims=True) + norm_epsilon)
    hat = centred * scale
    w = grad * gain
    back = scale * (w - jnp.mean(w, -1, keepdims=True) - hat * jnp.mean(w * hat, -1, keepdims=True))
    return back, col_sum(grad * hat), col_sum(grad)


def col_sum(a):
    return jnp.sum(a, 0, keepdims=True)


def swap_halves(u):
    lane = lax.broadcasted_iota(jnp.int32, u.shape, 1)
    half = HEAD_DIM // 2
    return jnp.where(lane % HEAD_DIM < half, pltpu.roll(u, PAIR - half, 1), pltpu.roll(u, half, 1))


def turn(u, cosine, sine):
    return u * cosine + swap_halves(u) * sine


def turn_back(u, cosine, sine):
    return u * cosine - swap_halves(u) * sine


def other_half(u):
    return pltpu.roll(u.astype(F32), HEAD_DIM, 1).astype(u.dtype)


def is_low(count):
    return lax.broadcasted_iota(jnp.int32, (count, PAIR), 1) < HEAD_DIM


def matrix(ref, start=0, stop=None):
    stop = ref.shape[4] if stop is None else stop
    return ref[:, 0, 0, :, start:stop].reshape(ref.shape[0] * ref.shape[3], stop - start)


def put_rows(ref, i, value, cols=None):
    blocks, rows = ref.shape[0], ref.shape[3]
    cols = slice(None) if cols is None else cols
    value = value.astype(ref.dtype)
    if blocks == 1:
        ref[0, 0, 0, pl.ds(pl.multiple_of(i * PART, PART), PART), cols] = value
    else:
        k = PART // rows
        ref[pl.ds(i * k, k), 0, 0, :, cols] = value.reshape(k, rows, value.shape[-1])


def store_heads(ref, at, tiles, cosine, sine):
    low = is_low(tiles[0].shape[0])
    scale = HEAD_DIM ** -0.5
    mixed = turn(tiles[1], cosine, sine)
    done = (turn(tiles[0], cosine, sine) * scale, jnp.where(low, mixed * scale, mixed), turn(tiles[2], cosine, sine), tiles[3], tiles[4])
    for i, tile in enumerate(done):
        ref[0, at, i * PAIR : (i + 1) * PAIR] = tile.astype(BF)


def split_tiles(a):
    return [a[:, i * PAIR : (i + 1) * PAIR] for i in range(a.shape[1] // PAIR)]


def norm_kernel(x_ref, gain_ref, shift_ref, n_ref):
    n_ref[...] = normed(x_ref[...].astype(F32), gain_ref[...], shift_ref[...])


def self_in_kernel(n_ref, w_ref, bias_ref, cos_ref, sin_ref, heads_ref):
    w = matrix(w_ref, 0, 5 * PAIR)
    bias = bias_ref[0, :, : 5 * PAIR]

    def one(i, at, c):
        store_heads(heads_ref, at, split_tiles(mm(n_ref[at, :], w) + bias), cos_ref[at, :], sin_ref[at, :])

    each(n_ref.shape[0], TALL, one)


def cross_in_kernel(n_ref, side_ref, w_ref, bias_ref, cos_ref, sin_ref, heads_ref):
    wq = matrix(w_ref, 0, 2 * PAIR)
    wkv = matrix(w_ref, PAIR, 5 * PAIR)
    bias = split_tiles(bias_ref[0, :, : 5 * PAIR])
    low = is_low(TALL)

    def one(i, at, c):
        q0, q2 = split_tiles(mm(n_ref[at, :], wq))
        k2, k0, v0, v2 = split_tiles(mm(side_ref[at, :], wkv))
        tiles = [q0, jnp.where(low, q2, k2), k0, v0, v2]
        store_heads(heads_ref, at, [t + b for t, b in zip(tiles, bias)], cos_ref[at, :], sin_ref[at, :])

    each(n_ref.shape[0], TALL, one)


def spans(rows):
    return ((0, LONGEST), (LONGEST, rows - LONGEST))


def attend_kernel(heads_ref, qf_ref, kf_ref, o_ref, lse_ref, *, tile):
    rows = heads_ref.shape[1]
    for start, size in spans(rows):
        near = pl.ds(start, size)
        low = is_low(size)
        t3, t1, t2, t4 = [heads_ref[0, near, i * PAIR : (i + 1) * PAIR] for i in range(1, 5)]
        kf = kf_ref[near, :]
        one = jnp.ones_like(t2)
        keys = (jnp.where(low, t1, kf), jnp.where(low, kf, t1), jnp.where(low, other_half(t3), kf))
        vals = (jnp.where(low, t2, one), jnp.where(low, one, t2), jnp.where(low, one, other_half(t4)))
        step = min(tile, size)
        low_t = is_low(step)
        for t in range(size // step):
            at = pl.ds(start + t * step, step)
            qf = qf_ref[at, :]
            q0 = heads_ref[0, at, :PAIR]
            queries = (jnp.where(low_t, q0, qf), jnp.where(low_t, qf, q0), jnp.where(low_t, heads_ref[0, at, PAIR : 2 * PAIR], qf))
            outs, lses = [], []
            for h in range(3):
                s = mm_t(queries[h], keys[h])
                top = jnp.max(s, -1, keepdims=True)
                o = mm(jnp.exp(s - top).astype(BF), vals[h])
                total = pltpu.roll(o, HEAD_DIM, 1)
                outs.append(o / total)
                lses.append(top + jnp.log(total))
            o_ref[0, at, :PAIR] = jnp.where(low_t, 0.0, outs[2]).astype(BF)
            o_ref[0, at, PAIR:] = jnp.where(low_t, outs[0], outs[1]).astype(BF)
            lse_ref[0, at, :PAIR] = jnp.where(low_t, 0.0, lses[2])
            lse_ref[0, at, PAIR:] = jnp.where(low_t, lses[0], lses[1])


def three_parts(u):
    a = u.astype(BF).astype(F32)
    b = (u - a).astype(BF).astype(F32)
    return a, b, u - a - b


def attend_back_kernel(heads_ref, o_ref, do_ref, lse_ref, qf_ref, kf_ref, cos_ref, sin_ref, out_ref, dq2_acc, dk_acc, dv_acc, *, tile):
    rows = heads_ref.shape[1]
    scale = HEAD_DIM ** -0.5
    for start, size in spans(rows):
        near = pl.ds(start, size)
        low = is_low(size)
        within = lax.broadcasted_iota(jnp.int32, (size, PAIR), 1) % HEAD_DIM
        t3, t1, t2, t4 = [heads_ref[0, near, i * PAIR : (i + 1) * PAIR] for i in range(1, 5)]
        ones3 = jnp.where(within < 3, 1.0, 0.0).astype(BF)
        kf = kf_ref[near, :] + jnp.where((within >= 3) & (within < 6), 1.0, 0.0).astype(BF)
        k2 = other_half(t3)
        raw_keys = (t1, t1, k2)
        keys = (jnp.where(low, t1, kf), jnp.where(low, kf, t1), jnp.where(low, k2, kf))
        vals = (jnp.where(low, t2, ones3), jnp.where(low, ones3, t2), jnp.where(low, t4, ones3))
        step = min(tile, size)
        low_t = is_low(step)
        high_t = ~low_t
        within_t = lax.broadcasted_iota(jnp.int32, (step, PAIR), 1) % HEAD_DIM
        for t in range(size // step):
            at = pl.ds(start + t * step, step)
            q0, q2 = heads_ref[0, at, :PAIR], heads_ref[0, at, PAIR : 2 * PAIR]
            do2, do0 = do_ref[0, at, :PAIR], do_ref[0, at, PAIR:]
            prod2 = do2.astype(F32) * o_ref[0, at, :PAIR].astype(F32)
            prod0 = do0.astype(F32) * o_ref[0, at, PAIR:].astype(F32)
            lse2, lse0 = lse_ref[0, at, :PAIR], lse_ref[0, at, PAIR:]
            qf = qf_ref[at, :].astype(F32)
            lse_swapped = pltpu.roll(lse0, HEAD_DIM, 1)
            items = ((q0, do0, low_t, low_t, prod0, lse_swapped), (q0, do0, high_t, high_t, prod0, lse_swapped), (q2, other_half(do2), low_t, high_t, prod2, lse2))
            dqs = []
            for h, (q, do, mine, where_o, prod, lse) in enumerate(items):
                a, b, c = three_parts(-jnp.sum(jnp.where(where_o, prod, 0.0), -1, keepdims=True))
                feat = jnp.where(within_t == 0, a, jnp.where(within_t == 1, b, jnp.where(within_t == 2, c, 0.0)))
                doh = jnp.where(mine, do, feat.astype(BF))
                a, b, c = three_parts(-lse)
                feat = jnp.where(within_t == 3, a, jnp.where(within_t == 4, b, jnp.where(within_t == 5, c, qf)))
                qh = jnp.where(mine, q, feat.astype(BF))
                p = jnp.exp(mm_t(keys[h], qh))
                ds = (p * mm_t(vals[h], doh)).astype(BF)
                dv = mm(p.astype(BF), do)
                dk = mm(ds, q)
                dqs.append(t_mm(ds, raw_keys[h]) * scale)
                if t == 0:
                    dv_acc[h, near, :] = dv
                    dk_acc[h, near, :] = dk
                else:
                    dv_acc[h, near, :] += dv
                    dk_acc[h, near, :] += dk
            dq = jnp.where(low_t, dqs[0], dqs[1])
            out_ref[0, at, :PAIR] = turn_back(dq, cos_ref[at, :], sin_ref[at, :]).astype(BF)
            dq2_acc[at, :] = dqs[2]

    def finish(i, at, c):
        low_r = is_low(ROWS)
        cosine, sine = cos_ref[at, :], sin_ref[at, :]
        out_ref[0, at, 2 * PAIR : 3 * PAIR] = turn_back(jnp.where(low_r, dk_acc[0, at, :], dk_acc[1, at, :]), cosine, sine).astype(BF)
        out_ref[0, at, 3 * PAIR : 4 * PAIR] = jnp.where(low_r, dv_acc[0, at, :], dv_acc[1, at, :]).astype(BF)
        last = jnp.where(low_r, dq2_acc[at, :], pltpu.roll(dk_acc[2, at, :], HEAD_DIM, 1))
        out_ref[0, at, PAIR : 2 * PAIR] = turn_back(last, cosine, sine).astype(BF)
        out_ref[0, at, 4 * PAIR :] = jnp.where(low_r, dv_acc[2, at, :], 0.0).astype(BF)

    each(rows, ROWS, finish)


def out_kernel(att_ref, w_ref, res_ref, bias_ref, gain_ref, shift_ref, mid_ref, n_ref):
    blocks, batches, two, deep, cols = w_ref.shape
    total = None
    for b in range(batches):
        for t in range(two):
            part = mm_t(att_ref[2 * b + t], w_ref[:, b, t].reshape(blocks * deep, cols))
            total = part if total is None else total + part
    mid = res_ref[...].astype(F32) + total + bias_ref[...]
    mid_ref[...] = mid
    n_ref[...] = normed(mid, gain_ref[...], shift_ref[...])


def clear(*refs):
    @pl.when(pl.program_id(0) == 0)
    def _():
        def zero(i, at, c):
            for ref in refs:
                ref[at, :] = jnp.zeros((ROWS, ref.shape[1]), F32)

        each(refs[0].shape[0], ROWS, zero)


def ffn_kernel(mid_ref, n_ref, dz_ref, up_ref, down_ref, upb_ref, downb_ref, gain_ref,
               out_ref, dmid_ref, dlow_ref, dw_ref, dupb_ref, dgain_ref, dshift_ref, ddownb_ref, dcob_ref,
               acc_out, acc_dn, hid, dhid):
    j = pl.program_id(0)
    rows = mid_ref.shape[0]
    width = mid_ref.shape[1]
    up = matrix(up_ref)
    down = matrix(down_ref)
    bias = upb_ref[0]
    clear(acc_out, acc_dn)

    def one(i, at, total):
        h = mm(n_ref[at, :], up) + bias
        phi = 0.5 * (1.0 + lax.erf(h * (0.5 ** 0.5)))
        slope = phi + h * jnp.exp(-0.5 * h * h) * (0.5 / math.pi) ** 0.5
        low = (h * phi).astype(BF)
        hid[at, :] = low
        acc_out[at, :] += mm_t(low, down)
        d = (mm(dz_ref[at, :], down) * slope).astype(BF)
        dhid[at, :] = d
        acc_dn[at, :] += mm_t(d, up)
        return total + col_sum(d.astype(F32))

    dupb_ref[0] = each(rows, FFN_ROWS, one, jnp.zeros((1, up.shape[1]), F32))

    def weight(i, at, c):
        put_rows(dw_ref, i, t_mm(n_ref[:, at], dhid[...]), slice(0, dhid.shape[1]))
        put_rows(dw_ref, i, t_mm(dz_ref[:, at], hid[...]), slice(dhid.shape[1], None))

    each(width, PART, weight)

    @pl.when(j == pl.num_programs(0) - 1)
    def _():
        def last(i, at, sums):
            mid = mid_ref[at, :]
            out_ref[at, :] = (mid + acc_out[at, :] + downb_ref[...]).astype(BF)
            back, dg, ds = norm_back(acc_dn[at, :], mid, gain_ref[...])
            dz = dz_ref[at, :].astype(F32)
            total = dz + back
            dmid_ref[at, :] = total
            low = total.astype(BF)
            dlow_ref[at, :] = low
            return tuple(s + a for s, a in zip(sums, (dg, ds, col_sum(dz), col_sum(low.astype(F32)))))

        sums = each(rows, ROWS, last, (jnp.zeros((1, width), F32),) * 4)
        dgain_ref[...], dshift_ref[...], ddownb_ref[...], dcob_ref[...] = sums


def out_back_kernel(d_ref, w_ref, datt_ref):
    datt_ref[0] = mm(d_ref[...], matrix(w_ref)).astype(BF)


def cross_back_kernel(dh_ref, w_ref, n_ref, side_ref, dlow_ref, att_ref, mid_ref, dmid_ref, gain_ref,
                      dw_ref, dbias_ref, dout_ref, dbranch_ref, dg_ref, ds_ref, dob_ref, acc_n):
    j = pl.program_id(0)
    rows, width = mid_ref.shape
    wq = matrix(w_ref, 0, 2 * PAIR)
    low = is_low(TALL)
    nought = jnp.zeros((TALL, PAIR), BF)
    clear(acc_n)

    def one(i, at, total):
        d = dh_ref[0, at, :]
        acc_n[at, :] += mm_t(jnp.concatenate([d[:, :PAIR], jnp.where(low, d[:, PAIR : 2 * PAIR], nought)], 1), wq)
        return total + col_sum(d.astype(F32))

    dbias_ref[0, :, : 5 * PAIR] = each(rows, TALL, one, jnp.zeros((1, 5 * PAIR), F32))
    dbias_ref[0, :, 5 * PAIR :] = jnp.zeros((1, PAIR), F32)
    low_p = is_low(PART)

    def weight(i, at, c):
        dq = t_mm(n_ref[:, at], dh_ref[0, :, : 2 * PAIR])
        dkv = t_mm(side_ref[:, at], dh_ref[0, :, PAIR:])
        do = t_mm(dlow_ref[:, at], att_ref[0])
        put_rows(dw_ref, i, dq[:, :PAIR], slice(0, PAIR))
        put_rows(dw_ref, i, jnp.where(low_p, dq[:, PAIR:], dkv[:, :PAIR]), slice(PAIR, 2 * PAIR))
        put_rows(dw_ref, i, dkv[:, PAIR : 3 * PAIR], slice(2 * PAIR, 4 * PAIR))
        put_rows(dw_ref, i, dkv[:, 3 * PAIR :] + do[:, :PAIR], slice(4 * PAIR, 5 * PAIR))
        put_rows(dw_ref, i, do[:, PAIR:], slice(5 * PAIR, 6 * PAIR))

    each(width, PART, weight)

    @pl.when(j == pl.num_programs(0) - 1)
    def _():
        def last(i, at, sums):
            back, dg, ds = norm_back(acc_n[at, :], mid_ref[at, :], gain_ref[...])
            total = dmid_ref[at, :] + back
            dout_ref[at, :] = total
            branch = total.astype(BF)
            dbranch_ref[at, :] = branch
            return tuple(s + a for s, a in zip(sums, (dg, ds, col_sum(branch.astype(F32)))))

        sums = each(rows, ROWS, last, (jnp.zeros((1, width), F32),) * 3)
        dg_ref[...], ds_ref[...], dob_ref[...] = sums


def side_back_kernel(dh_ref, w_ref, y_ref, gain_ref, other_ref, dg_ref, ds_ref, acc):
    rows, width = y_ref.shape
    w = matrix(w_ref, PAIR, 5 * PAIR)
    low = is_low(TALL)
    nought = jnp.zeros((TALL, PAIR), BF)
    clear(acc)

    def one(i, at, c):
        d = dh_ref[0, at, :]
        acc[at, :] += mm_t(jnp.concatenate([jnp.where(low, nought, d[:, PAIR : 2 * PAIR]), d[:, 2 * PAIR :]], 1), w)

    each(rows, TALL, one)

    @pl.when(pl.program_id(0) == pl.num_programs(0) - 1)
    def _():
        def last(i, at, sums):
            other, dg, ds = norm_back(acc[at, :], y_ref[at, :].astype(F32), gain_ref[...])
            other_ref[at, :] = other.astype(BF)
            return sums[0] + dg, sums[1] + ds

        dg_ref[...], ds_ref[...] = each(rows, ROWS, last, (jnp.zeros((1, width), F32),) * 2)


def self_back_part(dh_ref, w_ref, n_ref, dlow_ref, att_ref, dw_ref, dbias_ref, acc_ref):
    rows, width = n_ref.shape
    w = matrix(w_ref, 0, 5 * PAIR)
    clear(acc_ref)

    def one(i, at, total):
        d = dh_ref[0, at, :]
        acc_ref[at, :] += mm_t(d, w)
        return total + col_sum(d.astype(F32))

    dbias_ref[0, :, : 5 * PAIR] = each(rows, TALL, one, jnp.zeros((1, 5 * PAIR), F32))
    dbias_ref[0, :, 5 * PAIR :] = jnp.zeros((1, PAIR), F32)

    def weight(i, at, c):
        dqkv = t_mm(n_ref[:, at], dh_ref[0])
        do = t_mm(dlow_ref[:, at], att_ref[0])
        put_rows(dw_ref, i, dqkv[:, : 4 * PAIR], slice(0, 4 * PAIR))
        put_rows(dw_ref, i, dqkv[:, 4 * PAIR :] + do[:, :PAIR], slice(4 * PAIR, 5 * PAIR))
        put_rows(dw_ref, i, do[:, PAIR:], slice(5 * PAIR, 6 * PAIR))

    each(width, PART, weight)


def self_back_first_kernel(dh_ref, w_ref, n_ref, dlow_ref, att_ref, dw_ref, dbias_ref, acc_ref):
    self_back_part(dh_ref, w_ref, n_ref, dlow_ref, att_ref, dw_ref, dbias_ref, acc_ref)


def self_weight_kernel(dh_ref, n_ref, dlow_ref, att_ref, dw_ref):
    def weight(i, at, c):
        dqkv = t_mm(n_ref[:, at], dh_ref[0])
        do = t_mm(dlow_ref[:, at], att_ref[0])
        put_rows(dw_ref, i, dqkv[:, : 4 * PAIR], slice(0, 4 * PAIR))
        put_rows(dw_ref, i, dqkv[:, 4 * PAIR :] + do[:, :PAIR], slice(4 * PAIR, 5 * PAIR))
        put_rows(dw_ref, i, do[:, PAIR:], slice(5 * PAIR, 6 * PAIR))

    each(n_ref.shape[1], PART, weight)


def self_rows_part(dh_ref, w_ref, dbias_ref, acc_ref):
    rows = acc_ref.shape[0]
    w = matrix(w_ref, 0, 5 * PAIR)
    clear(acc_ref)

    def one(i, at, total):
        d = dh_ref[0, at, :]
        acc_ref[at, :] += mm_t(d, w)
        return total + col_sum(d.astype(F32))

    dbias_ref[0, :, : 5 * PAIR] = each(rows, TALL, one, jnp.zeros((1, 5 * PAIR), F32))
    dbias_ref[0, :, 5 * PAIR :] = jnp.zeros((1, PAIR), F32)


def self_rows_last_kernel(dh_ref, w_ref, x_ref, dmid_ref, before_ref, gain_ref, dbias_ref, own_ref, dg_ref, ds_ref, acc_ref):
    rows, width = x_ref.shape
    self_rows_part(dh_ref, w_ref, dbias_ref, acc_ref)

    @pl.when(pl.program_id(0) == pl.num_programs(0) - 1)
    def _():
        def last(i, at, sums):
            back, dg, ds = norm_back(acc_ref[at, :] + before_ref[at, :], x_ref[at, :].astype(F32), gain_ref[...])
            own_ref[at, :] = (dmid_ref[at, :] + back).astype(BF)
            return sums[0] + dg, sums[1] + ds

        dg_ref[...], ds_ref[...] = each(rows, ROWS, last, (jnp.zeros((1, width), F32),) * 2)


def collect_kernel(*refs):
    *ins, out_ref = refs
    out_ref[...] = jnp.zeros(out_ref.shape, F32)
    at = 0
    for ref in ins:
        for i in range(ref.shape[0]):
            out_ref[at : at + 1, :] = ref[i] if len(ref.shape) == 3 else ref[...]
            at += 1


def tables(image_sizes, count):
    images = image_sizes.shape[0]
    ends = jnp.cumsum(image_sizes)
    first = jnp.sum(jnp.where(image_sizes == LONGEST, ends - image_sizes, 0))
    places = (jnp.arange(count, dtype=jnp.int32) + first) % count
    passed = places[:, None] >= ends[None, :]
    segment = jnp.sum(passed.astype(jnp.int32), -1)
    start = jnp.sum(jnp.where(passed, image_sizes[None, :], 0), -1)
    place = (places - start).astype(F32)
    half = HEAD_DIM // 2
    lane = jnp.arange(PAIR, dtype=jnp.int32)
    freqs = 100.0 ** (-((lane % half).astype(F32) / half))
    angles = place[:, None] * freqs[None, :]
    sign = jnp.where(lane % HEAD_DIM < half, -1.0, 1.0)
    member = (lane % HEAD_DIM)[None, :] == segment[:, None]
    slot = ((lane % HEAD_DIM) < images)[None, :]
    kf = member.astype(BF)
    qf = jnp.where(slot & ~member, -FAR, 0.0).astype(BF)
    return first, qf, kf, jnp.cos(angles), jnp.sin(angles) * sign[None, :]


def whole(a):
    return pl.BlockSpec(a.shape, lambda j: (0,) * a.ndim)


def per_step(a, side=None):
    return pl.BlockSpec((1,) + a.shape[1:], lambda j: (j if side is None else 2 * j + side,) + (0,) * (a.ndim - 1))


def weight_block(g, cols, at, side=None):
    return pl.BlockSpec((g.shape[0], 1, 1, g.shape[3], cols), lambda j: (0, j // 2, j % 2, 0, at) if side is None else (0, j, side, 0, at))


def sds(shape, dtype):
    return jax.ShapeDtypeStruct(shape, dtype)


def call(kernel, name, steps, ins, outs, scratch=(), flops=0, moved=0, exps=0):
    return pl.pallas_call(
        kernel,
        grid=(steps,),
        in_specs=[s for _, s in ins],
        out_specs=[s for _, s in outs],
        out_shape=[o for o, _ in outs],
        scratch_shapes=list(scratch),
        cost_estimate=pl.CostEstimate(flops=int(flops) // CHEAP, bytes_accessed=int(moved) // CHEAP, transcendentals=int(exps) // CHEAP),
        name=name,
    )(*[a for a, _ in ins])


def body(tokens, cotangent, lengths, norm1_gain, norm1_shift, qkv_w, qkv_b, out_w, out_b, norm2_gain, norm2_shift,
         normy_gain, normy_shift, cq_w, cq_b, ckv_w, ckv_b, cout_w, cout_b, norm3_gain, norm3_shift, up_w, up_b, down_w, down_b):
    batches = tokens.shape[0]
    members = lax.axis_size("mp")
    n_dp = lax.axis_size("dp")
    assert members == 2 * batches
    me = lax.axis_index("mp")
    view = me // batches
    batch = me % batches
    local = tokens.shape[2]
    rows = local * members
    width = tokens.shape[3]
    r = qkv_w.shape[1]
    hw = cq_w.shape[2]
    fw = up_w.shape[2]
    partner = [(i, (i + batches) % members) for i in range(members)]
    groups = [[d * members + v * batches + b for d in range(n_dp) for b in range(batches)] for v in range(2)]
    both = ("dp", "mp")
    split = r % 16 == 0
    blocks, deep = (n_dp, r) if split else (1, n_dp * r)

    def of_view(a, which):
        return lax.dynamic_index_in_dim(a, which, 0, keepdims=False)

    def cols(q, k, v, o):
        return jnp.concatenate([q, k[..., PAIR:], k[..., :PAIR], v, o[..., PAIR:], o[..., :PAIR]], -1)

    def uncols(a):
        t = [a[..., i * PAIR : (i + 1) * PAIR] for i in range(a.shape[-1] // PAIR)]
        h = HEAD_DIM
        join = lambda x, y: jnp.concatenate([x, y], -1)
        heads = (join(t[0], t[1][..., :h]), join(t[2], t[1][..., h:]), join(t[3], t[4][..., :h]))
        return heads + ((join(t[5], t[4][..., h:]),) if len(t) > 5 else ())

    def pair_of(pack):
        return jnp.stack([of_view(pack, view), lax.ppermute(of_view(pack, 1 - view), "mp", partner)], 0)

    def gather(pair):
        got = lax.all_gather(pair, both, axis=0, axis_index_groups=groups).reshape(n_dp, batches, 2, r, -1)
        return got if split else got.transpose(1, 2, 0, 3, 4).reshape(1, batches, 2, deep, -1)

    flip = lambda a: a.swapaxes(-1, -2)
    pack_self = cols(qkv_w[:, :, 0], qkv_w[:, :, 1], qkv_w[:, :, 2], flip(out_w))
    pack_cross = cols(cq_w, ckv_w[:, :, 0], ckv_w[:, :, 1], flip(cout_w))
    w_att = gather(pair_of(jnp.concatenate([pack_self, pack_cross], -1)))
    pair_ffn = pair_of(jnp.concatenate([up_w, flip(down_w)], -1))

    none = jnp.zeros_like(cq_b)
    bias_pack = jnp.concatenate([cols(qkv_b[:, 0], qkv_b[:, 1], qkv_b[:, 2], none), cols(cq_b, ckv_b[:, 0], ckv_b[:, 1], none), up_b], -1)
    bias_rows = bias_pack.shape[-1] // width
    bias_pack = jnp.broadcast_to(bias_pack.reshape(2, 1, bias_rows, width), (2, batches, bias_rows, width))
    by_view = tokens.swapaxes(0, 1)
    sent_x = jnp.concatenate([by_view, bias_pack], 2).reshape(members, local + bias_rows, width)
    got_x = lax.all_to_all(sent_x, "mp", 0, 0, tiled=True)
    got_y = lax.all_to_all(by_view[::-1].reshape(members, local, width), "mp", 0, 0, tiled=True)
    got_z = lax.all_to_all(cotangent.swapaxes(0, 1).reshape(members, local, width), "mp", 0, 0, tiled=True)
    first, qf, kf, cosine, sine = tables(of_view(lengths[:, 0], batch), rows)

    def from_row(a, at):
        return lax.dynamic_slice_in_dim(jnp.concatenate([a, a], 0), at, rows, 0)

    x = from_row(got_x[:, :local].reshape(rows, width), first)
    y = from_row(got_y.reshape(rows, width), first)
    dz = from_row(got_z.reshape(rows, width), first)

    def by_step(a):
        a = a.reshape((2, batches) + a.shape[1:])
        return jnp.where(view == 0, a, a[::-1]).swapaxes(0, 1).reshape((members,) + a.shape[2:])

    def by_member(a):
        a = a.reshape((batches, 2) + a.shape[1:]).swapaxes(0, 1)
        return jnp.where(view == 0, a, a[::-1]).reshape((members,) + a.shape[2:])

    biases = by_step(got_x[:, local:]).astype(F32)
    self_bias, cross_bias, up_bias = biases[:, 0:1], biases[:, 1:2], biases[:, 2:]
    up_bias = up_bias.reshape(members, 1, fw)

    def mine(a):
        return of_view(a, view).astype(F32)[None]

    g1, s1, ob, g2, s2, gy, sy, cob, g3, s3, db = [
        mine(a) for a in (norm1_gain, norm1_shift, out_b, norm2_gain, norm2_shift, normy_gain, normy_shift, cout_b, norm3_gain, norm3_shift, down_b)]
    def given(*arrays):
        return [(a, whole(a)) for a in arrays]

    def steps(*arrays):
        return [(a, per_step(a)) for a in arrays]

    def full(*shape_types):
        return [(s, whole(s)) for s in shape_types]

    low = sds((rows, width), BF)
    high = sds((rows, width), F32)
    line = sds((1, width), F32)
    heads = sds((members, rows, 5 * PAIR), BF)
    att_low = sds((members, rows, 2 * PAIR), BF)
    att_high = sds((members, rows, 2 * PAIR), F32)
    bias_out = sds((members, 1, 6 * PAIR), F32)
    gemm = 2 * rows * width * width * members

    def attend(h):
        return call(functools.partial(attend_kernel, tile=384), "attend", members, steps(h) + given(qf, kf), [(s, per_step(s)) for s in (att_low, att_high)],
                    flops=12 * members * rows * rows * PAIR, moved=members * rows * PAIR * 22, exps=3 * members * rows * rows)

    def attend_back(h, o, do, lse, side=None):
        count = members if side is None else batches
        out = sds((count, rows, 5 * PAIR), BF)
        acc = pltpu.VMEM((3, rows, PAIR), F32)
        ins = [(a, per_step(a, side)) for a in (h, o, do, lse)]
        return call(functools.partial(attend_back_kernel, tile=256), "attend_back", count, ins + given(qf, kf, cosine, sine), [(out, per_step(out))],
                    [pltpu.VMEM((rows, PAIR), F32), acc, acc], flops=30 * count * rows * rows * PAIR, moved=count * rows * PAIR * 40,
                    exps=3 * count * rows * rows)[0]

    def project(att, at, res, bias, gain, shift):
        tall = 512
        part = lambda cols: pl.BlockSpec((tall, cols), lambda i: (i, 0))
        att_spec = pl.BlockSpec((members, tall, 2 * PAIR), lambda i: (0, i, 0))
        w_spec = pl.BlockSpec((blocks, batches, 2, deep, 2 * PAIR), lambda i: (0, 0, 0, 0, at))
        return call(out_kernel, "project", rows // tall, [(att, att_spec), (w_att, w_spec), (res, part(width))] + given(bias, gain, shift),
                    [(high, part(width)), (low, part(width))], flops=gemm / 3, moved=rows * width * 14)

    def project_back(d, at):
        return call(out_back_kernel, "project_back", members, given(d) + [(w_att, weight_block(w_att, 2 * PAIR, at))], [(att_low, per_step(att_low))],
                    flops=gemm / 3, moved=rows * width * 8)[0]

    def norm(a, gain, shift):
        spec = pl.BlockSpec((ROWS, width), lambda i: (i, 0))
        return call(norm_kernel, "norm", rows // ROWS, [(a, spec)] + given(gain, shift), [(low, spec)], moved=rows * width * 4)[0]

    def by_owner(piece):
        if not split:
            piece = piece.reshape(batches, piece.shape[2], n_dp, r, -1).transpose(2, 0, 1, 3, 4)
        return piece

    def scatter(piece):
        whole_piece = by_owner(piece).reshape(n_dp * batches, 2, r, -1)
        total = lax.psum_scatter(whole_piece, both, scatter_dimension=0, axis_index_groups=groups)
        return with_layout_constraint(total, Layout(major_to_minor=(0, 1, 2)))

    core_pairs = [(i, i ^ 1) for i in range(members)]
    x_pairs = [(i, i ^ 1) for i in range(n_dp)]
    place = lax.axis_index("dp")
    lines = n_dp // 2

    def pick(a, i, axis):
        return lax.dynamic_index_in_dim(a, i, axis, keepdims=False)

    by_hand = batches == 2 and n_dp <= 8
    x_place, z_place = place % 2, place // 2

    def added(terms):
        total = terms[0].astype(F32)
        for term in terms[1:]:
            total = total + term.astype(F32)
        return total

    def hop(terms, axis, other, mine, name, perm):
        got = lax.ppermute(added([pick(t, other, axis) for t in terms]).astype(BF), name, perm)
        return [pick(t, mine, axis) for t in terms] + [got]

    def over_cores(piece):
        return hop([piece], 1, 1 - batch, batch, "mp", core_pairs)

    def over_x(terms):
        terms = [t.reshape((t.shape[0] // 2, 2) + t.shape[1:]) for t in terms]
        return hop(terms, 1, 1 - x_place, x_place, "dp", x_pairs)

    def over_z(terms):
        total = added([pick(t, z_place, 0) for t in terms])
        for s in range(1, lines):
            perm = [(i, (i + 2 * s) % n_dp) for i in range(n_dp)]
            total = total + lax.ppermute(added([pick(t, (z_place + s) % lines, 0) for t in terms]).astype(BF), "dp", perm).astype(F32)
        return total.astype(BF)

    def to_partner(a):
        return lax.ppermute(a, "mp", partner)

    def both_views(keep, theirs):
        keep, theirs = keep.astype(F32), theirs.astype(F32)
        return jnp.stack([jnp.where(view == 0, keep, theirs), jnp.where(view == 0, theirs, keep)], 0)

    n1 = norm(x, g1, s1)
    side = norm(y, gy, sy)
    pair_ffn, n1, side, qf, kf, cosine, sine = lax.optimization_barrier((pair_ffn, n1, side, qf, kf, cosine, sine))
    w_ffn = gather(pair_ffn)
    hs = call(self_in_kernel, "self_in", members, given(n1) + [(w_att, weight_block(w_att, 6 * PAIR, 0))] + steps(self_bias) + given(cosine, sine),
              [(heads, per_step(heads))], flops=gemm, moved=rows * width * 16)[0]
    att, lse = attend(hs)
    middle, n2 = project(att, 2, x, ob, g2, s2)
    hc = call(cross_in_kernel, "cross_in", members, given(n2, side) + [(w_att, weight_block(w_att, 6 * PAIR, 1))] + steps(cross_bias) + given(cosine, sine),
              [(heads, per_step(heads))], flops=gemm, moved=rows * width * 16)[0]
    catt, clse = attend(hc)
    middle2, n3 = project(catt, 5, middle, cob, g3, s3)

    dw_ffn = sds((blocks, batches, 2, deep, 2 * fw), BF)
    dw_ffn_spec = pl.BlockSpec((blocks, 1, 1, deep, 2 * fw), lambda j: (0, j // 2, j % 2, 0, 0))
    up_line = sds((members, 1, fw), F32)
    output, d_mid2, d_cross, dw_f, d_upb, gg3, gs3, d_db, d_cob = call(
        ffn_kernel, "ffn", members,
        given(middle2, n3, dz) + [(w_ffn, weight_block(w_ffn, fw, 0)), (w_ffn, weight_block(w_ffn, fw, 1))] + steps(up_bias) + given(db, g3),
        full(low, high, low) + [(dw_ffn, dw_ffn_spec), (up_line, per_step(up_line))] + full(line, line, line, line),
        [pltpu.VMEM((rows, width), F32)] * 2 + [pltpu.VMEM((rows, fw), BF)] * 2,
        flops=6 * gemm, moved=rows * width * 60, exps=rows * fw * members * 2)

    total_ffn = scatter(dw_f)
    d_catt = project_back(d_cross, 5)
    d_hc = attend_back(hc, catt, d_catt, clse)
    dw_att = sds((blocks, batches, 2, deep, 6 * PAIR), BF)
    dw_spec = pl.BlockSpec((blocks, 1, 1, deep, 6 * PAIR), lambda j: (0, j // 2, j % 2, 0, 0))
    dw_cross, d_crossb, d_mid, d_branch, gg2, gs2, d_ob = call(
        cross_back_kernel, "cross_back", members,
        steps(d_hc) + [(w_att, weight_block(w_att, 6 * PAIR, 1))] + given(n2, side, d_cross) + steps(catt) + given(middle, d_mid2, g2),
        [(dw_att, dw_spec), (bias_out, per_step(bias_out))] + full(high, low, line, line, line),
        [pltpu.VMEM((rows, width), F32)], flops=2 * gemm, moved=rows * width * 30)

    def side_back(dh):
        return call(side_back_kernel, "side_back", members, steps(dh) + [(w_att, weight_block(w_att, 6 * PAIR, 1))] + given(y, gy),
                    full(low, line, line), [pltpu.VMEM((rows, width), F32)], flops=gemm, moved=rows * width * 16)

    d_att = project_back(d_branch, 2)
    total_cross = scatter(dw_cross)

    dw_part = sds((blocks, batches, 1, deep, 6 * PAIR), BF)
    dw_part_spec = pl.BlockSpec((blocks, 1, 1, deep, 6 * PAIR), lambda j: (0, j, 0, 0, 0))
    bias_part = sds((batches, 1, 6 * PAIR), F32)

    def self_back_first(t, dh):
        ins = steps(dh) + [(w_att, weight_block(w_att, 6 * PAIR, 0, t))] + given(n1, d_branch) + [(att, per_step(att, t))]
        outs = [(dw_part, dw_part_spec), (bias_part, per_step(bias_part))]
        return call(self_back_first_kernel, "self_back_first", batches, ins, outs + full(high), flops=1.5 * gemm, moved=rows * width * 24)

    def self_weight(t, dh):
        ins = steps(dh) + given(n1, d_branch) + [(att, per_step(att, t))]
        return call(self_weight_kernel, "self_weight", batches, ins, [(dw_part, dw_part_spec)], flops=gemm, moved=rows * width * 16)[0]

    def self_rows(t, dh, *more):
        ins = steps(dh) + [(w_att, weight_block(w_att, 6 * PAIR, 0, t))] + given(*more)
        return call(self_rows_last_kernel, "self_rows", batches, ins, [(bias_part, per_step(bias_part))] + full(low, line, line),
                    [pltpu.VMEM((rows, width), F32)], flops=gemm / 2, moved=rows * width * 20)

    def home(a):
        return lax.all_to_all(a.reshape(members, local, width), "mp", 0, 0, tiled=True).reshape(2, batches, local, width)

    d_h1 = attend_back(hs, att, d_att, lse, 1)
    dw_self1, d_selfb1, acc = self_back_first(1, d_h1)
    d_att, acc, dw_self1 = lax.optimization_barrier((d_att, acc, dw_self1))
    output = from_row(output, rows - first)
    if by_hand:
        self1 = over_cores(by_owner(dw_self1))
        d_att, output, got = lax.optimization_barrier((d_att, output, self1[1]))
        self1 = over_x([self1[0], got])
    got_output = home(output)
    d_h0 = attend_back(hs, att, d_att, lse, 0)
    d_h0, total_ffn, got_output = lax.optimization_barrier((d_h0, total_ffn, got_output))
    their_ffn = to_partner(total_ffn[1])
    if by_hand:
        d_h0, got = lax.optimization_barrier((d_h0, self1[2]))
        self1 = self1[:2] + [got]

        def z_hop(s):
            send = added([pick(t, (z_place + s) % lines, 0) for t in self1]).astype(BF)
            return lax.ppermute(send, "dp", [(i, (i + 2 * s) % n_dp) for i in range(n_dp)])

        near = z_hop(1)
    dw_self0 = self_weight(0, d_h0)
    if by_hand:
        dw_self0, d_h0, near = lax.optimization_barrier((dw_self0, d_h0, near))
        self0 = over_cores(by_owner(dw_self0))
        far = [z_hop(s) for s in range(2, lines)]
    d_selfb0, own, gg1, gs1 = self_rows(0, d_h0, x, d_mid, acc, g1)
    if by_hand:
        own, gg1, their_ffn, got, *far = lax.optimization_barrier((own, gg1, their_ffn, self0[1], *far))
        total1 = added([pick(t, z_place, 0) for t in self1] + [near] + far).astype(BF)
        self0 = [t.reshape((lines, 2) + t.shape[1:]) for t in (self0[0], got)]
        send = added([pick(t, 1 - x_place, 1) for t in self0]).astype(BF)
        own, send, d_hc = lax.optimization_barrier((own, send, d_hc))
        self0 = [pick(t, x_place, 1) for t in self0] + [lax.ppermute(send, "dp", x_pairs)]
    own = from_row(own, rows - first)
    got_own = home(own)
    other, ggy, gsy = side_back(d_hc)
    if by_hand:
        other, x_sum = lax.optimization_barrier((other, self0[2]))
        self0 = self0[:2] + [x_sum]
    lines_out = [gg1, gs1, d_ob, gg2, gs2, ggy, gsy, d_cob, gg3, gs3, d_db, d_selfb0, d_selfb1, d_crossb, d_upb]
    count = 11 + 3 * members
    collected = sds((-(-count // 8) * 8, width), F32)
    small = call(collect_kernel, "collect", 1, given(*lines_out), full(collected))[0]
    if by_hand:
        small = small + lax.ppermute(small, "mp", core_pairs)
        sum_ffn = both_views(total_ffn[0], their_ffn)
        up_wg, down_wg = sum_ffn[..., :fw], flip(sum_ffn[..., fw:])
        their1 = to_partner(total1)
        flat = small + lax.ppermute(small, "dp", x_pairs)
        flat, got, their1, got_own, other, up_wg, down_wg, total_cross = lax.optimization_barrier((flat, self0[2], their1, got_own, other, up_wg, down_wg, total_cross))
        other = from_row(other, rows - first)
        got_other = home(other)
        their_cross = to_partner(total_cross[1])
        flat = lax.reduce_precision(flat, 8, 7)
        self0 = self0[:2] + [got]
        total0 = added([pick(t, z_place, 0) for t in self0])
        on_line = [flat]
        for s in range(1, lines):
            send = added([pick(t, (z_place + s) % lines, 0) for t in self0]).astype(BF)
            got = lax.ppermute(jnp.concatenate([send.reshape(-1, width), flat.astype(BF)], 0), "dp", [(i, (i + 2 * s) % n_dp) for i in range(n_dp)])
            total0 = total0 + got[: send.size // width].reshape(total0.shape).astype(F32)
            on_line.append(got[send.size // width :].astype(F32))
        on_line = jnp.stack(on_line, 0)
        flat = sum(pick(on_line, (z_place - p) % lines, 0) for p in range(lines))
        flat_in = to_partner(flat)
        sum_self = both_views(total0[0], their1[0])
    else:
        got_other = home(from_row(other, rows - first))
        total_self = scatter(jnp.concatenate([dw_self0, dw_self1], 2))
        their_cross = to_partner(total_cross[1])
        sum_self = both_views(total_self[0], to_partner(total_self[1]))
        sums = lax.psum(jnp.stack([jnp.where(view == 0, small, 0.0), jnp.where(view == 1, small, 0.0)], 0), both)
        flat, flat_in = pick(sums, view, 0), pick(sums, 1 - view, 0)
        sum_ffn = both_views(total_ffn[0], their_ffn)
        up_wg, down_wg = sum_ffn[..., :fw], flip(sum_ffn[..., fw:])
    sum_cross = both_views(total_cross[0], their_cross)

    sums = both_views(flat[:11].reshape(-1), flat_in[:11].reshape(-1))
    g1g, s1g, obg, g2g, s2g, gyg, syg, cobg, g3g, s3g, dbg = [sums[:, i * width : (i + 1) * width] for i in range(11)]

    def member_row(own_row, other_row):
        return both_views(pick(flat, own_row, 0), pick(flat_in, other_row, 0))

    self_part = uncols(member_row(11 + batch, 11 + batches + batch)[:, : 5 * PAIR])
    start = 11 + members + 2 * batch
    cross_part = uncols(member_row(start, start + 1)[:, : 5 * PAIR])
    upb_grad = member_row(start + members, start + members + 1)

    block_output = got_output.swapaxes(0, 1)
    input_grad = (got_own.astype(F32) + got_other[::-1].astype(F32)).swapaxes(0, 1)

    q, k, v, o = uncols(sum_self)
    cq, ck, cv, co = uncols(sum_cross)
    return (block_output, input_grad, g1g, s1g, jnp.stack([q, k, v], 2), jnp.stack(self_part, 1), flip(o), obg, g2g, s2g, gyg, syg,
            cq, cross_part[0], jnp.stack([ck, cv], 2), jnp.stack(cross_part[1:], 1), flip(co), cobg, g3g, s3g,
            up_wg, upb_grad, down_wg, dbg)


def solution(mesh):
    rows = P(None, None, ("dp", "mp"), None)
    wide = P(None, "dp", None, "mp")
    by_rows = P(None, "dp", "mp")
    by_cols = P(None, "mp", "dp")
    parts = P(None, None, "mp")
    flat = P(None, "mp")
    same = P()
    in_specs = (rows, rows, P(None, "dp", None), same, same, wide, parts, by_cols, same, same, same, same, same, by_rows, flat, wide, parts,
                by_cols, same, same, same, by_rows, flat, by_cols, same)
    out_specs = (rows, rows, same, same, wide, parts, by_cols, same, same, same, same, same, by_rows, flat, wide, parts, by_cols, same,
                 same, same, by_rows, flat, by_cols, same)
    return jax.shard_map(body, mesh=mesh, in_specs=in_specs, out_specs=out_specs, check_vma=False)
```

```python
import functools
import math

import jax
import jax.numpy as jnp
from jax import lax
from jax.experimental import pallas as pl
from jax.experimental.layout import Layout, with_layout_constraint
from jax.experimental.pallas import tpu as pltpu
from jax.sharding import PartitionSpec as P

HEAD_DIM = 64
PAIR = 2 * HEAD_DIM
FAR = 1e30
BF = jnp.bfloat16
F32 = jnp.float32
LONGEST = 768
ROWS = 256
TALL = 1024
CHEAP = 16
FFN_ROWS = 1024
PART = 768
norm_epsilon = 1e-06


def mm(a, b):
    return jnp.dot(a, b, preferred_element_type=F32)


def mm_t(a, b):
    return lax.dot_general(a, b, (((1,), (1,)), ((), ())), preferred_element_type=F32)


def t_mm(a, b):
    return lax.dot_general(a, b, (((0,), (0,)), ((), ())), preferred_element_type=F32)


def each(count, size, step, carry=None):
    def go(i, c):
        return step(i, pl.ds(pl.multiple_of(i * size, size), size), c)

    return lax.fori_loop(0, count // size, go, carry)


def normed(rows, gain, shift):
    centred = rows - jnp.mean(rows, -1, keepdims=True)
    spread = jnp.mean(centred * centred, -1, keepdims=True)
    return (centred * lax.rsqrt(spread + norm_epsilon) * gain + shift).astype(BF)


def norm_back(grad, rows, gain):
    centred = rows - jnp.mean(rows, -1, keepdims=True)
    scale = lax.rsqrt(jnp.mean(centred * centred, -1, keepdims=True) + norm_epsilon)
    hat = centred * scale
    w = grad * gain
    back = scale * (w - jnp.mean(w, -1, keepdims=True) - hat * jnp.mean(w * hat, -1, keepdims=True))
    return back, col_sum(grad * hat), col_sum(grad)


def col_sum(a):
    return jnp.sum(a, 0, keepdims=True)


def swap_halves(u):
    lane = lax.broadcasted_iota(jnp.int32, u.shape, 1)
    half = HEAD_DIM // 2
    return jnp.where(lane % HEAD_DIM < half, pltpu.roll(u, PAIR - half, 1), pltpu.roll(u, half, 1))


def turn(u, cosine, sine):
    return u * cosine + swap_halves(u) * sine


def turn_back(u, cosine, sine):
    return u * cosine - swap_halves(u) * sine


def other_half(u):
    return pltpu.roll(u.astype(F32), HEAD_DIM, 1).astype(u.dtype)


def is_low(count):
    return lax.broadcasted_iota(jnp.int32, (count, PAIR), 1) < HEAD_DIM


def matrix(ref, start=0, stop=None):
    stop = ref.shape[4] if stop is None else stop
    return ref[:, 0, 0, :, start:stop].reshape(ref.shape[0] * ref.shape[3], stop - start)


def put_rows(ref, i, value, cols=None):
    blocks, rows = ref.shape[0], ref.shape[3]
    cols = slice(None) if cols is None else cols
    value = value.astype(ref.dtype)
    if blocks == 1:
        ref[0, 0, 0, pl.ds(pl.multiple_of(i * PART, PART), PART), cols] = value
    else:
        k = PART // rows
        ref[pl.ds(i * k, k), 0, 0, :, cols] = value.reshape(k, rows, value.shape[-1])


def store_heads(ref, at, tiles, cosine, sine):
    low = is_low(tiles[0].shape[0])
    scale = HEAD_DIM ** -0.5
    mixed = turn(tiles[1], cosine, sine)
    done = (turn(tiles[0], cosine, sine) * scale, jnp.where(low, mixed * scale, mixed), turn(tiles[2], cosine, sine), tiles[3], tiles[4])
    for i, tile in enumerate(done):
        ref[0, at, i * PAIR : (i + 1) * PAIR] = tile.astype(BF)


def split_tiles(a):
    return [a[:, i * PAIR : (i + 1) * PAIR] for i in range(a.shape[1] // PAIR)]


def norm_kernel(x_ref, gain_ref, shift_ref, n_ref):
    n_ref[...] = normed(x_ref[...].astype(F32), gain_ref[...], shift_ref[...])


def self_in_kernel(n_ref, w_ref, bias_ref, cos_ref, sin_ref, heads_ref):
    w = matrix(w_ref, 0, 5 * PAIR)
    bias = bias_ref[0, :, : 5 * PAIR]

    def one(i, at, c):
        store_heads(heads_ref, at, split_tiles(mm(n_ref[at, :], w) + bias), cos_ref[at, :], sin_ref[at, :])

    each(n_ref.shape[0], TALL, one)


def cross_in_kernel(n_ref, side_ref, w_ref, bias_ref, cos_ref, sin_ref, heads_ref):
    wq = matrix(w_ref, 0, 2 * PAIR)
    wkv = matrix(w_ref, PAIR, 5 * PAIR)
    bias = split_tiles(bias_ref[0, :, : 5 * PAIR])
    low = is_low(TALL)

    def one(i, at, c):
        q0, q2 = split_tiles(mm(n_ref[at, :], wq))
        k2, k0, v0, v2 = split_tiles(mm(side_ref[at, :], wkv))
        tiles = [q0, jnp.where(low, q2, k2), k0, v0, v2]
        store_heads(heads_ref, at, [t + b for t, b in zip(tiles, bias)], cos_ref[at, :], sin_ref[at, :])

    each(n_ref.shape[0], TALL, one)


def spans(rows):
    return ((0, LONGEST), (LONGEST, rows - LONGEST))


def attend_kernel(heads_ref, qf_ref, kf_ref, o_ref, lse_ref, *, tile):
    rows = heads_ref.shape[1]
    for start, size in spans(rows):
        near = pl.ds(start, size)
        low = is_low(size)
        t3, t1, t2, t4 = [heads_ref[0, near, i * PAIR : (i + 1) * PAIR] for i in range(1, 5)]
        kf = kf_ref[near, :]
        one = jnp.ones_like(t2)
        keys = (jnp.where(low, t1, kf), jnp.where(low, kf, t1), jnp.where(low, other_half(t3), kf))
        vals = (jnp.where(low, t2, one), jnp.where(low, one, t2), jnp.where(low, one, other_half(t4)))
        step = min(tile, size)
        low_t = is_low(step)
        for t in range(size // step):
            at = pl.ds(start + t * step, step)
            qf = qf_ref[at, :]
            q0 = heads_ref[0, at, :PAIR]
            queries = (jnp.where(low_t, q0, qf), jnp.where(low_t, qf, q0), jnp.where(low_t, heads_ref[0, at, PAIR : 2 * PAIR], qf))
            outs, lses = [], []
            for h in range(3):
                s = mm_t(queries[h], keys[h])
                top = jnp.max(s, -1, keepdims=True)
                o = mm(jnp.exp(s - top).astype(BF), vals[h])
                total = pltpu.roll(o, HEAD_DIM, 1)
                outs.append(o / total)
                lses.append(top + jnp.log(total))
            o_ref[0, at, :PAIR] = jnp.where(low_t, 0.0, outs[2]).astype(BF)
            o_ref[0, at, PAIR:] = jnp.where(low_t, outs[0], outs[1]).astype(BF)
            lse_ref[0, at, :PAIR] = jnp.where(low_t, 0.0, lses[2])
            lse_ref[0, at, PAIR:] = jnp.where(low_t, lses[0], lses[1])


def three_parts(u):
    a = u.astype(BF).astype(F32)
    b = (u - a).astype(BF).astype(F32)
    return a, b, u - a - b


def attend_back_kernel(heads_ref, o_ref, do_ref, lse_ref, qf_ref, kf_ref, cos_ref, sin_ref, out_ref, dq2_acc, dk_acc, dv_acc, *, tile):
    rows = heads_ref.shape[1]
    scale = HEAD_DIM ** -0.5
    for start, size in spans(rows):
        near = pl.ds(start, size)
        low = is_low(size)
        within = lax.broadcasted_iota(jnp.int32, (size, PAIR), 1) % HEAD_DIM
        t3, t1, t2, t4 = [heads_ref[0, near, i * PAIR : (i + 1) * PAIR] for i in range(1, 5)]
        ones3 = jnp.where(within < 3, 1.0, 0.0).astype(BF)
        kf = kf_ref[near, :] + jnp.where((within >= 3) & (within < 6), 1.0, 0.0).astype(BF)
        k2 = other_half(t3)
        raw_keys = (t1, t1, k2)
        keys = (jnp.where(low, t1, kf), jnp.where(low, kf, t1), jnp.where(low, k2, kf))
        vals = (jnp.where(low, t2, ones3), jnp.where(low, ones3, t2), jnp.where(low, t4, ones3))
        step = min(tile, size)
        low_t = is_low(step)
        high_t = ~low_t
        within_t = lax.broadcasted_iota(jnp.int32, (step, PAIR), 1) % HEAD_DIM
        for t in range(size // step):
            at = pl.ds(start + t * step, step)
            q0, q2 = heads_ref[0, at, :PAIR], heads_ref[0, at, PAIR : 2 * PAIR]
            do2, do0 = do_ref[0, at, :PAIR], do_ref[0, at, PAIR:]
            prod2 = do2.astype(F32) * o_ref[0, at, :PAIR].astype(F32)
            prod0 = do0.astype(F32) * o_ref[0, at, PAIR:].astype(F32)
            lse2, lse0 = lse_ref[0, at, :PAIR], lse_ref[0, at, PAIR:]
            qf = qf_ref[at, :].astype(F32)
            lse_swapped = pltpu.roll(lse0, HEAD_DIM, 1)
            items = ((q0, do0, low_t, low_t, prod0, lse_swapped), (q0, do0, high_t, high_t, prod0, lse_swapped), (q2, other_half(do2), low_t, high_t, prod2, lse2))
            dqs = []
            for h, (q, do, mine, where_o, prod, lse) in enumerate(items):
                a, b, c = three_parts(-jnp.sum(jnp.where(where_o, prod, 0.0), -1, keepdims=True))
                feat = jnp.where(within_t == 0, a, jnp.where(within_t == 1, b, jnp.where(within_t == 2, c, 0.0)))
                doh = jnp.where(mine, do, feat.astype(BF))
                a, b, c = three_parts(-lse)
                feat = jnp.where(within_t == 3, a, jnp.where(within_t == 4, b, jnp.where(within_t == 5, c, qf)))
                qh = jnp.where(mine, q, feat.astype(BF))
                p = jnp.exp(mm_t(keys[h], qh))
                ds = (p * mm_t(vals[h], doh)).astype(BF)
                dv = mm(p.astype(BF), do)
                dk = mm(ds, q)
                dqs.append(t_mm(ds, raw_keys[h]) * scale)
                if t == 0:
                    dv_acc[h, near, :] = dv
                    dk_acc[h, near, :] = dk
                else:
                    dv_acc[h, near, :] += dv
                    dk_acc[h, near, :] += dk
            dq = jnp.where(low_t, dqs[0], dqs[1])
            out_ref[0, at, :PAIR] = turn_back(dq, cos_ref[at, :], sin_ref[at, :]).astype(BF)
            dq2_acc[at, :] = dqs[2]

    def finish(i, at, c):
        low_r = is_low(ROWS)
        cosine, sine = cos_ref[at, :], sin_ref[at, :]
        out_ref[0, at, 2 * PAIR : 3 * PAIR] = turn_back(jnp.where(low_r, dk_acc[0, at, :], dk_acc[1, at, :]), cosine, sine).astype(BF)
        out_ref[0, at, 3 * PAIR : 4 * PAIR] = jnp.where(low_r, dv_acc[0, at, :], dv_acc[1, at, :]).astype(BF)
        last = jnp.where(low_r, dq2_acc[at, :], pltpu.roll(dk_acc[2, at, :], HEAD_DIM, 1))
        out_ref[0, at, PAIR : 2 * PAIR] = turn_back(last, cosine, sine).astype(BF)
        out_ref[0, at, 4 * PAIR :] = jnp.where(low_r, dv_acc[2, at, :], 0.0).astype(BF)

    each(rows, ROWS, finish)


def out_kernel(att_ref, w_ref, res_ref, bias_ref, gain_ref, shift_ref, mid_ref, n_ref):
    blocks, batches, two, deep, cols = w_ref.shape
    total = None
    for b in range(batches):
        for t in range(two):
            part = mm_t(att_ref[2 * b + t], w_ref[:, b, t].reshape(blocks * deep, cols))
            total = part if total is None else total + part
    mid = res_ref[...].astype(F32) + total + bias_ref[...]
    mid_ref[...] = mid
    n_ref[...] = normed(mid, gain_ref[...], shift_ref[...])


def clear(*refs):
    @pl.when(pl.program_id(0) == 0)
    def _():
        def zero(i, at, c):
            for ref in refs:
                ref[at, :] = jnp.zeros((ROWS, ref.shape[1]), F32)

        each(refs[0].shape[0], ROWS, zero)


def ffn_kernel(mid_ref, n_ref, dz_ref, up_ref, down_ref, upb_ref, downb_ref, gain_ref,
               out_ref, dmid_ref, dlow_ref, dw_ref, dupb_ref, dgain_ref, dshift_ref, ddownb_ref, dcob_ref,
               acc_out, acc_dn, hid, dhid):
    j = pl.program_id(0)
    rows = mid_ref.shape[0]
    width = mid_ref.shape[1]
    up = matrix(up_ref)
    down = matrix(down_ref)
    bias = upb_ref[0]
    clear(acc_out, acc_dn)

    def one(i, at, total):
        h = mm(n_ref[at, :], up) + bias
        phi = 0.5 * (1.0 + lax.erf(h * (0.5 ** 0.5)))
        slope = phi + h * jnp.exp(-0.5 * h * h) * (0.5 / math.pi) ** 0.5
        low = (h * phi).astype(BF)
        hid[at, :] = low
        acc_out[at, :] += mm_t(low, down)
        d = (mm(dz_ref[at, :], down) * slope).astype(BF)
        dhid[at, :] = d
        acc_dn[at, :] += mm_t(d, up)
        return total + col_sum(d.astype(F32))

    dupb_ref[0] = each(rows, FFN_ROWS, one, jnp.zeros((1, up.shape[1]), F32))

    def weight(i, at, c):
        put_rows(dw_ref, i, t_mm(n_ref[:, at], dhid[...]), slice(0, dhid.shape[1]))
        put_rows(dw_ref, i, t_mm(dz_ref[:, at], hid[...]), slice(dhid.shape[1], None))

    each(width, PART, weight)

    @pl.when(j == pl.num_programs(0) - 1)
    def _():
        def last(i, at, sums):
            mid = mid_ref[at, :]
            out_ref[at, :] = (mid + acc_out[at, :] + downb_ref[...]).astype(BF)
            back, dg, ds = norm_back(acc_dn[at, :], mid, gain_ref[...])
            dz = dz_ref[at, :].astype(F32)
            total = dz + back
            dmid_ref[at, :] = total
            low = total.astype(BF)
            dlow_ref[at, :] = low
            return tuple(s + a for s, a in zip(sums, (dg, ds, col_sum(dz), col_sum(low.astype(F32)))))

        sums = each(rows, ROWS, last, (jnp.zeros((1, width), F32),) * 4)
        dgain_ref[...], dshift_ref[...], ddownb_ref[...], dcob_ref[...] = sums


def out_back_kernel(d_ref, w_ref, datt_ref):
    datt_ref[0] = mm(d_ref[...], matrix(w_ref)).astype(BF)


def cross_back_kernel(dh_ref, w_ref, n_ref, side_ref, dlow_ref, att_ref, mid_ref, dmid_ref, gain_ref,
                      dw_ref, dbias_ref, dout_ref, dbranch_ref, dg_ref, ds_ref, dob_ref, acc_n):
    j = pl.program_id(0)
    rows, width = mid_ref.shape
    wq = matrix(w_ref, 0, 2 * PAIR)
    low = is_low(TALL)
    nought = jnp.zeros((TALL, PAIR), BF)
    clear(acc_n)

    def one(i, at, total):
        d = dh_ref[0, at, :]
        acc_n[at, :] += mm_t(jnp.concatenate([d[:, :PAIR], jnp.where(low, d[:, PAIR : 2 * PAIR], nought)], 1), wq)
        return total + col_sum(d.astype(F32))

    dbias_ref[0, :, : 5 * PAIR] = each(rows, TALL, one, jnp.zeros((1, 5 * PAIR), F32))
    dbias_ref[0, :, 5 * PAIR :] = jnp.zeros((1, PAIR), F32)
    low_p = is_low(PART)

    def weight(i, at, c):
        dq = t_mm(n_ref[:, at], dh_ref[0, :, : 2 * PAIR])
        dkv = t_mm(side_ref[:, at], dh_ref[0, :, PAIR:])
        do = t_mm(dlow_ref[:, at], att_ref[0])
        put_rows(dw_ref, i, dq[:, :PAIR], slice(0, PAIR))
        put_rows(dw_ref, i, jnp.where(low_p, dq[:, PAIR:], dkv[:, :PAIR]), slice(PAIR, 2 * PAIR))
        put_rows(dw_ref, i, dkv[:, PAIR : 3 * PAIR], slice(2 * PAIR, 4 * PAIR))
        put_rows(dw_ref, i, dkv[:, 3 * PAIR :] + do[:, :PAIR], slice(4 * PAIR, 5 * PAIR))
        put_rows(dw_ref, i, do[:, PAIR:], slice(5 * PAIR, 6 * PAIR))

    each(width, PART, weight)

    @pl.when(j == pl.num_programs(0) - 1)
    def _():
        def last(i, at, sums):
            back, dg, ds = norm_back(acc_n[at, :], mid_ref[at, :], gain_ref[...])
            total = dmid_ref[at, :] + back
            dout_ref[at, :] = total
            branch = total.astype(BF)
            dbranch_ref[at, :] = branch
            return tuple(s + a for s, a in zip(sums, (dg, ds, col_sum(branch.astype(F32)))))

        sums = each(rows, ROWS, last, (jnp.zeros((1, width), F32),) * 3)
        dg_ref[...], ds_ref[...], dob_ref[...] = sums


def side_back_kernel(dh_ref, w_ref, y_ref, gain_ref, other_ref, dg_ref, ds_ref, acc):
    rows, width = y_ref.shape
    w = matrix(w_ref, PAIR, 5 * PAIR)
    low = is_low(TALL)
    nought = jnp.zeros((TALL, PAIR), BF)
    clear(acc)

    def one(i, at, c):
        d = dh_ref[0, at, :]
        acc[at, :] += mm_t(jnp.concatenate([jnp.where(low, nought, d[:, PAIR : 2 * PAIR]), d[:, 2 * PAIR :]], 1), w)

    each(rows, TALL, one)

    @pl.when(pl.program_id(0) == pl.num_programs(0) - 1)
    def _():
        def last(i, at, sums):
            other, dg, ds = norm_back(acc[at, :], y_ref[at, :].astype(F32), gain_ref[...])
            other_ref[at, :] = other.astype(BF)
            return sums[0] + dg, sums[1] + ds

        dg_ref[...], ds_ref[...] = each(rows, ROWS, last, (jnp.zeros((1, width), F32),) * 2)


def self_back_part(dh_ref, w_ref, n_ref, dlow_ref, att_ref, dw_ref, dbias_ref, acc_ref):
    rows, width = n_ref.shape
    w = matrix(w_ref, 0, 5 * PAIR)
    clear(acc_ref)

    def one(i, at, total):
        d = dh_ref[0, at, :]
        acc_ref[at, :] += mm_t(d, w)
        return total + col_sum(d.astype(F32))

    dbias_ref[0, :, : 5 * PAIR] = each(rows, TALL, one, jnp.zeros((1, 5 * PAIR), F32))
    dbias_ref[0, :, 5 * PAIR :] = jnp.zeros((1, PAIR), F32)

    def weight(i, at, c):
        dqkv = t_mm(n_ref[:, at], dh_ref[0])
        do = t_mm(dlow_ref[:, at], att_ref[0])
        put_rows(dw_ref, i, dqkv[:, : 4 * PAIR], slice(0, 4 * PAIR))
        put_rows(dw_ref, i, dqkv[:, 4 * PAIR :] + do[:, :PAIR], slice(4 * PAIR, 5 * PAIR))
        put_rows(dw_ref, i, do[:, PAIR:], slice(5 * PAIR, 6 * PAIR))

    each(width, PART, weight)


def self_back_first_kernel(dh_ref, w_ref, n_ref, dlow_ref, att_ref, dw_ref, dbias_ref, acc_ref):
    self_back_part(dh_ref, w_ref, n_ref, dlow_ref, att_ref, dw_ref, dbias_ref, acc_ref)


def self_back_last_kernel(dh_ref, w_ref, n_ref, dlow_ref, att_ref, x_ref, dmid_ref, before_ref, gain_ref,
                          dw_ref, dbias_ref, own_ref, dg_ref, ds_ref, acc_ref):
    j = pl.program_id(0)
    rows, width = x_ref.shape
    self_back_part(dh_ref, w_ref, n_ref, dlow_ref, att_ref, dw_ref, dbias_ref, acc_ref)

    @pl.when(j == pl.num_programs(0) - 1)
    def _():
        def last(i, at, sums):
            back, dg, ds = norm_back(acc_ref[at, :] + before_ref[at, :], x_ref[at, :].astype(F32), gain_ref[...])
            own_ref[at, :] = (dmid_ref[at, :] + back).astype(BF)
            return sums[0] + dg, sums[1] + ds

        dg_ref[...], ds_ref[...] = each(rows, ROWS, last, (jnp.zeros((1, width), F32),) * 2)


def collect_kernel(*refs):
    *ins, out_ref = refs
    out_ref[...] = jnp.zeros(out_ref.shape, F32)
    at = 0
    for ref in ins:
        for i in range(ref.shape[0]):
            out_ref[at : at + 1, :] = ref[i] if len(ref.shape) == 3 else ref[...]
            at += 1


def tables(image_sizes, count):
    images = image_sizes.shape[0]
    ends = jnp.cumsum(image_sizes)
    first = jnp.sum(jnp.where(image_sizes == LONGEST, ends - image_sizes, 0))
    places = (jnp.arange(count, dtype=jnp.int32) + first) % count
    passed = places[:, None] >= ends[None, :]
    segment = jnp.sum(passed.astype(jnp.int32), -1)
    start = jnp.sum(jnp.where(passed, image_sizes[None, :], 0), -1)
    place = (places - start).astype(F32)
    half = HEAD_DIM // 2
    lane = jnp.arange(PAIR, dtype=jnp.int32)
    freqs = 100.0 ** (-((lane % half).astype(F32) / half))
    angles = place[:, None] * freqs[None, :]
    sign = jnp.where(lane % HEAD_DIM < half, -1.0, 1.0)
    member = (lane % HEAD_DIM)[None, :] == segment[:, None]
    slot = ((lane % HEAD_DIM) < images)[None, :]
    kf = member.astype(BF)
    qf = jnp.where(slot & ~member, -FAR, 0.0).astype(BF)
    return first, qf, kf, jnp.cos(angles), jnp.sin(angles) * sign[None, :]


def whole(a):
    return pl.BlockSpec(a.shape, lambda j: (0,) * a.ndim)


def per_step(a, side=None):
    return pl.BlockSpec((1,) + a.shape[1:], lambda j: (j if side is None else 2 * j + side,) + (0,) * (a.ndim - 1))


def weight_block(g, cols, at, side=None):
    return pl.BlockSpec((g.shape[0], 1, 1, g.shape[3], cols), lambda j: (0, j // 2, j % 2, 0, at) if side is None else (0, j, side, 0, at))


def sds(shape, dtype):
    return jax.ShapeDtypeStruct(shape, dtype)


def call(kernel, name, steps, ins, outs, scratch=(), flops=0, moved=0, exps=0):
    return pl.pallas_call(
        kernel,
        grid=(steps,),
        in_specs=[s for _, s in ins],
        out_specs=[s for _, s in outs],
        out_shape=[o for o, _ in outs],
        scratch_shapes=list(scratch),
        cost_estimate=pl.CostEstimate(flops=int(flops) // CHEAP, bytes_accessed=int(moved) // CHEAP, transcendentals=int(exps) // CHEAP),
        name=name,
    )(*[a for a, _ in ins])


def body(tokens, cotangent, lengths, norm1_gain, norm1_shift, qkv_w, qkv_b, out_w, out_b, norm2_gain, norm2_shift,
         normy_gain, normy_shift, cq_w, cq_b, ckv_w, ckv_b, cout_w, cout_b, norm3_gain, norm3_shift, up_w, up_b, down_w, down_b):
    batches = tokens.shape[0]
    members = lax.axis_size("mp")
    n_dp = lax.axis_size("dp")
    assert members == 2 * batches
    me = lax.axis_index("mp")
    view = me // batches
    batch = me % batches
    local = tokens.shape[2]
    rows = local * members
    width = tokens.shape[3]
    r = qkv_w.shape[1]
    hw = cq_w.shape[2]
    fw = up_w.shape[2]
    partner = [(i, (i + batches) % members) for i in range(members)]
    groups = [[d * members + v * batches + b for d in range(n_dp) for b in range(batches)] for v in range(2)]
    both = ("dp", "mp")
    split = r % 16 == 0
    blocks, deep = (n_dp, r) if split else (1, n_dp * r)

    def of_view(a, which):
        return lax.dynamic_index_in_dim(a, which, 0, keepdims=False)

    def cols(q, k, v, o):
        return jnp.concatenate([q, k[..., PAIR:], k[..., :PAIR], v, o[..., PAIR:], o[..., :PAIR]], -1)

    def uncols(a):
        t = [a[..., i * PAIR : (i + 1) * PAIR] for i in range(a.shape[-1] // PAIR)]
        h = HEAD_DIM
        join = lambda x, y: jnp.concatenate([x, y], -1)
        heads = (join(t[0], t[1][..., :h]), join(t[2], t[1][..., h:]), join(t[3], t[4][..., :h]))
        return heads + ((join(t[5], t[4][..., h:]),) if len(t) > 5 else ())

    def pair_of(pack):
        return jnp.stack([of_view(pack, view), lax.ppermute(of_view(pack, 1 - view), "mp", partner)], 0)

    def gather(pair):
        got = lax.all_gather(pair, both, axis=0, axis_index_groups=groups).reshape(n_dp, batches, 2, r, -1)
        return got if split else got.transpose(1, 2, 0, 3, 4).reshape(1, batches, 2, deep, -1)

    flip = lambda a: a.swapaxes(-1, -2)
    pack_self = cols(qkv_w[:, :, 0], qkv_w[:, :, 1], qkv_w[:, :, 2], flip(out_w))
    pack_cross = cols(cq_w, ckv_w[:, :, 0], ckv_w[:, :, 1], flip(cout_w))
    w_att = gather(pair_of(jnp.concatenate([pack_self, pack_cross], -1)))
    pair_ffn = pair_of(jnp.concatenate([up_w, flip(down_w)], -1))

    none = jnp.zeros_like(cq_b)
    bias_pack = jnp.concatenate([cols(qkv_b[:, 0], qkv_b[:, 1], qkv_b[:, 2], none), cols(cq_b, ckv_b[:, 0], ckv_b[:, 1], none), up_b], -1)
    bias_rows = bias_pack.shape[-1] // width
    bias_pack = jnp.broadcast_to(bias_pack.reshape(2, 1, bias_rows, width), (2, batches, bias_rows, width))
    by_view = tokens.swapaxes(0, 1)
    sent_x = jnp.concatenate([by_view, bias_pack], 2).reshape(members, local + bias_rows, width)
    got_x = lax.all_to_all(sent_x, "mp", 0, 0, tiled=True)
    got_y = lax.all_to_all(by_view[::-1].reshape(members, local, width), "mp", 0, 0, tiled=True)
    got_z = lax.all_to_all(cotangent.swapaxes(0, 1).reshape(members, local, width), "mp", 0, 0, tiled=True)
    first, qf, kf, cosine, sine = tables(of_view(lengths[:, 0], batch), rows)

    def from_row(a, at):
        return lax.dynamic_slice_in_dim(jnp.concatenate([a, a], 0), at, rows, 0)

    x = from_row(got_x[:, :local].reshape(rows, width), first)
    y = from_row(got_y.reshape(rows, width), first)
    dz = from_row(got_z.reshape(rows, width), first)

    def by_step(a):
        a = a.reshape((2, batches) + a.shape[1:])
        return jnp.where(view == 0, a, a[::-1]).swapaxes(0, 1).reshape((members,) + a.shape[2:])

    def by_member(a):
        a = a.reshape((batches, 2) + a.shape[1:]).swapaxes(0, 1)
        return jnp.where(view == 0, a, a[::-1]).reshape((members,) + a.shape[2:])

    biases = by_step(got_x[:, local:]).astype(F32)
    self_bias, cross_bias, up_bias = biases[:, 0:1], biases[:, 1:2], biases[:, 2:]
    up_bias = up_bias.reshape(members, 1, fw)

    def mine(a):
        return of_view(a, view).astype(F32)[None]

    g1, s1, ob, g2, s2, gy, sy, cob, g3, s3, db = [
        mine(a) for a in (norm1_gain, norm1_shift, out_b, norm2_gain, norm2_shift, normy_gain, normy_shift, cout_b, norm3_gain, norm3_shift, down_b)]
    def given(*arrays):
        return [(a, whole(a)) for a in arrays]

    def steps(*arrays):
        return [(a, per_step(a)) for a in arrays]

    def full(*shape_types):
        return [(s, whole(s)) for s in shape_types]

    low = sds((rows, width), BF)
    high = sds((rows, width), F32)
    line = sds((1, width), F32)
    heads = sds((members, rows, 5 * PAIR), BF)
    att_low = sds((members, rows, 2 * PAIR), BF)
    att_high = sds((members, rows, 2 * PAIR), F32)
    bias_out = sds((members, 1, 6 * PAIR), F32)
    gemm = 2 * rows * width * width * members

    def attend(h):
        return call(functools.partial(attend_kernel, tile=384), "attend", members, steps(h) + given(qf, kf), [(s, per_step(s)) for s in (att_low, att_high)],
                    flops=12 * members * rows * rows * PAIR, moved=members * rows * PAIR * 22, exps=3 * members * rows * rows)

    def attend_back(h, o, do, lse, side=None):
        count = members if side is None else batches
        out = sds((count, rows, 5 * PAIR), BF)
        acc = pltpu.VMEM((3, rows, PAIR), F32)
        ins = [(a, per_step(a, side)) for a in (h, o, do, lse)]
        return call(functools.partial(attend_back_kernel, tile=256), "attend_back", count, ins + given(qf, kf, cosine, sine), [(out, per_step(out))],
                    [pltpu.VMEM((rows, PAIR), F32), acc, acc], flops=30 * count * rows * rows * PAIR, moved=count * rows * PAIR * 40,
                    exps=3 * count * rows * rows)[0]

    def project(att, at, res, bias, gain, shift):
        tall = 512
        part = lambda cols: pl.BlockSpec((tall, cols), lambda i: (i, 0))
        att_spec = pl.BlockSpec((members, tall, 2 * PAIR), lambda i: (0, i, 0))
        w_spec = pl.BlockSpec((blocks, batches, 2, deep, 2 * PAIR), lambda i: (0, 0, 0, 0, at))
        return call(out_kernel, "project", rows // tall, [(att, att_spec), (w_att, w_spec), (res, part(width))] + given(bias, gain, shift),
                    [(high, part(width)), (low, part(width))], flops=gemm / 3, moved=rows * width * 14)

    def project_back(d, at):
        return call(out_back_kernel, "project_back", members, given(d) + [(w_att, weight_block(w_att, 2 * PAIR, at))], [(att_low, per_step(att_low))],
                    flops=gemm / 3, moved=rows * width * 8)[0]

    def norm(a, gain, shift):
        spec = pl.BlockSpec((ROWS, width), lambda i: (i, 0))
        return call(norm_kernel, "norm", rows // ROWS, [(a, spec)] + given(gain, shift), [(low, spec)], moved=rows * width * 4)[0]

    def by_owner(piece):
        if not split:
            piece = piece.reshape(batches, piece.shape[2], n_dp, r, -1).transpose(2, 0, 1, 3, 4)
        return piece

    def scatter(piece):
        whole_piece = by_owner(piece).reshape(n_dp * batches, 2, r, -1)
        total = lax.psum_scatter(whole_piece, both, scatter_dimension=0, axis_index_groups=groups)
        return with_layout_constraint(total, Layout(major_to_minor=(0, 1, 2)))

    core_pairs = [(i, i ^ 1) for i in range(members)]
    x_pairs = [(i, i ^ 1) for i in range(n_dp)]
    place = lax.axis_index("dp")
    lines = n_dp // 2

    def pick(a, i, axis):
        return lax.dynamic_index_in_dim(a, i, axis, keepdims=False)

    by_hand = batches == 2 and n_dp <= 8
    x_place, z_place = place % 2, place // 2

    def added(terms):
        total = terms[0].astype(F32)
        for term in terms[1:]:
            total = total + term.astype(F32)
        return total

    def hop(terms, axis, other, mine, name, perm):
        got = lax.ppermute(added([pick(t, other, axis) for t in terms]).astype(BF), name, perm)
        return [pick(t, mine, axis) for t in terms] + [got]

    def over_cores(piece):
        return hop([piece], 1, 1 - batch, batch, "mp", core_pairs)

    def over_x(terms):
        terms = [t.reshape((t.shape[0] // 2, 2) + t.shape[1:]) for t in terms]
        return hop(terms, 1, 1 - x_place, x_place, "dp", x_pairs)

    def over_z(terms):
        total = added([pick(t, z_place, 0) for t in terms])
        for s in range(1, lines):
            perm = [(i, (i + 2 * s) % n_dp) for i in range(n_dp)]
            total = total + lax.ppermute(added([pick(t, (z_place + s) % lines, 0) for t in terms]).astype(BF), "dp", perm).astype(F32)
        return total.astype(BF)

    def to_partner(a):
        return lax.ppermute(a, "mp", partner)

    def both_views(keep, theirs):
        keep, theirs = keep.astype(F32), theirs.astype(F32)
        return jnp.stack([jnp.where(view == 0, keep, theirs), jnp.where(view == 0, theirs, keep)], 0)

    n1 = norm(x, g1, s1)
    side = norm(y, gy, sy)
    pair_ffn, n1, side, qf, kf, cosine, sine = lax.optimization_barrier((pair_ffn, n1, side, qf, kf, cosine, sine))
    w_ffn = gather(pair_ffn)
    hs = call(self_in_kernel, "self_in", members, given(n1) + [(w_att, weight_block(w_att, 6 * PAIR, 0))] + steps(self_bias) + given(cosine, sine),
              [(heads, per_step(heads))], flops=gemm, moved=rows * width * 16)[0]
    att, lse = attend(hs)
    middle, n2 = project(att, 2, x, ob, g2, s2)
    hc = call(cross_in_kernel, "cross_in", members, given(n2, side) + [(w_att, weight_block(w_att, 6 * PAIR, 1))] + steps(cross_bias) + given(cosine, sine),
              [(heads, per_step(heads))], flops=gemm, moved=rows * width * 16)[0]
    catt, clse = attend(hc)
    middle2, n3 = project(catt, 5, middle, cob, g3, s3)

    dw_ffn = sds((blocks, batches, 2, deep, 2 * fw), BF)
    dw_ffn_spec = pl.BlockSpec((blocks, 1, 1, deep, 2 * fw), lambda j: (0, j // 2, j % 2, 0, 0))
    up_line = sds((members, 1, fw), F32)
    output, d_mid2, d_cross, dw_f, d_upb, gg3, gs3, d_db, d_cob = call(
        ffn_kernel, "ffn", members,
        given(middle2, n3, dz) + [(w_ffn, weight_block(w_ffn, fw, 0)), (w_ffn, weight_block(w_ffn, fw, 1))] + steps(up_bias) + given(db, g3),
        full(low, high, low) + [(dw_ffn, dw_ffn_spec), (up_line, per_step(up_line))] + full(line, line, line, line),
        [pltpu.VMEM((rows, width), F32)] * 2 + [pltpu.VMEM((rows, fw), BF)] * 2,
        flops=6 * gemm, moved=rows * width * 60, exps=rows * fw * members * 2)

    total_ffn = scatter(dw_f)
    d_catt = project_back(d_cross, 5)
    d_hc = attend_back(hc, catt, d_catt, clse)
    dw_att = sds((blocks, batches, 2, deep, 6 * PAIR), BF)
    dw_spec = pl.BlockSpec((blocks, 1, 1, deep, 6 * PAIR), lambda j: (0, j // 2, j % 2, 0, 0))
    dw_cross, d_crossb, d_mid, d_branch, gg2, gs2, d_ob = call(
        cross_back_kernel, "cross_back", members,
        steps(d_hc) + [(w_att, weight_block(w_att, 6 * PAIR, 1))] + given(n2, side, d_cross) + steps(catt) + given(middle, d_mid2, g2),
        [(dw_att, dw_spec), (bias_out, per_step(bias_out))] + full(high, low, line, line, line),
        [pltpu.VMEM((rows, width), F32)], flops=2 * gemm, moved=rows * width * 30)

    def side_back(dh):
        return call(side_back_kernel, "side_back", members, steps(dh) + [(w_att, weight_block(w_att, 6 * PAIR, 1))] + given(y, gy),
                    full(low, line, line), [pltpu.VMEM((rows, width), F32)], flops=gemm, moved=rows * width * 16)

    d_att = project_back(d_branch, 2)
    total_cross = scatter(dw_cross)

    dw_part = sds((blocks, batches, 1, deep, 6 * PAIR), BF)
    dw_part_spec = pl.BlockSpec((blocks, 1, 1, deep, 6 * PAIR), lambda j: (0, j, 0, 0, 0))
    bias_part = sds((batches, 1, 6 * PAIR), F32)

    def self_back(t, dh, *more):
        ins = steps(dh) + [(w_att, weight_block(w_att, 6 * PAIR, 0, t))] + given(n1, d_branch) + [(att, per_step(att, t))]
        outs = [(dw_part, dw_part_spec), (bias_part, per_step(bias_part))]
        if more:
            return call(self_back_last_kernel, "self_back_last", batches, ins + given(*more), outs + full(low, line, line),
                        [pltpu.VMEM((rows, width), F32)], flops=1.5 * gemm, moved=rows * width * 30)
        return call(self_back_first_kernel, "self_back_first", batches, ins, outs + full(high), flops=1.5 * gemm, moved=rows * width * 24)

    def home(a):
        return lax.all_to_all(a.reshape(members, local, width), "mp", 0, 0, tiled=True).reshape(2, batches, local, width)

    d_h1 = attend_back(hs, att, d_att, lse, 1)
    dw_self1, d_selfb1, acc = self_back(1, d_h1)
    d_att, acc, dw_self1 = lax.optimization_barrier((d_att, acc, dw_self1))
    output = from_row(output, rows - first)
    if by_hand:
        self1 = over_cores(by_owner(dw_self1))
        d_att, output, got = lax.optimization_barrier((d_att, output, self1[1]))
        self1 = over_x([self1[0], got])
    got_output = home(output)
    d_h0 = attend_back(hs, att, d_att, lse, 0)
    d_h0, total_ffn, got_output = lax.optimization_barrier((d_h0, total_ffn, got_output))
    their_ffn = to_partner(total_ffn[1])
    if by_hand:
        d_h0, got = lax.optimization_barrier((d_h0, self1[2]))
        total1 = over_z(self1[:2] + [got])
    dw_self0, d_selfb0, own, gg1, gs1 = self_back(0, d_h0, x, d_mid, acc, g1)
    if by_hand:
        own, dw_self0, gg1, their_ffn, total1 = lax.optimization_barrier((own, dw_self0, gg1, their_ffn, total1))
        self0 = over_cores(by_owner(dw_self0))
        own = from_row(own, rows - first)
        own, got, gg1 = lax.optimization_barrier((own, self0[1], gg1))
        self0 = [t.reshape((lines, 2) + t.shape[1:]) for t in (self0[0], got)]
        send = added([pick(t, 1 - x_place, 1) for t in self0]).astype(BF)
        own, send, d_hc = lax.optimization_barrier((own, send, d_hc))
        self0 = [pick(t, x_place, 1) for t in self0] + [lax.ppermute(send, "dp", x_pairs)]
    else:
        own = from_row(own, rows - first)
    got_own = home(own)
    other, ggy, gsy = side_back(d_hc)
    if by_hand:
        other, x_sum = lax.optimization_barrier((other, self0[2]))
        self0 = self0[:2] + [x_sum]
    lines_out = [gg1, gs1, d_ob, gg2, gs2, ggy, gsy, d_cob, gg3, gs3, d_db, d_selfb0, d_selfb1, d_crossb, d_upb]
    count = 11 + 3 * members
    collected = sds((-(-count // 8) * 8, width), F32)
    small = call(collect_kernel, "collect", 1, given(*lines_out), full(collected))[0]
    if by_hand:
        small = small + lax.ppermute(small, "mp", core_pairs)
        sum_ffn = both_views(total_ffn[0], their_ffn)
        up_wg, down_wg = sum_ffn[..., :fw], flip(sum_ffn[..., fw:])
        their1 = to_partner(total1)
        flat = lax.reduce_precision(small + lax.ppermute(small, "dp", x_pairs), 8, 7)
        flat = jnp.concatenate([flat, to_partner(flat.astype(BF)).astype(F32)], 0)
        flat, got, their1, got_own, other, up_wg, down_wg, total_cross = lax.optimization_barrier((flat, self0[2], their1, got_own, other, up_wg, down_wg, total_cross))
        other = from_row(other, rows - first)
        got_other = home(other)
        their_cross = to_partner(total_cross[1])
        self0 = self0[:2] + [got]
        total0 = added([pick(t, z_place, 0) for t in self0])
        on_line = [flat]
        for s in range(1, lines):
            send = added([pick(t, (z_place + s) % lines, 0) for t in self0]).astype(BF)
            got = lax.ppermute(jnp.concatenate([send.reshape(-1, width), flat.astype(BF)], 0), "dp", [(i, (i + 2 * s) % n_dp) for i in range(n_dp)])
            total0 = total0 + got[: send.size // width].reshape(total0.shape).astype(F32)
            on_line.append(got[send.size // width :].astype(F32))
        on_line = jnp.stack(on_line, 0)
        flat = sum(pick(on_line, (z_place - p) % lines, 0) for p in range(lines))
        flat, flat_in = flat[: small.shape[0]], flat[small.shape[0] :]
        sum_self = both_views(total0[0], their1[0])
    else:
        got_other = home(from_row(other, rows - first))
        total_self = scatter(jnp.concatenate([dw_self0, dw_self1], 2))
        their_cross = to_partner(total_cross[1])
        sum_self = both_views(total_self[0], to_partner(total_self[1]))
        sums = lax.psum(jnp.stack([jnp.where(view == 0, small, 0.0), jnp.where(view == 1, small, 0.0)], 0), both)
        flat, flat_in = pick(sums, view, 0), pick(sums, 1 - view, 0)
        sum_ffn = both_views(total_ffn[0], their_ffn)
        up_wg, down_wg = sum_ffn[..., :fw], flip(sum_ffn[..., fw:])
    sum_cross = both_views(total_cross[0], their_cross)

    sums = both_views(flat[:11].reshape(-1), flat_in[:11].reshape(-1))
    g1g, s1g, obg, g2g, s2g, gyg, syg, cobg, g3g, s3g, dbg = [sums[:, i * width : (i + 1) * width] for i in range(11)]

    def member_row(own_row, other_row):
        return both_views(pick(flat, own_row, 0), pick(flat_in, other_row, 0))

    self_part = uncols(member_row(11 + batch, 11 + batches + batch)[:, : 5 * PAIR])
    start = 11 + members + 2 * batch
    cross_part = uncols(member_row(start, start + 1)[:, : 5 * PAIR])
    upb_grad = member_row(start + members, start + members + 1)

    block_output = got_output.swapaxes(0, 1)
    input_grad = (got_own.astype(F32) + got_other[::-1].astype(F32)).swapaxes(0, 1)

    q, k, v, o = uncols(sum_self)
    cq, ck, cv, co = uncols(sum_cross)
    return (block_output, input_grad, g1g, s1g, jnp.stack([q, k, v], 2), jnp.stack(self_part, 1), flip(o), obg, g2g, s2g, gyg, syg,
            cq, cross_part[0], jnp.stack([ck, cv], 2), jnp.stack(cross_part[1:], 1), flip(co), cobg, g3g, s3g,
            up_wg, upb_grad, down_wg, dbg)


def solution(mesh):
    rows = P(None, None, ("dp", "mp"), None)
    wide = P(None, "dp", None, "mp")
    by_rows = P(None, "dp", "mp")
    by_cols = P(None, "mp", "dp")
    parts = P(None, None, "mp")
    flat = P(None, "mp")
    same = P()
    in_specs = (rows, rows, P(None, "dp", None), same, same, wide, parts, by_cols, same, same, same, same, same, by_rows, flat, wide, parts,
                by_cols, same, same, same, by_rows, flat, by_cols, same)
    out_specs = (rows, rows, same, same, wide, parts, by_cols, same, same, same, same, same, by_rows, flat, wide, parts, by_cols, same,
                 same, same, by_rows, flat, by_cols, same)
    return jax.shard_map(body, mesh=mesh, in_specs=in_specs, out_specs=out_specs, check_vma=False)
```
